32 devices in a mesh: seq: 4 (over y, core), fsdp: 8 (over z, x).
Axes of the slice: x: 2, y: 2, z: 4, core: 2. Of those that a mesh axis runs over, the one named last changes fastest.
Arguments:
- tokens: bfloat16 [8, 1024, 2048], P('fsdp', 'seq'), may hold values from -6 to 6
- cotangent: bfloat16 [8, 1024, 2048], P('fsdp', 'seq'), may hold values from -6 to 6
- lengths: int32 [8, 4], P('fsdp'), may hold values from 0 to 1024, as said below
- sequence_adapter: int32 [8, 4], P('fsdp'), may hold values from 0 to 7
- attention_norm_gain: float32 [2048], replicated, may hold values from 0.1 to 1.9
- feedfwd_norm_gain: float32 [2048], replicated, may hold values from 0.1 to 1.9
- query_matrix: bfloat16 [2048, 2048], P('fsdp'), may hold values from -0.5 to 0.5
- key_matrix: bfloat16 [2048, 512], P('fsdp'), may hold values from -0.5 to 0.5
- value_matrix: bfloat16 [2048, 512], P('fsdp'), may hold values from -0.125 to 0.125
- output_matrix: bfloat16 [2048, 2048], P('fsdp'), may hold values from -1.5 to 1.5
- gate_matrix: bfloat16 [2048, 8192], P('fsdp'), may hold values from -0.125 to 0.125
- up_matrix: bfloat16 [2048, 8192], P('fsdp'), may hold values from -0.125 to 0.125
- down_matrix: bfloat16 [8192, 2048], P('fsdp'), may hold values from -0.25 to 0.25
- adapter_first_factors: bfloat16 [6, 2048, 128], replicated, may hold values from -0.125 to 0.125
- adapter_first_down: bfloat16 [8192, 128], replicated, may hold values from -0.0625 to 0.0625
- adapter_second_model: bfloat16 [3, 128, 2048], replicated, may hold values from -1.5 to 1.5
- adapter_second_keyvalue: bfloat16 [2, 128, 512], replicated, may hold values from -1.5 to 1.5
- adapter_second_feedfwd: bfloat16 [2, 128, 8192], replicated, may hold values from -1.5 to 1.5
Outputs:
- layer_out: bfloat16 [8, 1024, 2048], P('fsdp', 'seq')
- grad_tokens: bfloat16 [8, 1024, 2048], P('fsdp', 'seq')
- grad_lora_a: float32 [6, 2048, 128], replicated
- grad_lora_a_down: float32 [8192, 128], replicated
- grad_lora_b_model: float32 [3, 128, 2048], replicated
- grad_lora_b_kv: float32 [2, 128, 512], replicated
- grad_lora_b_ffn: float32 [2, 128, 8192], replicated
The draws below stay inside these ranges and needn't reach their ends.
Inputs may be any that keep to these rules, and one draw needn't show every extreme that they name: In each pack the lengths add up to 1024 or less; pack 0 holds one sequence of exactly 1024 tokens and three empty ones; in every other pack each sequence has 1 token or more and the first 512 or more; padded slots follow the last sequence.
All inputs are finite; a program needn't handle non-finite values.
Results may differ from the reference program's by a relative error of at most 0.018.
The reference program's roundings to bfloat16 on the way count: a program that leaves them out, or rounds other values in their place, can miss the bound.
Values may be sent and summed in bfloat16 or wider, within the bound.
No kernel may reach another device: no remote copies, remote signals or barrier semaphores. Data moves between devices by JAX's collectives and lax.ppermute only.
A program may use at most 384 MiB of HBM per device.

```python
import math
import jax
import jax.numpy as jnp
from jax import lax

MODEL_WIDTH = 2048
HEADS = 32
KV_HEADS = 8
HEAD_DIM = 64
FEEDFWD_UNITS = 8192
ADAPTER_RANK = 16
ADAPTER_TOTAL = 8
NSEQ = 4
PACK = 1024
QBLOCK = 512
KEY_HEAD_WIDTH = 512
N_FSDP = 8


def draw_lengths(key, part):
    key_used, key_first, key_second, key_third = jax.random.split(key, 4)
    used_len = jax.random.randint(key_used, (N_FSDP,), 3 * PACK // 4, PACK + 1)
    front_len = jax.random.randint(key_first, (N_FSDP,), PACK // 2, used_len - 2)
    remain = used_len - front_len
    second_len = jax.random.randint(key_second, (N_FSDP,), 1, remain - 1)
    third_len = jax.random.randint(key_third, (N_FSDP,), 1, remain - second_len)
    fourth_len = remain - second_len - third_len
    table = jnp.stack([front_len, second_len, third_len, fourth_len], axis=1).astype(jnp.int32)
    first_row = jnp.zeros((NSEQ,), jnp.int32).at[0].set(PACK)
    return table.at[0].set(first_row).astype(jnp.int32)


def set_ends(drawn, rng, least, largest):
    place = [jax.random.randint(jax.random.fold_in(rng, axis), (), 0, length) for axis, length in enumerate(drawn.shape)]
    main_axis = drawn.shape.index(max(drawn.shape))
    next_to = place[:main_axis] + [(place[main_axis] + 1) % drawn.shape[main_axis]] + place[main_axis + 1:]
    return drawn.at[tuple(place)].set(least).at[tuple(next_to)].set(largest)


def block_levels(own_key, extent, cuts, smallest, largest):
    loudness, own = 1.0, jax.random.fold_in(own_key, 6)
    for dim, shards_of in cuts:
        steps = jnp.exp(jax.random.uniform(jax.random.fold_in(own, dim), (shards_of,), jnp.float32, smallest / len(cuts), largest / len(cuts)))
        loudness = loudness * jnp.repeat(steps, extent[dim] // shards_of).reshape([-1 if axis == dim else 1 for axis in range(len(extent))])
    return loudness


def scatter_about(own_key, dims, deviation, bound, shards=(), kind=jnp.bfloat16):
    loudness = block_levels(own_key, dims, shards, -0.22, 0.18) if shards else 1.0
    entries = jax.random.normal(own_key, dims, jnp.float32) * deviation * loudness
    return jnp.minimum(jnp.maximum(entries, -bound), bound).astype(kind)


def setup_inputs(seed: int = 0) -> dict:
    arg_keys = jax.random.split(jax.random.key(seed), 19)
    return {
        "tokens": scatter_about(arg_keys[0], (N_FSDP, PACK, MODEL_WIDTH), 1.0, 6.0, ((0, 8), (1, 4))),
        "cotangent": scatter_about(arg_keys[1], (N_FSDP, PACK, MODEL_WIDTH), 1.0, 6.0, ((0, 8), (1, 4))),
        "lengths": draw_lengths(jax.random.fold_in(arg_keys[18], 71), 0),
        "sequence_adapter": set_ends(jax.random.randint(arg_keys[3], (N_FSDP, NSEQ), 0, ADAPTER_TOTAL), jax.random.fold_in(arg_keys[3], 1), 0, ADAPTER_TOTAL - 1).astype(jnp.int32),
        "attention_norm_gain": jnp.clip(1.0 + 0.18 * jax.random.normal(arg_keys[4], (MODEL_WIDTH,), jnp.float32), 0.1, 1.9),
        "feedfwd_norm_gain": jnp.clip(1.0 + 0.18 * jax.random.normal(arg_keys[5], (MODEL_WIDTH,), jnp.float32), 0.1, 1.9),
        "query_matrix": scatter_about(arg_keys[6], (MODEL_WIDTH, MODEL_WIDTH), (MODEL_WIDTH // 16) ** -0.5, 0.5, ((0, 8),)),
        "key_matrix": scatter_about(arg_keys[7], (MODEL_WIDTH, KEY_HEAD_WIDTH), (MODEL_WIDTH // 16) ** -0.5, 0.5, ((0, 8),)),
        "value_matrix": scatter_about(arg_keys[8], (MODEL_WIDTH, KEY_HEAD_WIDTH), MODEL_WIDTH ** -0.5, 0.125, ((0, 8),)),
        "output_matrix": scatter_about(arg_keys[9], (MODEL_WIDTH, MODEL_WIDTH), (max(1, MODEL_WIDTH // 128)) ** -0.5, 1.5, ((0, 8),)),
        "gate_matrix": scatter_about(arg_keys[10], (MODEL_WIDTH, FEEDFWD_UNITS), MODEL_WIDTH ** -0.5, 0.125, ((0, 8),)),
        "up_matrix": scatter_about(arg_keys[11], (MODEL_WIDTH, FEEDFWD_UNITS), MODEL_WIDTH ** -0.5, 0.125, ((0, 8),)),
        "down_matrix": scatter_about(arg_keys[12], (FEEDFWD_UNITS, MODEL_WIDTH), (FEEDFWD_UNITS // 16) ** -0.5, 0.25, ((0, 8),)),
        "adapter_first_factors": scatter_about(arg_keys[13], (6, MODEL_WIDTH, ADAPTER_TOTAL * ADAPTER_RANK), MODEL_WIDTH ** -0.5, 0.125),
        "adapter_first_down": scatter_about(arg_keys[14], (FEEDFWD_UNITS, ADAPTER_TOTAL * ADAPTER_RANK), FEEDFWD_UNITS ** -0.5, 0.0625),
        "adapter_second_model": scatter_about(arg_keys[15], (3, ADAPTER_TOTAL * ADAPTER_RANK, MODEL_WIDTH), ADAPTER_RANK ** -0.5, 1.5),
        "adapter_second_keyvalue": scatter_about(arg_keys[16], (2, ADAPTER_TOTAL * ADAPTER_RANK, KEY_HEAD_WIDTH), ADAPTER_RANK ** -0.5, 1.5),
        "adapter_second_feedfwd": scatter_about(arg_keys[17], (2, ADAPTER_TOTAL * ADAPTER_RANK, FEEDFWD_UNITS), ADAPTER_RANK ** -0.5, 1.5),
    }


SCORE_SCALE = 0.015625
RESIDUAL_FACTOR = 0.22
NORM_EPSILON = 1e-05
ROPE_BASE = 10000000.0
MASK_FILL = 1e+30

@jax.custom_vjp
def lowrank_rows(v):
    return lax.optimization_barrier(v.astype(jnp.bfloat16)).astype(jnp.float32)

@jax.custom_vjp
def lowrank_backward(v):
    return v

def low_keep(v):
    return (lowrank_rows(v), None)

def low_pass(kept, grad):
    return (grad,)

def back_keep(v):
    return (v, None)

def back_low(kept, grad):
    return (lowrank_rows(grad),)
lowrank_rows.defvjp(low_keep, low_pass)
lowrank_backward.defvjp(back_keep, back_low)

def matrix_product(left, right):
    return jnp.dot(left, right, precision=lax.Precision.HIGHEST)

def rms_norm(hidden, gain_vec):
    mean_square = lax.optimization_barrier(jnp.mean(hidden * hidden, axis=-1, keepdims=True))
    return hidden * lax.rsqrt(mean_square + NORM_EPSILON) * gain_vec

def rotate(vectors, cosine, sine_table):
    half_dim = vectors.shape[-1] // 2
    front_half = vectors[..., :half_dim]
    back_half = vectors[..., half_dim:]
    turned = jnp.concatenate([-back_half, front_half], axis=-1)
    return vectors * cosine + turned * sine_table

def pack_tables(seq_lengths, adapter_id, token_count, adapter_count):
    slots = seq_lengths.shape[0]
    places = jnp.arange(token_count, dtype=jnp.int32)
    seq_ends = jnp.cumsum(seq_lengths).astype(jnp.int32)
    seq_starts = seq_ends - seq_lengths
    used_len = seq_ends[slots - 1]
    segment = lax.optimization_barrier(jnp.sum((places[:, None] >= seq_ends[None, :]).astype(jnp.int32), axis=1))
    member = segment[:, None] == jnp.arange(slots, dtype=jnp.int32)[None, :]
    start_tok = lax.optimization_barrier(jnp.sum(jnp.where(member, seq_starts[None, :], 0), axis=1)) + jnp.where(segment == slots, used_len, 0)
    position = places - start_tok
    valid_row = segment < slots
    chosen = adapter_id[:, None] == jnp.arange(adapter_count, dtype=jnp.int32)[None, :]
    onehot = lax.optimization_barrier(jnp.sum(jnp.where(member[:, :, None] & chosen[None, :, :], 1.0, 0.0), axis=1)).astype(jnp.float32)
    return (segment, position, valid_row, onehot)

def rope_tables(position, head_size):
    frequency = ROPE_BASE ** (-(jnp.arange(head_size // 2, dtype=jnp.float32) * 2.0) / head_size)
    angles = position.astype(jnp.float32)[:, None] * frequency[None, :]
    angles = jnp.concatenate([angles, angles], axis=1)
    return (jnp.cos(angles)[:, None, :], jnp.sin(angles)[:, None, :])

def layer(hidden_in, adapter_stack, frozen, tables):
    adapter_first_factors, adapter_first_down, adapter_second_model, adapter_second_keyvalue, adapter_second_feedfwd = adapter_stack
    gain_one, gain_two, query_matrix, key_matrix, value_matrix, output_matrix, gate_matrix, up_matrix, down_matrix = frozen
    segment, valid_col, adapter_mask_repeated, cosine, sine_table = tables
    token_count = hidden_in.shape[0]
    adapter_columns_span = ADAPTER_TOTAL * ADAPTER_RANK
    group_ratio = HEADS // KV_HEADS
    first_normed_input = lowrank_rows(rms_norm(hidden_in, gain_one))
    adapter_input = jnp.concatenate([adapter_first_factors[0], adapter_first_factors[1], adapter_first_factors[2]], axis=1)
    lowrank_attention = lowrank_backward(lowrank_rows(jnp.tile(adapter_mask_repeated, (1, 3)) * matrix_product(first_normed_input, adapter_input)))
    query_rows_full = lowrank_backward(matrix_product(first_normed_input, query_matrix) + matrix_product(lowrank_attention[:, :adapter_columns_span], adapter_second_model[0]))
    key_portion = lowrank_backward(matrix_product(first_normed_input, key_matrix) + matrix_product(lowrank_attention[:, adapter_columns_span:2 * adapter_columns_span], adapter_second_keyvalue[0]))
    value_portion = lowrank_backward(matrix_product(first_normed_input, value_matrix) + matrix_product(lowrank_attention[:, 2 * adapter_columns_span:], adapter_second_keyvalue[1]))
    query_r = rotate(query_rows_full.reshape(token_count, HEADS, HEAD_DIM), cosine, sine_table)
    key_r = rotate(key_portion.reshape(token_count, KV_HEADS, HEAD_DIM), cosine, sine_table)
    queries = lowrank_backward(lowrank_rows(query_r)).reshape(token_count, KV_HEADS, group_ratio, HEAD_DIM)
    key_rows = lowrank_backward(lowrank_rows(key_r))
    value_rows = lowrank_backward(lowrank_rows(value_portion)).reshape(token_count, KV_HEADS, HEAD_DIM)
    places = jnp.arange(token_count, dtype=jnp.int32)

    def one_block(block_index):
        first_row = block_index * QBLOCK
        query_block = lax.dynamic_slice_in_dim(queries, first_row, QBLOCK, 0)
        scores = jnp.einsum('qgjd,kgd->gjqk', query_block, key_rows, precision=lax.Precision.HIGHEST) * SCORE_SCALE
        scores = lowrank_backward(scores)
        query_seg = lax.dynamic_slice_in_dim(segment, first_row, QBLOCK, 0)
        query_pos = first_row + jnp.arange(QBLOCK, dtype=jnp.int32)
        allowed = (query_seg[:, None] == segment[None, :]) & (places[None, :] <= query_pos[:, None])
        scores = jnp.where(allowed, scores, -MASK_FILL)
        row_max = lax.optimization_barrier(jnp.max(scores, axis=-1, keepdims=True))
        exponent = jnp.exp(scores - row_max)
        attn_probs = lowrank_rows(exponent / lax.optimization_barrier(jnp.sum(exponent, axis=-1, keepdims=True)))
        return jnp.einsum('gjqk,kgd->qgjd', attn_probs, value_rows, precision=lax.Precision.HIGHEST)
    block_outs = lax.map(jax.checkpoint(one_block), jnp.arange(token_count // QBLOCK, dtype=jnp.int32))
    attention_output = lowrank_backward(lowrank_rows(block_outs.reshape(token_count, MODEL_WIDTH)))
    lowrank_output = lowrank_backward(lowrank_rows(adapter_mask_repeated * matrix_product(attention_output, adapter_first_factors[3])))
    residual_branch = lowrank_backward(matrix_product(attention_output, output_matrix) + matrix_product(lowrank_output, adapter_second_model[1]))
    hidden_mid = hidden_in + RESIDUAL_FACTOR * residual_branch
    second_normed_input = lowrank_rows(rms_norm(hidden_mid, gain_two))
    adapter_feedfwd = jnp.concatenate([adapter_first_factors[4], adapter_first_factors[5]], axis=1)
    lowrank_feedfwd = lowrank_backward(lowrank_rows(jnp.tile(adapter_mask_repeated, (1, 2)) * matrix_product(second_normed_input, adapter_feedfwd)))
    gate_projected = lowrank_backward(matrix_product(second_normed_input, gate_matrix) + matrix_product(lowrank_feedfwd[:, :adapter_columns_span], adapter_second_feedfwd[0]))
    up_projected = lowrank_backward(matrix_product(second_normed_input, up_matrix) + matrix_product(lowrank_feedfwd[:, adapter_columns_span:], adapter_second_feedfwd[1]))
    swiglu_output = lowrank_rows(jax.nn.sigmoid(gate_projected) * gate_projected * up_projected)
    lowrank_down = lowrank_backward(lowrank_rows(adapter_mask_repeated * matrix_product(swiglu_output, adapter_first_down)))
    down_result = lowrank_backward(matrix_product(swiglu_output, down_matrix) + matrix_product(lowrank_down, adapter_second_model[2]))
    return valid_col * (hidden_mid + RESIDUAL_FACTOR * down_result)

def reference(tokens, cotangent, lengths, sequence_adapter, attention_norm_gain, feedfwd_norm_gain, query_matrix, key_matrix, value_matrix, output_matrix, gate_matrix, up_matrix, down_matrix, adapter_first_factors, adapter_first_down, adapter_second_model, adapter_second_keyvalue, adapter_second_feedfwd):
    frozen = tuple((operand_matrix.astype(jnp.float32) for operand_matrix in (attention_norm_gain, feedfwd_norm_gain, query_matrix, key_matrix, value_matrix, output_matrix, gate_matrix, up_matrix, down_matrix)))
    adapter_stack = tuple((operand_matrix.astype(jnp.float32) for operand_matrix in (adapter_first_factors, adapter_first_down, adapter_second_model, adapter_second_keyvalue, adapter_second_feedfwd)))

    def per_pack(running, inputs):
        hidden, cot_rows, seq_lengths, adapter_id = inputs
        segment, position, valid_row, onehot = pack_tables(seq_lengths, adapter_id, PACK, ADAPTER_TOTAL)
        adapter_mask_repeated = jnp.repeat(onehot, ADAPTER_RANK, axis=1)
        cosine, sine_table = rope_tables(position, HEAD_DIM)
        tables = (segment, jnp.where(valid_row, 1.0, 0.0).astype(jnp.float32)[:, None], adapter_mask_repeated, cosine, sine_table)

        def forward(hidden_arg, adapter_arg):
            return layer(hidden_arg, adapter_arg, frozen, tables)
        result, pullback = jax.vjp(forward, hidden.astype(jnp.float32), adapter_stack)
        grad_hidden, grad_adapters = pullback(cot_rows.astype(jnp.float32))
        running = jax.tree.map(lambda left, right: left + right, running, grad_adapters)
        return (running, (result.astype(jnp.bfloat16), grad_hidden.astype(jnp.bfloat16)))
    zero_grads = jax.tree.map(jnp.zeros_like, adapter_stack)
    grad_sums, (layer_out, grad_tokens) = lax.scan(per_pack, zero_grads, (tokens, cotangent, lengths, sequence_adapter))
    factor = ADAPTER_TOTAL / math.sqrt(PACK * N_FSDP)
    return (layer_out, grad_tokens, grad_sums[0] * factor, grad_sums[1] * factor, grad_sums[2] * factor, grad_sums[3] * factor, grad_sums[4] * factor)
```

```python
import math

import jax
import jax.numpy as jnp
from jax import lax
from jax.experimental import pallas as pl
from jax.experimental.pallas import tpu as pltpu
from jax.sharding import PartitionSpec as P

MODEL_WIDTH = 2048
HEADS = 32
KV_HEADS = 8
HEAD_DIM = 64
ADAPTER_RANK = 16
ADAPTER_TOTAL = 8
PACK = 1024
QBLOCK = 256
SPAN = ADAPTER_TOTAL * ADAPTER_RANK
GROUP = HEADS // KV_HEADS

SCORE_SCALE = 0.015625
RESIDUAL_FACTOR = 0.22
NORM_EPSILON = 1e-05
ROPE_BASE = 10000000.0
MASK_FILL = 1e30

BF16 = jnp.bfloat16
F32 = jnp.float32


def mm(left, right):
    return jnp.dot(left, right, preferred_element_type=F32)


def mm_nt(left, right):
    return lax.dot_general(left, right, (((1,), (1,)), ((), ())), preferred_element_type=F32)


def mm_tn(left, right):
    return lax.dot_general(left, right, (((0,), (0,)), ((), ())), preferred_element_type=F32)


def rms_norm(hidden, gain_vec):
    mean_square = jnp.mean(hidden * hidden, axis=-1, keepdims=True)
    return hidden * lax.rsqrt(mean_square + NORM_EPSILON) * gain_vec


def pack_tables(seq_lengths, adapter_id, token_count, adapter_count):
    slots = seq_lengths.shape[0]
    places = jnp.arange(token_count, dtype=jnp.int32)
    seq_ends = jnp.cumsum(seq_lengths)
    seq_starts = seq_ends - seq_lengths
    used_len = seq_ends[slots - 1]
    segment = jnp.sum((places[:, None] >= seq_ends[None, :]).astype(jnp.int32), axis=1)
    member = segment[:, None] == jnp.arange(slots, dtype=jnp.int32)[None, :]
    start_tok = jnp.sum(jnp.where(member, seq_starts[None, :], 0), axis=1) + jnp.where(
        segment == slots, used_len, 0
    )
    position = places - start_tok
    valid_row = segment < slots
    chosen = adapter_id[:, None] == jnp.arange(adapter_count, dtype=jnp.int32)[None, :]
    onehot = jnp.sum(jnp.where(member[:, :, None] & chosen[None, :, :], 1.0, 0.0), axis=1).astype(F32)
    return (segment, position, valid_row, onehot)


def rope_tables(position, head_size, copies):
    frequency = ROPE_BASE ** (-(jnp.arange(head_size // 2, dtype=F32) * 2.0) / head_size)
    angles = position.astype(F32)[:, None] * frequency[None, :]
    cosine, sine = jnp.cos(angles), jnp.sin(angles)
    return (jnp.tile(cosine, (1, 2 * copies)), jnp.tile(sine, (1, 2 * copies)))


def bits_down(count):
    bits, bit = [], count >> 1
    while bit:
        bits.append(bit)
        bit >>= 1
    return bits


def relative_order(count):
    order = [0]
    for bit in bits_down(count):
        order = order + [o ^ bit for o in order]
    return order


def swap(block, axis, offset):
    count = lax.axis_size(axis)
    return lax.ppermute(block, axis, [(i, i ^ offset) for i in range(count)])


def gather_relative(block, axis):
    pieces = [block]
    for bit in bits_down(lax.axis_size(axis)):
        pieces = pieces + [swap(piece, axis, bit) for piece in pieces]
    return pieces


def reduce_relative(pieces, axis):
    for bit in reversed(bits_down(lax.axis_size(axis))):
        half = len(pieces) // 2
        got = [swap(piece.astype(BF16), axis, bit) for piece in pieces[half:]]
        pieces = [mine.astype(F32) + other.astype(F32) for mine, other in zip(pieces[:half], got)]
    return pieces[0]


def cycle_of(count):
    return list(range(0, count, 2)) + list(range(count - 1, 0, -2))


class Rings:
    WINDOW = 2

    def __init__(self):
        self.count = lax.axis_size("fsdp")
        cycle = cycle_of(self.count)
        place = {device: k for k, device in enumerate(cycle)}
        table = [
            [cycle[(place[device] - k) % self.count] for k in range(self.count)]
            for device in range(self.count)
        ]
        self.owner = lax.dynamic_index_in_dim(
            jnp.array(table, jnp.int32), lax.axis_index("fsdp"), 0, keepdims=False
        )
        ahead = [(cycle[k], cycle[(k + 1) % self.count]) for k in range(self.count)]
        self.perms = (ahead, [(b, a) for a, b in ahead])
        self.sent = ([], [])

    def send(self, way, block):
        sent = self.sent[way]
        if len(sent) >= self.WINDOW:
            block, _ = lax.optimization_barrier((block, sent[-self.WINDOW]))
        got = lax.ppermute(block, "fsdp", self.perms[way])
        sent.append(got)
        return got

    def gather(self, blocks):
        half = self.count // 2
        lag = max(half // 2, 1)
        found = [{0: block} for block in blocks]
        latest = [[block, block] for block in blocks]
        for time in range(half + lag * (len(blocks) - 1)):
            for which in range(len(blocks)):
                step = time - lag * which + 1
                if not 1 <= step <= half:
                    continue
                for way in (0, 1):
                    if step == half and way != which % 2:
                        continue
                    got = self.send(way, latest[which][way])
                    latest[which][way] = got
                    found[which][step if way == 0 else self.count - step] = got
        return [[f[k] for k in range(self.count)] for f in found]


def place_blocks(pieces, counts, targets):
    rows = pieces[0].shape[0] // counts
    columns = pieces[0].shape[1]
    total = len(pieces) * counts

    def body(target_ref, *refs):
        out_ref, held, came, left = refs[-4:]
        arrivals, departures = [], []
        for i in range(len(pieces)):
            for j in range(counts):
                k = i * counts + j
                first = pl.multiple_of(target_ref[k] * rows, rows)
                arrivals.append(
                    pltpu.make_async_copy(
                        refs[i].at[pl.ds(j * rows, rows), :], held.at[k], came.at[k]
                    )
                )
                departures.append(
                    pltpu.make_async_copy(
                        held.at[k], out_ref.at[pl.ds(first, rows), :], left.at[k]
                    )
                )
        for copy in arrivals:
            copy.start()
        for arrival, departure in zip(arrivals, departures):
            arrival.wait()
            departure.start()
        for copy in departures:
            copy.wait()

    return pl.pallas_call(
        body,
        out_shape=jax.ShapeDtypeStruct((rows * total, columns), pieces[0].dtype),
        grid_spec=pltpu.PrefetchScalarGridSpec(
            num_scalar_prefetch=1,
            grid=(),
            in_specs=[pl.BlockSpec(memory_space=pl.ANY)] * len(pieces),
            out_specs=pl.BlockSpec(memory_space=pl.ANY),
            scratch_shapes=[
                pltpu.VMEM((total, rows, columns), pieces[0].dtype),
                pltpu.SemaphoreType.DMA((total,)),
                pltpu.SemaphoreType.DMA((total,)),
            ],
        ),
        cost_estimate=pl.CostEstimate(
            flops=0, transcendentals=0, bytes_accessed=4 * rows * total * columns
        ),
        name="place_blocks",
    )(targets.astype(jnp.int32), *pieces)


def half_lanes(shape):
    lane = lax.broadcasted_iota(jnp.int32, shape, 1)
    return lane % HEAD_DIM < HEAD_DIM // 2


def turn_tile(x, cosine, sine):
    quarter = HEAD_DIM // 2
    ahead = pltpu.roll(x, 2 * HEAD_DIM - quarter, 1)
    behind = pltpu.roll(x, quarter, 1)
    return x * cosine + jnp.where(half_lanes(x.shape), -ahead, behind) * sine


def dot_tn(left, right):
    return lax.dot_general(left, right, (((0,), (0,)), ((), ())), preferred_element_type=F32)


def dot_nt(left, right):
    return lax.dot_general(left, right, (((1,), (1,)), ((), ())), preferred_element_type=F32)


def allowed_pairs(seg_col, seg_row, block):
    keys = (block + 1) * QBLOCK
    shape = (keys, QBLOCK)
    key_at = lax.broadcasted_iota(jnp.int32, shape, 0)
    query_at = lax.broadcasted_iota(jnp.int32, shape, 1) + block * QBLOCK
    same = seg_col[:keys, :] == seg_row[:, block * QBLOCK : keys]
    return same & (key_at <= query_at)


def forward_body(
    blocks, slot_ref, q_ref, k_ref, v_ref, cos_ref, sin_ref, col_ref, row_ref,
    qn_ref, kn_ref, vn_ref, out_ref, lse_ref,
):
    for j in range(blocks):
        here = slice(j * QBLOCK, (j + 1) * QBLOCK)
        there = pl.ds(pl.multiple_of(slot_ref[j] * QBLOCK, QBLOCK), QBLOCK)
        cosine, sine = cos_ref[here, :], sin_ref[here, :]
        qn_ref[here, :] = turn_tile(q_ref[there, :], cosine, sine).astype(BF16)
        kn_ref[here, :] = turn_tile(k_ref[there, :], cosine, sine).astype(BF16)
        vn_ref[here, :] = v_ref[there, :].astype(BF16)
    lane = lax.broadcasted_iota(jnp.int32, (QBLOCK, 2 * HEAD_DIM), 1)
    row = lax.broadcasted_iota(jnp.int32, (2 * HEAD_DIM, QBLOCK), 0)
    for i in range(blocks):
        here = slice(i * QBLOCK, (i + 1) * QBLOCK)
        keys = (i + 1) * QBLOCK
        allowed = allowed_pairs(col_ref[...], row_ref[...], i)
        query = (qn_ref[here, :].astype(F32) * SCORE_SCALE).astype(BF16)
        outs = []
        for e in range(2):
            mine = jnp.where(lane // HEAD_DIM == e, query, jnp.zeros_like(query))
            scores = jnp.where(allowed, dot_nt(kn_ref[:keys, :], mine), -MASK_FILL)
            most = jnp.max(scores, axis=0, keepdims=True)
            exponent = jnp.exp(scores - most)
            total = jnp.sum(exponent, axis=0, keepdims=True)
            probs = (exponent * (1.0 / total)).astype(BF16)
            lse_ref[0, e : e + 1, here] = most + jnp.log(total)
            outs.append(dot_tn(vn_ref[:keys, :], probs))
        out = jnp.where(row < HEAD_DIM, outs[0], outs[1]).T
        there = pl.ds(pl.multiple_of(slot_ref[i] * QBLOCK, QBLOCK), QBLOCK)
        out_ref[there, :] = out.astype(BF16)


def backward_body(
    blocks, slot_ref, qn_ref, kn_ref, vn_ref, do_ref, lse_ref, cos_ref, sin_ref, col_ref, row_ref,
    dq_ref, dk_ref, dv_ref, dk_sum, dv_sum,
):
    pairs_per_group = GROUP // 2
    step = lax.rem(pl.program_id(0), pairs_per_group)

    @pl.when(step == 0)
    def _():
        dk_sum[...] = jnp.zeros_like(dk_sum)
        dv_sum[...] = jnp.zeros_like(dv_sum)

    lane = lax.broadcasted_iota(jnp.int32, (QBLOCK, 2 * HEAD_DIM), 1)
    row = lax.broadcasted_iota(jnp.int32, (2 * HEAD_DIM, QBLOCK), 0)
    for i in range(blocks):
        here = slice(i * QBLOCK, (i + 1) * QBLOCK)
        there = pl.ds(pl.multiple_of(slot_ref[i] * QBLOCK, QBLOCK), QBLOCK)
        keys = (i + 1) * QBLOCK
        allowed = allowed_pairs(col_ref[...], row_ref[...], i)
        query = (qn_ref[here, :].astype(F32) * SCORE_SCALE).astype(BF16)
        grad = do_ref[there, :]
        outs = []
        for e in range(2):
            mine = jnp.where(lane // HEAD_DIM == e, query, jnp.zeros_like(query))
            grad_mine = jnp.where(lane // HEAD_DIM == e, grad, jnp.zeros_like(grad))
            scores = jnp.where(allowed, dot_nt(kn_ref[:keys, :], mine), -MASK_FILL)
            probs = jnp.exp(scores - lse_ref[0, e : e + 1, here])
            grad_probs = dot_nt(vn_ref[:keys, :], grad_mine)
            delta = jnp.sum(probs * grad_probs, axis=0, keepdims=True)
            grad_scores = (probs * (grad_probs - delta)).astype(BF16)
            dv_sum[:keys, :] += jnp.dot(probs.astype(BF16), grad_mine, preferred_element_type=F32)
            dk_sum[:keys, :] += jnp.dot(grad_scores, mine, preferred_element_type=F32)
            outs.append(dot_tn(kn_ref[:keys, :], grad_scores))
        out = jnp.where(row < HEAD_DIM, outs[0], outs[1]).T * SCORE_SCALE
        out = out.astype(BF16).astype(F32)
        dq_ref[there, :] = turn_tile(out, cos_ref[here, :], -sin_ref[here, :]).astype(BF16)

    @pl.when(step == pairs_per_group - 1)
    def _():
        for j in range(blocks):
            here = slice(j * QBLOCK, (j + 1) * QBLOCK)
            there = pl.ds(pl.multiple_of(slot_ref[j] * QBLOCK, QBLOCK), QBLOCK)
            dk = dk_sum[here, :]
            dk = (dk + pltpu.roll(dk, HEAD_DIM, 1)).astype(BF16).astype(F32)
            dk_ref[there, :] = turn_tile(dk, cos_ref[here, :], -sin_ref[here, :]).astype(BF16)
            dv = dv_sum[here, :]
            dv_ref[there, :] = (dv + pltpu.roll(dv, HEAD_DIM, 1)).astype(BF16)


def attention_specs():
    tile = pl.BlockSpec((PACK, 2 * HEAD_DIM), lambda p, slot: (0, p))
    group = pl.BlockSpec((PACK, 2 * HEAD_DIM), lambda p, slot: (0, p // (GROUP // 2)))
    lse = pl.BlockSpec((1, 2, PACK), lambda p, slot: (p, 0, 0))
    table = pl.BlockSpec((PACK, 2 * HEAD_DIM), lambda p, slot: (0, 0))
    col = pl.BlockSpec((PACK, 1), lambda p, slot: (0, 0))
    row = pl.BlockSpec((1, PACK), lambda p, slot: (0, 0))
    return tile, group, lse, [table, table, col, row]


def attend_forward(slots, query, key, value, tables):
    pairs = query.shape[1] // (2 * HEAD_DIM)
    groups = key.shape[1] // (2 * HEAD_DIM)
    tile, group, lse, rest = attention_specs()
    blocks = PACK // QBLOCK
    return pl.pallas_call(
        lambda *refs: forward_body(blocks, *refs),
        grid_spec=pltpu.PrefetchScalarGridSpec(
            num_scalar_prefetch=1,
            grid=(pairs,),
            in_specs=[tile, group, group] + rest,
            out_specs=[tile, group, group, tile, lse],
        ),
        out_shape=[
            jax.ShapeDtypeStruct((PACK, pairs * 2 * HEAD_DIM), BF16),
            jax.ShapeDtypeStruct((PACK, groups * 2 * HEAD_DIM), BF16),
            jax.ShapeDtypeStruct((PACK, groups * 2 * HEAD_DIM), BF16),
            jax.ShapeDtypeStruct((PACK, pairs * 2 * HEAD_DIM), BF16),
            jax.ShapeDtypeStruct((pairs, 2, PACK), F32),
        ],
        cost_estimate=pl.CostEstimate(
            flops=4 * pairs * 2 * PACK * PACK * HEAD_DIM,
            transcendentals=pairs * PACK * PACK,
            bytes_accessed=8 * PACK * MODEL_WIDTH,
        ),
        name="attend_forward",
    )(slots, query, key, value, *tables)


def attend_backward(slots, saved, grad, log_totals, tables):
    query, key, value = saved
    pairs = query.shape[1] // (2 * HEAD_DIM)
    groups = key.shape[1] // (2 * HEAD_DIM)
    tile, group, lse, rest = attention_specs()
    blocks = PACK // QBLOCK
    return pl.pallas_call(
        lambda *refs: backward_body(blocks, *refs),
        grid_spec=pltpu.PrefetchScalarGridSpec(
            num_scalar_prefetch=1,
            grid=(pairs,),
            in_specs=[tile, group, group, tile, lse] + rest,
            out_specs=[tile, group, group],
            scratch_shapes=[pltpu.VMEM((PACK, 2 * HEAD_DIM), F32)] * 2,
        ),
        out_shape=[
            jax.ShapeDtypeStruct((PACK, pairs * 2 * HEAD_DIM), BF16),
            jax.ShapeDtypeStruct((PACK, groups * 2 * HEAD_DIM), BF16),
            jax.ShapeDtypeStruct((PACK, groups * 2 * HEAD_DIM), BF16),
        ],
        cost_estimate=pl.CostEstimate(
            flops=10 * pairs * 2 * PACK * PACK * HEAD_DIM,
            transcendentals=pairs * PACK * PACK,
            bytes_accessed=8 * PACK * MODEL_WIDTH,
        ),
        name="attend_backward",
    )(slots, query, key, value, grad, log_totals, *tables)


def reverse_bits(value, count):
    out, bit, other = 0, 1, count >> 1
    while other:
        out = out + jnp.where((value & bit) != 0, other, 0)
        bit, other = bit << 1, other >> 1
    return out


def reduce_scatter_rows(total):
    count = lax.axis_size("fsdp")
    me = lax.axis_index("fsdp")
    for bit in reversed(bits_down(count)):
        half = total.shape[0] // 2
        high = ((me & bit) != 0).astype(jnp.int32)
        keep = lax.dynamic_slice_in_dim(total, high * half, half, 0)
        give = lax.dynamic_slice_in_dim(total, (1 - high) * half, half, 0)
        got = swap(give.astype(BF16), "fsdp", bit)
        total = (keep.astype(F32) + got.astype(F32)).astype(BF16)
    return total


def share_out(total):
    count, seqs = lax.axis_size("fsdp"), lax.axis_size("seq")
    me, me_seq = lax.axis_index("fsdp"), lax.axis_index("seq")
    rows, columns = total.shape
    piece = reduce_scatter_rows(total.astype(BF16))
    for bit in bits_down(count):
        piece = jnp.concatenate([piece, swap(piece, "fsdp", bit)], axis=0)
    pieces = gather_relative(piece, "seq")
    targets = jnp.stack(
        [
            (me_seq ^ s) * count + reverse_bits(me ^ o, count)
            for s in relative_order(seqs)
            for o in relative_order(count)
        ]
    )
    return place_blocks(pieces, count, targets).reshape(seqs, rows, columns)


def shards(
    tokens,
    cotangent,
    lengths,
    sequence_adapter,
    attention_norm_gain,
    feedfwd_norm_gain,
    query_matrix,
    key_matrix,
    value_matrix,
    output_matrix,
    gate_matrix,
    up_matrix,
    down_matrix,
    adapter_first_factors,
    adapter_first_down,
    adapter_second_model,
    adapter_second_keyvalue,
    adapter_second_feedfwd,
):
    seqs, fsdps = lax.axis_size("seq"), lax.axis_size("fsdp")
    me = lax.axis_index("seq")
    order = relative_order(seqs)
    peers = [me ^ o for o in order]
    resid_in = tokens[0]
    row_count = resid_in.shape[0]
    width = MODEL_WIDTH // seqs
    kv_width = KV_HEADS * HEAD_DIM // seqs
    my_groups = KV_HEADS // seqs
    feed_units = gate_matrix.shape[1]
    unit_block = feed_units // (seqs * fsdps)
    units = feed_units // seqs
    parts = units // width

    def columns_of(array, peer, count):
        return lax.dynamic_slice_in_dim(array, peer * count, count, array.ndim - 1)

    def rows_of(array, peer):
        return lax.dynamic_slice_in_dim(array, peer * row_count, row_count, 0)

    def relative_rows(array):
        return jnp.concatenate([rows_of(array, peer) for peer in peers], axis=0)

    def blocks_of(array):
        return [array[k * row_count : (k + 1) * row_count] for k in range(seqs)]

    def exchange(pieces):
        return [p if o == 0 else swap(p, "seq", o) for o, p in zip(order, pieces)]

    def place_columns(pieces):
        rows, count = pieces[0].shape
        whole = jnp.zeros((rows, count * seqs), pieces[0].dtype)
        for peer, piece in zip(peers, pieces):
            whole = lax.dynamic_update_slice(whole, piece, (0, peer * count))
        return whole

    def my_units(matrix):
        parted = matrix.reshape(matrix.shape[0], fsdps, seqs, unit_block)
        return lax.dynamic_index_in_dim(parted, me, 2, keepdims=False).reshape(
            matrix.shape[0], units
        )

    rings = Rings()
    qkv_share = jnp.concatenate(
        [
            columns_of(query_matrix, me, width),
            columns_of(key_matrix, me, kv_width),
            columns_of(value_matrix, me, kv_width),
        ],
        axis=1,
    )
    out_share = columns_of(output_matrix, me, width)
    gate_share, up_share = my_units(gate_matrix), my_units(up_matrix)
    down_share = lax.dynamic_slice_in_dim(down_matrix, me * unit_block, unit_block, 0)
    lists = rings.gather([qkv_share, out_share, gate_share, up_share, down_share])
    qkv_mine, out_mine, gate_full, up_full, down_full = (
        place_blocks(blocks, 1, rings.owner) for blocks in lists
    )

    segment, position, valid_row, onehot = pack_tables(
        lengths[0], sequence_adapter[0], PACK, ADAPTER_TOTAL
    )
    valid_all = jnp.where(valid_row, 1.0, 0.0).astype(F32)[:, None]
    mask_all = jnp.repeat(onehot, ADAPTER_RANK, axis=1).astype(BF16)
    valid_rel = relative_rows(valid_all)
    mask_rel = relative_rows(mask_all)
    valid_col, mask_own = valid_rel[:row_count], mask_rel[:row_count]
    mask_own_three = jnp.tile(mask_own, (1, 3))
    mask_rel_two = jnp.tile(mask_rel, (1, 2))
    mask_rel_three = jnp.tile(mask_rel, (1, 3))
    cosine, sine = rope_tables(position, HEAD_DIM, 2)
    tables = (cosine, sine, segment[:, None], segment[None, :])
    slot_of = [0] * seqs
    for k, o in enumerate(order):
        slot_of[o] = k
    slot_table = jnp.array(slot_of, jnp.int32)
    sub = row_count // QBLOCK if row_count >= QBLOCK else 1
    if row_count >= QBLOCK:
        slots = jnp.stack(
            [
                slot_table[me ^ (j // sub)] * sub + j % sub
                for j in range(PACK // QBLOCK)
            ]
        )
    else:
        slots = jnp.arange(PACK // QBLOCK, dtype=jnp.int32)

    def to_kernel(array):
        if row_count >= QBLOCK:
            return array
        whole = jnp.zeros_like(array)
        for peer, piece in zip(peers, blocks_of(array)):
            whole = lax.dynamic_update_slice(whole, piece, (peer * row_count, 0))
        return whole

    def from_kernel(array):
        return array if row_count >= QBLOCK else relative_rows(array)

    hidden_in = resid_in.astype(F32)
    normed_own = rms_norm(hidden_in, attention_norm_gain).astype(BF16)
    normed_one = jnp.concatenate(gather_relative(normed_own, "seq"), axis=0)
    first_qkv = jnp.concatenate([adapter_first_factors[k] for k in range(3)], axis=1)
    low_qkv = (mm(normed_one, first_qkv) * mask_rel_three).astype(BF16)
    low_q, low_k, low_v = (low_qkv[:, k * SPAN : (k + 1) * SPAN] for k in range(3))
    second_q = [columns_of(adapter_second_model[0], peer, width) for peer in peers]
    second_k = [columns_of(adapter_second_keyvalue[0], peer, kv_width) for peer in peers]
    second_v = [columns_of(adapter_second_keyvalue[1], peer, kv_width) for peer in peers]

    def twice(rows):
        heads = [rows[:, g * HEAD_DIM : (g + 1) * HEAD_DIM] for g in range(my_groups)]
        return jnp.concatenate([h for h in heads for _ in (0, 1)], axis=1)

    projected = mm(normed_one, qkv_mine)
    query = projected[:, :width] + mm(low_q, second_q[0])
    key = projected[:, width : width + kv_width] + mm(low_k, second_k[0])
    value = projected[:, width + kv_width :] + mm(low_v, second_v[0])
    *saved, attn_heads, log_totals = attend_forward(
        slots, to_kernel(query), to_kernel(twice(key)), to_kernel(twice(value)), tables
    )
    attn_heads = from_kernel(attn_heads)
    attn_own = place_columns(exchange(blocks_of(attn_heads)))
    out_weights = gather_relative(out_mine, "seq")
    low_o = (mm(attn_own, adapter_first_factors[3]) * mask_own).astype(BF16)
    branch = place_columns([mm(attn_own, piece) for piece in out_weights]) + mm(
        low_o, adapter_second_model[1]
    )
    hidden_mid = hidden_in + RESIDUAL_FACTOR * branch
    normed_two_own = rms_norm(hidden_mid, feedfwd_norm_gain).astype(BF16)

    normed_two = jnp.concatenate(gather_relative(normed_two_own, "seq"), axis=0)
    cot_all = jnp.concatenate(gather_relative(cotangent[0], "seq"), axis=0)
    first_ffn = jnp.concatenate([adapter_first_factors[4], adapter_first_factors[5]], axis=1)
    low_ffn = (mm(normed_two, first_ffn) * mask_rel_two).astype(BF16)
    low_g, low_u = low_ffn[:, :SPAN], low_ffn[:, SPAN:]
    second_gate = my_units(adapter_second_feedfwd[0])
    second_up = my_units(adapter_second_feedfwd[1])
    gate = mm(normed_two, gate_full) + mm(low_g, second_gate)
    up = mm(normed_two, up_full) + mm(low_u, second_up)

    def swiglu(gate_arg, up_arg):
        return jax.nn.sigmoid(gate_arg) * gate_arg * up_arg

    act = swiglu(gate, up).astype(BF16)
    first_down = lax.dynamic_index_in_dim(
        adapter_first_down.reshape(fsdps, seqs, unit_block, SPAN), me, 1, keepdims=False
    ).reshape(units, SPAN)
    low_d = (mm(act, first_down) * mask_rel).astype(BF16)
    down_part = mm(act, down_full) + mm(low_d, adapter_second_model[2])
    down_sum = reduce_relative(blocks_of(down_part), "seq")
    layer_out = (valid_col * (hidden_mid + RESIDUAL_FACTOR * down_sum)).astype(BF16)

    grad_out = cotangent[0].astype(F32) * valid_col
    grad_down = (RESIDUAL_FACTOR * (cot_all.astype(F32) * valid_rel)).astype(BF16)
    grad_low_d = mm_nt(grad_down, adapter_second_model[2]).astype(BF16) * mask_rel
    grad_b_down = mm_tn(low_d, grad_down)
    grad_a_down = mm_tn(grad_low_d, act)
    grad_act = mm_nt(grad_down, down_full) + mm_nt(grad_low_d, first_down)
    _, swiglu_back = jax.vjp(swiglu, gate, up)
    grad_gate, grad_up = swiglu_back(grad_act)
    grad_gate, grad_up = grad_gate.astype(BF16), grad_up.astype(BF16)
    grad_low_ffn = (
        jnp.concatenate([mm_nt(grad_gate, second_gate), mm_nt(grad_up, second_up)], axis=1).astype(
            BF16
        )
        * mask_rel_two
    )
    grad_b_gate = mm_tn(low_g, grad_gate)
    grad_b_up = mm_tn(low_u, grad_up)
    grad_a_ffn = mm_tn(grad_low_ffn, normed_two)
    grad_normed_two = (
        mm_nt(grad_gate, gate_full) + mm_nt(grad_up, up_full) + mm_nt(grad_low_ffn, first_ffn)
    )
    grad_normed_two = reduce_relative(blocks_of(grad_normed_two), "seq")
    _, norm_two_back = jax.vjp(lambda hidden: rms_norm(hidden, feedfwd_norm_gain), hidden_mid)
    grad_mid = grad_out + norm_two_back(grad_normed_two)[0]

    grad_branch = (RESIDUAL_FACTOR * grad_mid).astype(BF16)
    grad_low_o = mm_nt(grad_branch, adapter_second_model[1]).astype(BF16) * mask_own
    grad_b_out = mm_tn(low_o, grad_branch)
    grad_a_out = mm_tn(grad_low_o, attn_own)
    grad_attn = mm_nt(grad_low_o, adapter_first_factors[3])
    for peer, piece in zip(peers, out_weights):
        grad_attn = grad_attn + mm_nt(columns_of(grad_branch, peer, width), piece)
    grad_attn = grad_attn.astype(BF16)
    grad_heads = jnp.concatenate(
        exchange([columns_of(grad_attn, peer, width) for peer in peers]), axis=0
    )
    grad_query, grad_key, grad_value = (
        from_kernel(g)
        for g in attend_backward(slots, saved, to_kernel(grad_heads), log_totals, tables)
    )

    def once(rows):
        return jnp.concatenate(
            [rows[:, 2 * g * HEAD_DIM : (2 * g + 1) * HEAD_DIM] for g in range(my_groups)], axis=1
        )

    grad_key, grad_value = once(grad_key), once(grad_value)
    grad_qkv = jnp.concatenate([grad_query, grad_key, grad_value], axis=1)
    grad_pieces = exchange(blocks_of(grad_qkv))
    qkv_weights = gather_relative(qkv_mine, "seq")
    grad_b_q = mm_tn(low_q, grad_query)
    grad_b_kv = [mm_tn(low_k, grad_key), mm_tn(low_v, grad_value)]
    low_grads = [jnp.zeros((row_count, SPAN), F32)] * 3
    for k in range(seqs):
        piece = grad_pieces[k]
        low_grads = [
            low_grads[0] + mm_nt(piece[:, :width], second_q[k]),
            low_grads[1] + mm_nt(piece[:, width : width + kv_width], second_k[k]),
            low_grads[2] + mm_nt(piece[:, width + kv_width :], second_v[k]),
        ]
    grad_low_qkv = jnp.concatenate(low_grads, axis=1).astype(BF16) * mask_own_three
    grad_low_all = jnp.concatenate(gather_relative(grad_low_qkv, "seq"), axis=0)
    grad_a_qkv = mm_tn(grad_low_all, columns_of(normed_one, me, width))
    grad_normed_one = mm_nt(grad_low_qkv, first_qkv)
    for k in range(seqs):
        grad_normed_one = grad_normed_one + mm_nt(grad_pieces[k], qkv_weights[k])
    _, norm_one_back = jax.vjp(lambda hidden: rms_norm(hidden, attention_norm_gain), hidden_in)
    grad_input = (grad_mid + norm_one_back(grad_normed_one)[0]).astype(BF16)

    factor = ADAPTER_TOTAL / math.sqrt(PACK * fsdps)

    def split_units(rows):
        return [rows[:, k * width : (k + 1) * width].astype(BF16) for k in range(parts)]

    def seq_share(rows):
        return reduce_relative(
            [columns_of(rows, peer, width) for peer in peers], "seq"
        ).astype(BF16)

    def rows_out(whole, first, count):
        return whole[:, first : first + count].transpose(1, 0, 2).reshape(count, MODEL_WIDTH)

    def units_out(whole, first):
        part = whole[:, first : first + parts * SPAN]
        part = part.reshape(seqs, parts, SPAN, fsdps // parts, unit_block)
        return part.transpose(2, 1, 3, 0, 4).reshape(SPAN, feed_units)

    early = share_out(
        jnp.concatenate(
            [seq_share(jnp.concatenate([grad_a_ffn, grad_b_down], axis=0))]
            + split_units(grad_a_down)
            + split_units(grad_b_gate)
            + split_units(grad_b_up),
            axis=0,
        )
    )
    blank = jnp.zeros((SPAN, width - 2 * kv_width), BF16)
    middle = share_out(
        jnp.concatenate(
            [
                seq_share(jnp.concatenate([grad_a_out, grad_b_out], axis=0)),
                grad_b_q.astype(BF16),
                jnp.concatenate([g.astype(BF16) for g in grad_b_kv] + [blank], axis=1),
            ],
            axis=0,
        )
    )
    late = share_out(grad_a_qkv)

    def scaled(array):
        return array.astype(F32) * factor

    a_rows = jnp.concatenate(
        [rows_out(late, 0, 3 * SPAN), rows_out(middle, 0, SPAN), rows_out(early, 0, 2 * SPAN)],
        axis=0,
    )
    base = 3 * SPAN
    b_kv = middle[:, 3 * SPAN :, : 2 * kv_width].reshape(seqs, SPAN, 2, kv_width)
    return (
        layer_out[None],
        grad_input[None],
        scaled(a_rows.reshape(6, SPAN, MODEL_WIDTH).transpose(0, 2, 1)),
        scaled(units_out(early, base).T),
        scaled(
            jnp.stack(
                [
                    rows_out(middle, 2 * SPAN, SPAN),
                    rows_out(middle, SPAN, SPAN),
                    rows_out(early, 2 * SPAN, SPAN),
                ]
            )
        ),
        scaled(b_kv.transpose(2, 1, 0, 3).reshape(2, SPAN, KV_HEADS * HEAD_DIM)),
        scaled(
            jnp.stack(
                [units_out(early, base + parts * SPAN), units_out(early, base + 2 * parts * SPAN)]
            )
        ),
    )


def solution(mesh):
    rows = P("fsdp", None)
    placed = (
        (P("fsdp", "seq", None),) * 2 + (rows,) * 2 + (P(),) * 2 + (rows,) * 7 + (P(),) * 5
    )
    return jax.shard_map(
        shards,
        mesh=mesh,
        in_specs=placed,
        out_specs=(P("fsdp", "seq", None), P("fsdp", "seq", None), P(), P(), P(), P(), P()),
        check_vma=False,
    )
```

```python
import math

import jax
import jax.numpy as jnp
from jax import lax
from jax.experimental import pallas as pl
from jax.experimental.pallas import tpu as pltpu
from jax.sharding import PartitionSpec as P

MODEL_WIDTH = 2048
HEADS = 32
KV_HEADS = 8
HEAD_DIM = 64
ADAPTER_RANK = 16
ADAPTER_TOTAL = 8
PACK = 1024
QBLOCK = 256
SPAN = ADAPTER_TOTAL * ADAPTER_RANK
GROUP = HEADS // KV_HEADS

SCORE_SCALE = 0.015625
RESIDUAL_FACTOR = 0.22
NORM_EPSILON = 1e-05
ROPE_BASE = 10000000.0
MASK_FILL = 1e30

BF16 = jnp.bfloat16
F32 = jnp.float32


def mm(left, right):
    return jnp.dot(left, right, preferred_element_type=F32)


def mm_nt(left, right):
    return lax.dot_general(left, right, (((1,), (1,)), ((), ())), preferred_element_type=F32)


def mm_tn(left, right):
    return lax.dot_general(left, right, (((0,), (0,)), ((), ())), preferred_element_type=F32)


def rms_norm(hidden, gain_vec):
    mean_square = jnp.mean(hidden * hidden, axis=-1, keepdims=True)
    return hidden * lax.rsqrt(mean_square + NORM_EPSILON) * gain_vec


def pack_tables(seq_lengths, adapter_id, token_count, adapter_count):
    slots = seq_lengths.shape[0]
    places = jnp.arange(token_count, dtype=jnp.int32)
    seq_ends = jnp.cumsum(seq_lengths)
    seq_starts = seq_ends - seq_lengths
    used_len = seq_ends[slots - 1]
    segment = jnp.sum((places[:, None] >= seq_ends[None, :]).astype(jnp.int32), axis=1)
    member = segment[:, None] == jnp.arange(slots, dtype=jnp.int32)[None, :]
    start_tok = jnp.sum(jnp.where(member, seq_starts[None, :], 0), axis=1) + jnp.where(
        segment == slots, used_len, 0
    )
    position = places - start_tok
    valid_row = segment < slots
    chosen = adapter_id[:, None] == jnp.arange(adapter_count, dtype=jnp.int32)[None, :]
    onehot = jnp.sum(jnp.where(member[:, :, None] & chosen[None, :, :], 1.0, 0.0), axis=1).astype(F32)
    return (segment, position, valid_row, onehot)


def rope_tables(position, head_size, copies):
    frequency = ROPE_BASE ** (-(jnp.arange(head_size // 2, dtype=F32) * 2.0) / head_size)
    angles = position.astype(F32)[:, None] * frequency[None, :]
    cosine, sine = jnp.cos(angles), jnp.sin(angles)
    return (jnp.tile(cosine, (1, 2 * copies)), jnp.tile(sine, (1, 2 * copies)))


def bits_down(count):
    bits, bit = [], count >> 1
    while bit:
        bits.append(bit)
        bit >>= 1
    return bits


def relative_order(count):
    order = [0]
    for bit in bits_down(count):
        order = order + [o ^ bit for o in order]
    return order


def swap(block, axis, offset):
    count = lax.axis_size(axis)
    return lax.ppermute(block, axis, [(i, i ^ offset) for i in range(count)])


def gather_relative(block, axis):
    pieces = [block]
    for bit in bits_down(lax.axis_size(axis)):
        pieces = pieces + [swap(piece, axis, bit) for piece in pieces]
    return pieces


def reduce_relative(pieces, axis):
    for bit in reversed(bits_down(lax.axis_size(axis))):
        half = len(pieces) // 2
        got = [swap(piece.astype(BF16), axis, bit) for piece in pieces[half:]]
        pieces = [mine.astype(F32) + other.astype(F32) for mine, other in zip(pieces[:half], got)]
    return pieces[0]


def cycle_of(count):
    return list(range(0, count, 2)) + list(range(count - 1, 0, -2))


class Rings:
    WINDOW = 3

    def __init__(self):
        self.count = lax.axis_size("fsdp")
        cycle = cycle_of(self.count)
        place = {device: k for k, device in enumerate(cycle)}
        table = [
            [cycle[(place[device] - k) % self.count] for k in range(self.count)]
            for device in range(self.count)
        ]
        self.owner = lax.dynamic_index_in_dim(
            jnp.array(table, jnp.int32), lax.axis_index("fsdp"), 0, keepdims=False
        )
        ahead = [(cycle[k], cycle[(k + 1) % self.count]) for k in range(self.count)]
        self.perms = (ahead, [(b, a) for a, b in ahead])
        self.sent = ([], [])

    def send(self, way, block):
        sent = self.sent[way]
        if len(sent) >= self.WINDOW:
            block, _ = lax.optimization_barrier((block, sent[-self.WINDOW]))
        got = lax.ppermute(block, "fsdp", self.perms[way])
        sent.append(got)
        return got

    def gather(self, blocks, starts):
        half = self.count // 2
        found = [{0: block} for block in blocks]
        latest = [[block, block] for block in blocks]
        for time in range(1, half + max(starts) + 1):
            for which in range(len(blocks)):
                step = time - starts[which]
                if not 1 <= step <= half:
                    continue
                for way in (0, 1):
                    if step == half and way != which % 2:
                        continue
                    got = self.send(way, latest[which][way])
                    latest[which][way] = got
                    found[which][step if way == 0 else self.count - step] = got
        return [[f[k] for k in range(self.count)] for f in found]


def place_blocks(pieces, counts, targets):
    rows = pieces[0].shape[0] // counts
    columns = pieces[0].shape[1]
    total = len(pieces) * counts

    def body(target_ref, *refs):
        out_ref, held, came, left = refs[-4:]
        arrivals, departures = [], []
        for i in range(len(pieces)):
            for j in range(counts):
                k = i * counts + j
                first = pl.multiple_of(target_ref[k] * rows, rows)
                arrivals.append(
                    pltpu.make_async_copy(
                        refs[i].at[pl.ds(j * rows, rows), :], held.at[k], came.at[k]
                    )
                )
                departures.append(
                    pltpu.make_async_copy(
                        held.at[k], out_ref.at[pl.ds(first, rows), :], left.at[k]
                    )
                )
        for copy in arrivals:
            copy.start()
        for arrival, departure in zip(arrivals, departures):
            arrival.wait()
            departure.start()
        for copy in departures:
            copy.wait()

    return pl.pallas_call(
        body,
        out_shape=jax.ShapeDtypeStruct((rows * total, columns), pieces[0].dtype),
        grid_spec=pltpu.PrefetchScalarGridSpec(
            num_scalar_prefetch=1,
            grid=(),
            in_specs=[pl.BlockSpec(memory_space=pl.ANY)] * len(pieces),
            out_specs=pl.BlockSpec(memory_space=pl.ANY),
            scratch_shapes=[
                pltpu.VMEM((total, rows, columns), pieces[0].dtype),
                pltpu.SemaphoreType.DMA((total,)),
                pltpu.SemaphoreType.DMA((total,)),
            ],
        ),
        cost_estimate=pl.CostEstimate(
            flops=0, transcendentals=0, bytes_accessed=4 * rows * total * columns
        ),
        name="place_blocks",
    )(targets.astype(jnp.int32), *pieces)


def after(value, *others):
    return lax.optimization_barrier((value, others))[0]


def take_units(matrices, peer, seqs, runs, unit_block):
    if unit_block % 128:
        return [
            lax.dynamic_index_in_dim(
                m.reshape(m.shape[0], runs, seqs, unit_block), peer, 2, keepdims=False
            ).reshape(m.shape[0], runs * unit_block)
            for m in matrices
        ]

    def body(peer_ref, *refs):
        for source, target in zip(refs[: len(matrices)], refs[len(matrices) :]):
            target[...] = source[...]

    return pl.pallas_call(
        body,
        grid_spec=pltpu.PrefetchScalarGridSpec(
            num_scalar_prefetch=1,
            grid=(runs,),
            in_specs=[
                pl.BlockSpec((m.shape[0], unit_block), lambda f, at: (0, f * seqs + at[0]))
                for m in matrices
            ],
            out_specs=[
                pl.BlockSpec((m.shape[0], unit_block), lambda f, at: (0, f)) for m in matrices
            ],
        ),
        out_shape=[
            jax.ShapeDtypeStruct((m.shape[0], runs * unit_block), m.dtype) for m in matrices
        ],
        name="take_units",
    )(peer.astype(jnp.int32)[None], *matrices)


def finish_units(whole, first, parts, runs, unit_block, factor):
    seqs, _, columns = whole.shape
    feed_units = seqs * runs * unit_block
    per = runs // parts

    def body(down_ref, gate_ref, up_ref, a_ref, b_ref):
        for s in range(seqs):
            here = slice(s * unit_block, (s + 1) * unit_block)
            a_ref[here, :] = down_ref[s].astype(F32).T * factor
            b_ref[0, :, here] = gate_ref[s].astype(F32) * factor
            b_ref[1, :, here] = up_ref[s].astype(F32) * factor

    def part(which):
        base = first // SPAN + which * parts
        return pl.BlockSpec((seqs, SPAN, unit_block), lambda k, g: (0, base + k, g))

    return pl.pallas_call(
        body,
        grid=(parts, per),
        in_specs=[part(0), part(1), part(2)],
        out_specs=[
            pl.BlockSpec((seqs * unit_block, SPAN), lambda k, g: (k * per + g, 0)),
            pl.BlockSpec((2, SPAN, seqs * unit_block), lambda k, g: (0, 0, k * per + g)),
        ],
        out_shape=[
            jax.ShapeDtypeStruct((feed_units, SPAN), F32),
            jax.ShapeDtypeStruct((2, SPAN, feed_units), F32),
        ],
        name="finish_units",
    )(whole, whole, whole)


def finish_model(early, middle, factor):
    seqs, _, columns = early.shape

    def body(early_ref, middle_ref, a_ref, b_ref):
        a_ref[0] = middle_ref[0, :SPAN].astype(F32).T * factor
        a_ref[1] = early_ref[0, :SPAN].astype(F32).T * factor
        a_ref[2] = early_ref[0, SPAN : 2 * SPAN].astype(F32).T * factor
        b_ref[0] = middle_ref[0, 2 * SPAN :].astype(F32) * factor
        b_ref[1] = middle_ref[0, SPAN : 2 * SPAN].astype(F32) * factor
        b_ref[2] = early_ref[0, 2 * SPAN :].astype(F32) * factor

    spec = pl.BlockSpec((1, 3 * SPAN, columns), lambda s: (s, 0, 0))
    return pl.pallas_call(
        body,
        grid=(seqs,),
        in_specs=[spec, spec],
        out_specs=[
            pl.BlockSpec((3, columns, SPAN), lambda s: (1, s, 0)),
            pl.BlockSpec((3, SPAN, columns), lambda s: (0, 0, s)),
        ],
        out_shape=[
            jax.ShapeDtypeStruct((6, MODEL_WIDTH, SPAN), F32),
            jax.ShapeDtypeStruct((3, SPAN, MODEL_WIDTH), F32),
        ],
        name="finish_model",
    )(early, middle)


def finish_late(late, a_all, factor):
    seqs, _, columns = late.shape

    def body(late_ref, held_ref, a_ref):
        for j in range(3):
            a_ref[j] = late_ref[0, j * SPAN : (j + 1) * SPAN].astype(F32).T * factor

    return pl.pallas_call(
        body,
        grid=(seqs,),
        in_specs=[
            pl.BlockSpec((1, 3 * SPAN, columns), lambda s: (s, 0, 0)),
            pl.BlockSpec(memory_space=pl.ANY),
        ],
        out_specs=pl.BlockSpec((3, columns, SPAN), lambda s: (0, s, 0)),
        out_shape=jax.ShapeDtypeStruct(a_all.shape, F32),
        input_output_aliases={1: 0},
        name="finish_late",
    )(late, a_all)


def half_lanes(shape):
    lane = lax.broadcasted_iota(jnp.int32, shape, 1)
    return lane % HEAD_DIM < HEAD_DIM // 2


def turn_tile(x, cosine, sine):
    quarter = HEAD_DIM // 2
    ahead = pltpu.roll(x, 2 * HEAD_DIM - quarter, 1)
    behind = pltpu.roll(x, quarter, 1)
    return x * cosine + jnp.where(half_lanes(x.shape), -ahead, behind) * sine


def dot_tn(left, right):
    return lax.dot_general(left, right, (((0,), (0,)), ((), ())), preferred_element_type=F32)


def dot_nt(left, right):
    return lax.dot_general(left, right, (((1,), (1,)), ((), ())), preferred_element_type=F32)


def allowed_pairs(seg_col, seg_row, block):
    keys = (block + 1) * QBLOCK
    shape = (keys, QBLOCK)
    key_at = lax.broadcasted_iota(jnp.int32, shape, 0)
    query_at = lax.broadcasted_iota(jnp.int32, shape, 1) + block * QBLOCK
    same = seg_col[:keys, :] == seg_row[:, block * QBLOCK : keys]
    return same & (key_at <= query_at)


def forward_body(
    blocks, slot_ref, q_ref, k_ref, v_ref, cos_ref, sin_ref, col_ref, row_ref,
    qn_ref, kn_ref, vn_ref, out_ref, lse_ref,
):
    for j in range(blocks):
        here = slice(j * QBLOCK, (j + 1) * QBLOCK)
        there = pl.ds(pl.multiple_of(slot_ref[j] * QBLOCK, QBLOCK), QBLOCK)
        cosine, sine = cos_ref[here, :], sin_ref[here, :]
        qn_ref[here, :] = turn_tile(q_ref[there, :], cosine, sine).astype(BF16)
        kn_ref[here, :] = turn_tile(k_ref[there, :], cosine, sine).astype(BF16)
        vn_ref[here, :] = v_ref[there, :].astype(BF16)
    lane = lax.broadcasted_iota(jnp.int32, (QBLOCK, 2 * HEAD_DIM), 1)
    row = lax.broadcasted_iota(jnp.int32, (2 * HEAD_DIM, QBLOCK), 0)
    for i in range(blocks):
        here = slice(i * QBLOCK, (i + 1) * QBLOCK)
        keys = (i + 1) * QBLOCK
        allowed = allowed_pairs(col_ref[...], row_ref[...], i)
        query = (qn_ref[here, :].astype(F32) * SCORE_SCALE).astype(BF16)
        outs = []
        for e in range(2):
            mine = jnp.where(lane // HEAD_DIM == e, query, jnp.zeros_like(query))
            scores = jnp.where(allowed, dot_nt(kn_ref[:keys, :], mine), -MASK_FILL)
            most = jnp.max(scores, axis=0, keepdims=True)
            exponent = jnp.exp(scores - most)
            total = jnp.sum(exponent, axis=0, keepdims=True)
            probs = (exponent * (1.0 / total)).astype(BF16)
            lse_ref[0, e : e + 1, here] = most + jnp.log(total)
            outs.append(dot_tn(vn_ref[:keys, :], probs))
        out = jnp.where(row < HEAD_DIM, outs[0], outs[1]).T
        there = pl.ds(pl.multiple_of(slot_ref[i] * QBLOCK, QBLOCK), QBLOCK)
        out_ref[there, :] = out.astype(BF16)


def backward_body(
    blocks, slot_ref, qn_ref, kn_ref, vn_ref, do_ref, lse_ref, cos_ref, sin_ref, col_ref, row_ref,
    dq_ref, dk_ref, dv_ref, dk_sum, dv_sum,
):
    pairs_per_group = GROUP // 2
    step = lax.rem(pl.program_id(0), pairs_per_group)

    @pl.when(step == 0)
    def _():
        dk_sum[...] = jnp.zeros_like(dk_sum)
        dv_sum[...] = jnp.zeros_like(dv_sum)

    lane = lax.broadcasted_iota(jnp.int32, (QBLOCK, 2 * HEAD_DIM), 1)
    row = lax.broadcasted_iota(jnp.int32, (2 * HEAD_DIM, QBLOCK), 0)
    for i in range(blocks):
        here = slice(i * QBLOCK, (i + 1) * QBLOCK)
        there = pl.ds(pl.multiple_of(slot_ref[i] * QBLOCK, QBLOCK), QBLOCK)
        keys = (i + 1) * QBLOCK
        allowed = allowed_pairs(col_ref[...], row_ref[...], i)
        query = (qn_ref[here, :].astype(F32) * SCORE_SCALE).astype(BF16)
        grad = do_ref[there, :]
        outs = []
        for e in range(2):
            mine = jnp.where(lane // HEAD_DIM == e, query, jnp.zeros_like(query))
            grad_mine = jnp.where(lane // HEAD_DIM == e, grad, jnp.zeros_like(grad))
            scores = jnp.where(allowed, dot_nt(kn_ref[:keys, :], mine), -MASK_FILL)
            probs = jnp.exp(scores - lse_ref[0, e : e + 1, here])
            grad_probs = dot_nt(vn_ref[:keys, :], grad_mine)
            delta = jnp.sum(probs * grad_probs, axis=0, keepdims=True)
            grad_scores = (probs * (grad_probs - delta)).astype(BF16)
            dv_sum[:keys, :] += jnp.dot(probs.astype(BF16), grad_mine, preferred_element_type=F32)
            dk_sum[:keys, :] += jnp.dot(grad_scores, mine, preferred_element_type=F32)
            outs.append(dot_tn(kn_ref[:keys, :], grad_scores))
        out = jnp.where(row < HEAD_DIM, outs[0], outs[1]).T * SCORE_SCALE
        out = out.astype(BF16).astype(F32)
        dq_ref[there, :] = turn_tile(out, cos_ref[here, :], -sin_ref[here, :]).astype(BF16)

    @pl.when(step == pairs_per_group - 1)
    def _():
        for j in range(blocks):
            here = slice(j * QBLOCK, (j + 1) * QBLOCK)
            there = pl.ds(pl.multiple_of(slot_ref[j] * QBLOCK, QBLOCK), QBLOCK)
            dk = dk_sum[here, :]
            dk = (dk + pltpu.roll(dk, HEAD_DIM, 1)).astype(BF16).astype(F32)
            dk_ref[there, :] = turn_tile(dk, cos_ref[here, :], -sin_ref[here, :]).astype(BF16)
            dv = dv_sum[here, :]
            dv_ref[there, :] = (dv + pltpu.roll(dv, HEAD_DIM, 1)).astype(BF16)


def attention_specs():
    tile = pl.BlockSpec((PACK, 2 * HEAD_DIM), lambda p, slot: (0, p))
    group = pl.BlockSpec((PACK, 2 * HEAD_DIM), lambda p, slot: (0, p // (GROUP // 2)))
    lse = pl.BlockSpec((1, 2, PACK), lambda p, slot: (p, 0, 0))
    table = pl.BlockSpec((PACK, 2 * HEAD_DIM), lambda p, slot: (0, 0))
    col = pl.BlockSpec((PACK, 1), lambda p, slot: (0, 0))
    row = pl.BlockSpec((1, PACK), lambda p, slot: (0, 0))
    return tile, group, lse, [table, table, col, row]


def attend_forward(slots, query, key, value, tables):
    pairs = query.shape[1] // (2 * HEAD_DIM)
    groups = key.shape[1] // (2 * HEAD_DIM)
    tile, group, lse, rest = attention_specs()
    blocks = PACK // QBLOCK
    return pl.pallas_call(
        lambda *refs: forward_body(blocks, *refs),
        grid_spec=pltpu.PrefetchScalarGridSpec(
            num_scalar_prefetch=1,
            grid=(pairs,),
            in_specs=[tile, group, group] + rest,
            out_specs=[tile, group, group, tile, lse],
        ),
        out_shape=[
            jax.ShapeDtypeStruct((PACK, pairs * 2 * HEAD_DIM), BF16),
            jax.ShapeDtypeStruct((PACK, groups * 2 * HEAD_DIM), BF16),
            jax.ShapeDtypeStruct((PACK, groups * 2 * HEAD_DIM), BF16),
            jax.ShapeDtypeStruct((PACK, pairs * 2 * HEAD_DIM), BF16),
            jax.ShapeDtypeStruct((pairs, 2, PACK), F32),
        ],
        cost_estimate=pl.CostEstimate(
            flops=4 * pairs * 2 * PACK * PACK * HEAD_DIM,
            transcendentals=pairs * PACK * PACK,
            bytes_accessed=8 * PACK * MODEL_WIDTH,
        ),
        name="attend_forward",
    )(slots, query, key, value, *tables)


def attend_backward(slots, saved, grad, log_totals, tables):
    query, key, value = saved
    pairs = query.shape[1] // (2 * HEAD_DIM)
    groups = key.shape[1] // (2 * HEAD_DIM)
    tile, group, lse, rest = attention_specs()
    blocks = PACK // QBLOCK
    return pl.pallas_call(
        lambda *refs: backward_body(blocks, *refs),
        grid_spec=pltpu.PrefetchScalarGridSpec(
            num_scalar_prefetch=1,
            grid=(pairs,),
            in_specs=[tile, group, group, tile, lse] + rest,
            out_specs=[tile, group, group],
            scratch_shapes=[pltpu.VMEM((PACK, 2 * HEAD_DIM), F32)] * 2,
        ),
        out_shape=[
            jax.ShapeDtypeStruct((PACK, pairs * 2 * HEAD_DIM), BF16),
            jax.ShapeDtypeStruct((PACK, groups * 2 * HEAD_DIM), BF16),
            jax.ShapeDtypeStruct((PACK, groups * 2 * HEAD_DIM), BF16),
        ],
        cost_estimate=pl.CostEstimate(
            flops=10 * pairs * 2 * PACK * PACK * HEAD_DIM,
            transcendentals=pairs * PACK * PACK,
            bytes_accessed=8 * PACK * MODEL_WIDTH,
        ),
        name="attend_backward",
    )(slots, query, key, value, grad, log_totals, *tables)


def reverse_bits(value, count):
    out, bit, other = 0, 1, count >> 1
    while other:
        out = out + jnp.where((value & bit) != 0, other, 0)
        bit, other = bit << 1, other >> 1
    return out


def reduce_scatter_rows(total):
    count = lax.axis_size("fsdp")
    me = lax.axis_index("fsdp")
    for bit in reversed(bits_down(count)):
        half = total.shape[0] // 2
        high = ((me & bit) != 0).astype(jnp.int32)
        keep = lax.dynamic_slice_in_dim(total, high * half, half, 0)
        give = lax.dynamic_slice_in_dim(total, (1 - high) * half, half, 0)
        got = swap(give.astype(BF16), "fsdp", bit)
        total = (keep.astype(F32) + got.astype(F32)).astype(BF16)
    return total


def share_out(total):
    count, seqs = lax.axis_size("fsdp"), lax.axis_size("seq")
    me, me_seq = lax.axis_index("fsdp"), lax.axis_index("seq")
    rows, columns = total.shape
    piece = reduce_scatter_rows(total.astype(BF16))
    for bit in bits_down(count):
        piece = jnp.concatenate([piece, swap(piece, "fsdp", bit)], axis=0)
    pieces = gather_relative(piece, "seq")
    targets = jnp.stack(
        [
            (me_seq ^ s) * count + reverse_bits(me ^ o, count)
            for s in relative_order(seqs)
            for o in relative_order(count)
        ]
    )
    return place_blocks(pieces, count, targets).reshape(seqs, rows, columns)


def shards(
    tokens,
    cotangent,
    lengths,
    sequence_adapter,
    attention_norm_gain,
    feedfwd_norm_gain,
    query_matrix,
    key_matrix,
    value_matrix,
    output_matrix,
    gate_matrix,
    up_matrix,
    down_matrix,
    adapter_first_factors,
    adapter_first_down,
    adapter_second_model,
    adapter_second_keyvalue,
    adapter_second_feedfwd,
):
    seqs, fsdps = lax.axis_size("seq"), lax.axis_size("fsdp")
    me = lax.axis_index("seq")
    order = relative_order(seqs)
    peers = [me ^ o for o in order]
    resid_in = tokens[0]
    row_count = resid_in.shape[0]
    width = MODEL_WIDTH // seqs
    kv_width = KV_HEADS * HEAD_DIM // seqs
    my_groups = KV_HEADS // seqs
    feed_units = gate_matrix.shape[1]
    unit_block = feed_units // (seqs * fsdps)
    units = feed_units // seqs
    parts = units // width

    def columns_of(array, peer, count):
        return lax.dynamic_slice_in_dim(array, peer * count, count, array.ndim - 1)

    def rows_of(array, peer):
        return lax.dynamic_slice_in_dim(array, peer * row_count, row_count, 0)

    def relative_rows(array):
        return jnp.concatenate([rows_of(array, peer) for peer in peers], axis=0)

    def blocks_of(array):
        return [array[k * row_count : (k + 1) * row_count] for k in range(seqs)]

    def exchange(pieces):
        return [p if o == 0 else swap(p, "seq", o) for o, p in zip(order, pieces)]

    def place_columns(pieces):
        rows, count = pieces[0].shape
        whole = jnp.zeros((rows, count * seqs), pieces[0].dtype)
        for peer, piece in zip(peers, pieces):
            whole = lax.dynamic_update_slice(whole, piece, (0, peer * count))
        return whole

    rings = Rings()
    qkv_share = jnp.concatenate(
        [
            columns_of(query_matrix, me, width),
            columns_of(key_matrix, me, kv_width),
            columns_of(value_matrix, me, kv_width),
        ],
        axis=1,
    )
    out_share = columns_of(output_matrix, me, width)
    gate_share, up_share = take_units([gate_matrix, up_matrix], me, seqs, fsdps, unit_block)
    down_share = lax.dynamic_slice_in_dim(down_matrix, me * unit_block, unit_block, 0)
    half_block = unit_block // 2
    lists = rings.gather(
        [
            qkv_share,
            out_share,
            gate_share,
            up_share,
            down_share[:half_block],
            down_share[half_block:],
        ],
        [0, 0, 3, 4, 7, 7],
    )
    qkv_mine, out_mine, gate_full, up_full = (
        place_blocks(blocks, 1, rings.owner) for blocks in lists[:4]
    )
    down_full = place_blocks(
        lists[4] + lists[5], 1, jnp.concatenate([rings.owner * 2, rings.owner * 2 + 1])
    )

    segment, position, valid_row, onehot = pack_tables(
        lengths[0], sequence_adapter[0], PACK, ADAPTER_TOTAL
    )
    valid_all = jnp.where(valid_row, 1.0, 0.0).astype(F32)[:, None]
    mask_all = jnp.repeat(onehot, ADAPTER_RANK, axis=1).astype(BF16)
    valid_rel = relative_rows(valid_all)
    mask_rel = relative_rows(mask_all)
    valid_col, mask_own = valid_rel[:row_count], mask_rel[:row_count]
    mask_own_three = jnp.tile(mask_own, (1, 3))
    mask_rel_two = jnp.tile(mask_rel, (1, 2))
    mask_rel_three = jnp.tile(mask_rel, (1, 3))
    cosine, sine = rope_tables(position, HEAD_DIM, 2)
    tables = (cosine, sine, segment[:, None], segment[None, :])
    slot_of = [0] * seqs
    for k, o in enumerate(order):
        slot_of[o] = k
    slot_table = jnp.array(slot_of, jnp.int32)
    sub = row_count // QBLOCK if row_count >= QBLOCK else 1
    if row_count >= QBLOCK:
        slots = jnp.stack(
            [
                slot_table[me ^ (j // sub)] * sub + j % sub
                for j in range(PACK // QBLOCK)
            ]
        )
    else:
        slots = jnp.arange(PACK // QBLOCK, dtype=jnp.int32)

    def to_kernel(array):
        if row_count >= QBLOCK:
            return array
        whole = jnp.zeros_like(array)
        for peer, piece in zip(peers, blocks_of(array)):
            whole = lax.dynamic_update_slice(whole, piece, (peer * row_count, 0))
        return whole

    def from_kernel(array):
        return array if row_count >= QBLOCK else relative_rows(array)

    hidden_in = resid_in.astype(F32)
    normed_own = rms_norm(hidden_in, attention_norm_gain).astype(BF16)
    normed_one = jnp.concatenate(gather_relative(normed_own, "seq"), axis=0)
    first_qkv = jnp.concatenate([adapter_first_factors[k] for k in range(3)], axis=1)
    low_qkv = (mm(normed_one, first_qkv) * mask_rel_three).astype(BF16)
    low_q, low_k, low_v = (low_qkv[:, k * SPAN : (k + 1) * SPAN] for k in range(3))
    second_q = [columns_of(adapter_second_model[0], peer, width) for peer in peers]
    second_k = [columns_of(adapter_second_keyvalue[0], peer, kv_width) for peer in peers]
    second_v = [columns_of(adapter_second_keyvalue[1], peer, kv_width) for peer in peers]

    def twice(rows):
        heads = [rows[:, g * HEAD_DIM : (g + 1) * HEAD_DIM] for g in range(my_groups)]
        return jnp.concatenate([h for h in heads for _ in (0, 1)], axis=1)

    projected = mm(normed_one, qkv_mine)
    query = projected[:, :width] + mm(low_q, second_q[0])
    key = projected[:, width : width + kv_width] + mm(low_k, second_k[0])
    value = projected[:, width + kv_width :] + mm(low_v, second_v[0])
    *saved, attn_heads, log_totals = attend_forward(
        slots, to_kernel(query), to_kernel(twice(key)), to_kernel(twice(value)), tables
    )
    attn_heads = from_kernel(attn_heads)
    attn_own = place_columns(exchange(blocks_of(attn_heads)))
    out_weights = gather_relative(out_mine, "seq")
    low_o = (mm(attn_own, adapter_first_factors[3]) * mask_own).astype(BF16)
    branch = place_columns([mm(attn_own, piece) for piece in out_weights]) + mm(
        low_o, adapter_second_model[1]
    )
    hidden_mid = hidden_in + RESIDUAL_FACTOR * branch
    normed_two_own = rms_norm(hidden_mid, feedfwd_norm_gain).astype(BF16)

    normed_two = jnp.concatenate(gather_relative(normed_two_own, "seq"), axis=0)
    cot_all = jnp.concatenate(gather_relative(cotangent[0], "seq"), axis=0)
    first_ffn = jnp.concatenate([adapter_first_factors[4], adapter_first_factors[5]], axis=1)
    low_ffn = (mm(normed_two, first_ffn) * mask_rel_two).astype(BF16)
    low_g, low_u = low_ffn[:, :SPAN], low_ffn[:, SPAN:]
    (second_ffn,) = take_units(
        [adapter_second_feedfwd.reshape(2 * SPAN, feed_units)], me, seqs, fsdps, unit_block
    )
    second_gate, second_up = second_ffn[:SPAN], second_ffn[SPAN:]
    gate = mm(normed_two, gate_full) + mm(low_g, second_gate)
    up = mm(normed_two, up_full) + mm(low_u, second_up)

    def swiglu(gate_arg, up_arg):
        return jax.nn.sigmoid(gate_arg) * gate_arg * up_arg

    act = swiglu(gate, up).astype(BF16)
    first_down = lax.dynamic_index_in_dim(
        adapter_first_down.reshape(fsdps, seqs, unit_block, SPAN), me, 1, keepdims=False
    ).reshape(units, SPAN)
    grad_out = cotangent[0].astype(F32) * valid_col
    grad_down = (RESIDUAL_FACTOR * (cot_all.astype(F32) * valid_rel)).astype(BF16)
    grad_low_d = mm_nt(grad_down, adapter_second_model[2]).astype(BF16) * mask_rel
    grad_act = mm_nt(grad_down, down_full) + mm_nt(grad_low_d, first_down)
    _, swiglu_back = jax.vjp(swiglu, gate, up)
    grad_gate, grad_up = swiglu_back(grad_act)
    grad_gate, grad_up = grad_gate.astype(BF16), grad_up.astype(BF16)
    grad_low_ffn = (
        jnp.concatenate([mm_nt(grad_gate, second_gate), mm_nt(grad_up, second_up)], axis=1).astype(
            BF16
        )
        * mask_rel_two
    )
    grad_normed_two = (
        mm_nt(grad_gate, gate_full) + mm_nt(grad_up, up_full) + mm_nt(grad_low_ffn, first_ffn)
    )
    act, grad_gate, grad_up = after((act, grad_gate, grad_up), grad_normed_two)
    grad_normed_two = reduce_relative(blocks_of(grad_normed_two), "seq")
    low_d = (mm(act, first_down) * mask_rel).astype(BF16)
    down_part = mm(act, down_full) + mm(low_d, adapter_second_model[2])
    down_sum = reduce_relative(blocks_of(down_part), "seq")
    layer_out = (valid_col * (hidden_mid + RESIDUAL_FACTOR * down_sum)).astype(BF16)

    grad_b_down = mm_tn(low_d, grad_down)
    grad_a_down = mm_tn(grad_low_d, act)
    grad_b_gate = mm_tn(low_g, grad_gate)
    grad_b_up = mm_tn(low_u, grad_up)
    grad_a_ffn = mm_tn(grad_low_ffn, normed_two)
    _, norm_two_back = jax.vjp(lambda hidden: rms_norm(hidden, feedfwd_norm_gain), hidden_mid)
    grad_mid = grad_out + norm_two_back(grad_normed_two)[0]

    grad_branch = (RESIDUAL_FACTOR * grad_mid).astype(BF16)
    grad_low_o = mm_nt(grad_branch, adapter_second_model[1]).astype(BF16) * mask_own
    grad_b_out = mm_tn(low_o, grad_branch)
    grad_a_out = mm_tn(grad_low_o, attn_own)
    grad_attn = mm_nt(grad_low_o, adapter_first_factors[3])
    for peer, piece in zip(peers, out_weights):
        grad_attn = grad_attn + mm_nt(columns_of(grad_branch, peer, width), piece)
    grad_attn = grad_attn.astype(BF16)
    grad_heads = jnp.concatenate(
        exchange([columns_of(grad_attn, peer, width) for peer in peers]), axis=0
    )
    grad_query, grad_key, grad_value = (
        from_kernel(g)
        for g in attend_backward(slots, saved, to_kernel(grad_heads), log_totals, tables)
    )

    def once(rows):
        return jnp.concatenate(
            [rows[:, 2 * g * HEAD_DIM : (2 * g + 1) * HEAD_DIM] for g in range(my_groups)], axis=1
        )

    grad_key, grad_value = once(grad_key), once(grad_value)
    grad_qkv = jnp.concatenate([grad_query, grad_key, grad_value], axis=1)
    grad_pieces = exchange(blocks_of(grad_qkv))
    qkv_weights = gather_relative(qkv_mine, "seq")
    grad_b_q = mm_tn(low_q, grad_query)
    grad_b_kv = [mm_tn(low_k, grad_key), mm_tn(low_v, grad_value)]
    low_grads = [jnp.zeros((row_count, SPAN), F32)] * 3
    for k in range(seqs):
        piece = grad_pieces[k]
        low_grads = [
            low_grads[0] + mm_nt(piece[:, :width], second_q[k]),
            low_grads[1] + mm_nt(piece[:, width : width + kv_width], second_k[k]),
            low_grads[2] + mm_nt(piece[:, width + kv_width :], second_v[k]),
        ]
    grad_low_qkv = jnp.concatenate(low_grads, axis=1).astype(BF16) * mask_own_three
    grad_low_all = jnp.concatenate(gather_relative(grad_low_qkv, "seq"), axis=0)
    grad_a_qkv = mm_tn(grad_low_all, columns_of(normed_one, me, width))
    grad_normed_one = mm_nt(grad_low_qkv, first_qkv)
    for k in range(seqs):
        grad_normed_one = grad_normed_one + mm_nt(grad_pieces[k], qkv_weights[k])
    _, norm_one_back = jax.vjp(lambda hidden: rms_norm(hidden, attention_norm_gain), hidden_in)
    grad_input = (grad_mid + norm_one_back(grad_normed_one)[0]).astype(BF16)

    factor = ADAPTER_TOTAL / math.sqrt(PACK * fsdps)

    def split_units(rows):
        return [rows[:, k * width : (k + 1) * width].astype(BF16) for k in range(parts)]

    def seq_share(rows):
        return reduce_relative(
            [columns_of(rows, peer, width) for peer in peers], "seq"
        ).astype(BF16)

    def units_out(whole, first):
        part = whole[:, first : first + parts * SPAN]
        part = part.reshape(seqs, parts, SPAN, fsdps // parts, unit_block)
        return part.transpose(2, 1, 3, 0, 4).reshape(SPAN, feed_units)

    early = share_out(
        jnp.concatenate(
            [seq_share(jnp.concatenate([grad_a_ffn, grad_b_down], axis=0))]
            + split_units(grad_a_down)
            + split_units(grad_b_gate)
            + split_units(grad_b_up),
            axis=0,
        )
    )
    blank = jnp.zeros((SPAN, width - 2 * kv_width), BF16)
    middle = share_out(
        jnp.concatenate(
            [
                seq_share(jnp.concatenate([grad_a_out, grad_b_out], axis=0)),
                grad_b_q.astype(BF16),
                jnp.concatenate([g.astype(BF16) for g in grad_b_kv] + [blank], axis=1),
            ],
            axis=0,
        )
    )
    late = share_out(grad_a_qkv)

    def scaled(array):
        return array.astype(F32) * factor

    base = 3 * SPAN
    b_kv = middle[:, 3 * SPAN :, : 2 * kv_width].reshape(seqs, SPAN, 2, kv_width)
    if unit_block % 128 == 0:
        a_down, b_ffn = finish_units(early, base, parts, fsdps, unit_block, factor)
    else:
        a_down = scaled(units_out(early, base).T)
        b_ffn = scaled(
            jnp.stack(
                [units_out(early, base + parts * SPAN), units_out(early, base + 2 * parts * SPAN)]
            )
        )
    a_all, b_model = finish_model(early, middle, factor)
    return (
        layer_out[None],
        grad_input[None],
        finish_late(late, a_all, factor),
        a_down,
        b_model,
        scaled(b_kv.transpose(2, 1, 0, 3).reshape(2, SPAN, KV_HEADS * HEAD_DIM)),
        b_ffn,
    )


def solution(mesh):
    rows = P("fsdp", None)
    placed = (
        (P("fsdp", "seq", None),) * 2 + (rows,) * 2 + (P(),) * 2 + (rows,) * 7 + (P(),) * 5
    )
    return jax.shard_map(
        shards,
        mesh=mesh,
        in_specs=placed,
        out_specs=(P("fsdp", "seq", None), P("fsdp", "seq", None), P(), P(), P(), P(), P()),
        check_vma=False,
    )
```

```python
import math

import jax
import jax.numpy as jnp
from jax import lax
from jax.experimental import pallas as pl
from jax.experimental.pallas import tpu as pltpu
from jax.sharding import PartitionSpec as P

MODEL_WIDTH = 2048
HEADS = 32
KV_HEADS = 8
HEAD_DIM = 64
ADAPTER_RANK = 16
ADAPTER_TOTAL = 8
PACK = 1024
QBLOCK = 256
SPAN = ADAPTER_TOTAL * ADAPTER_RANK
GROUP = HEADS // KV_HEADS

SCORE_SCALE = 0.015625
RESIDUAL_FACTOR = 0.22
NORM_EPSILON = 1e-05
ROPE_BASE = 10000000.0
MASK_FILL = 1e30

BF16 = jnp.bfloat16
F32 = jnp.float32


def mm(left, right):
    return jnp.dot(left, right, preferred_element_type=F32)


def mm_nt(left, right):
    return lax.dot_general(left, right, (((1,), (1,)), ((), ())), preferred_element_type=F32)


def mm_tn(left, right):
    return lax.dot_general(left, right, (((0,), (0,)), ((), ())), preferred_element_type=F32)


def rms_norm(hidden, gain_vec):
    mean_square = jnp.mean(hidden * hidden, axis=-1, keepdims=True)
    return hidden * lax.rsqrt(mean_square + NORM_EPSILON) * gain_vec


def pack_tables(seq_lengths, adapter_id, token_count, adapter_count):
    slots = seq_lengths.shape[0]
    places = jnp.arange(token_count, dtype=jnp.int32)
    seq_ends = jnp.cumsum(seq_lengths)
    seq_starts = seq_ends - seq_lengths
    used_len = seq_ends[slots - 1]
    segment = jnp.sum((places[:, None] >= seq_ends[None, :]).astype(jnp.int32), axis=1)
    member = segment[:, None] == jnp.arange(slots, dtype=jnp.int32)[None, :]
    start_tok = jnp.sum(jnp.where(member, seq_starts[None, :], 0), axis=1) + jnp.where(
        segment == slots, used_len, 0
    )
    position = places - start_tok
    valid_row = segment < slots
    chosen = adapter_id[:, None] == jnp.arange(adapter_count, dtype=jnp.int32)[None, :]
    onehot = jnp.sum(jnp.where(member[:, :, None] & chosen[None, :, :], 1.0, 0.0), axis=1).astype(F32)
    return (segment, position, valid_row, onehot)


def rope_tables(position, head_size, copies):
    frequency = ROPE_BASE ** (-(jnp.arange(head_size // 2, dtype=F32) * 2.0) / head_size)
    angles = position.astype(F32)[:, None] * frequency[None, :]
    cosine, sine = jnp.cos(angles), jnp.sin(angles)
    return (jnp.tile(cosine, (1, 2 * copies)), jnp.tile(sine, (1, 2 * copies)))


def bits_down(count):
    bits, bit = [], count >> 1
    while bit:
        bits.append(bit)
        bit >>= 1
    return bits


def relative_order(count):
    order = [0]
    for bit in bits_down(count):
        order = order + [o ^ bit for o in order]
    return order


def swap(block, axis, offset):
    count = lax.axis_size(axis)
    return lax.ppermute(block, axis, [(i, i ^ offset) for i in range(count)])


def gather_relative(block, axis, last=()):
    pieces = [block]
    for bit in bits_down(lax.axis_size(axis)):
        if bit == 1:
            pieces[-1] = after(pieces[-1], *last)
        pieces = pieces + [swap(piece, axis, bit) for piece in pieces]
    return pieces


def reduce_relative(pieces, axis, last=()):
    for bit in reversed(bits_down(lax.axis_size(axis))):
        half = len(pieces) // 2
        given = [piece.astype(BF16) for piece in pieces[half:]]
        if half == 1:
            given = [after(given[0], *last)]
        got = [swap(piece, axis, bit) for piece in given]
        pieces = [mine.astype(F32) + other.astype(F32) for mine, other in zip(pieces[:half], got)]
    return pieces[0]


def reduce_halves(keep, give, axis):
    bits = list(reversed(bits_down(lax.axis_size(axis))))
    for bit in bits:
        got = swap(give, axis, bit)
        total = keep.astype(F32) + got.astype(F32)
        half = total.shape[0] // 2
        keep, give = total[:half], total[half:].astype(BF16)
    return total


def cycle_of(count):
    return list(range(0, count, 2)) + list(range(count - 1, 0, -2))


class Rings:
    WINDOW = 3

    def __init__(self):
        self.count = lax.axis_size("fsdp")
        cycle = cycle_of(self.count)
        place = {device: k for k, device in enumerate(cycle)}
        table = [
            [cycle[(place[device] - k) % self.count] for k in range(self.count)]
            for device in range(self.count)
        ]
        self.owner = lax.dynamic_index_in_dim(
            jnp.array(table, jnp.int32), lax.axis_index("fsdp"), 0, keepdims=False
        )
        ahead = [(cycle[k], cycle[(k + 1) % self.count]) for k in range(self.count)]
        self.perms = (ahead, [(b, a) for a, b in ahead])
        self.sent = ([], [])

    def send(self, way, block):
        sent = self.sent[way]
        if len(sent) >= self.WINDOW:
            block, _ = lax.optimization_barrier((block, sent[-self.WINDOW]))
        got = lax.ppermute(block, "fsdp", self.perms[way])
        sent.append(got)
        return got

    def gather(self, blocks, starts):
        half = self.count // 2
        found = [{0: block} for block in blocks]
        latest = [[block, block] for block in blocks]
        for time in range(1, half + max(starts) + 1):
            for which in range(len(blocks)):
                step = time - starts[which]
                if not 1 <= step <= half:
                    continue
                for way in (0, 1):
                    if step == half and way != which % 2:
                        continue
                    got = self.send(way, latest[which][way])
                    latest[which][way] = got
                    found[which][step if way == 0 else self.count - step] = got
        return [[f[k] for k in range(self.count)] for f in found]


def place_blocks(pieces, counts, targets):
    rows = pieces[0].shape[0] // counts
    columns = pieces[0].shape[1]
    total = len(pieces) * counts

    def body(target_ref, *refs):
        out_ref, held, came, left = refs[-4:]
        arrivals, departures = [], []
        for i in range(len(pieces)):
            for j in range(counts):
                k = i * counts + j
                first = pl.multiple_of(target_ref[k] * rows, rows)
                arrivals.append(
                    pltpu.make_async_copy(
                        refs[i].at[pl.ds(j * rows, rows), :], held.at[k], came.at[k]
                    )
                )
                departures.append(
                    pltpu.make_async_copy(
                        held.at[k], out_ref.at[pl.ds(first, rows), :], left.at[k]
                    )
                )
        for copy in arrivals:
            copy.start()
        for arrival, departure in zip(arrivals, departures):
            arrival.wait()
            departure.start()
        for copy in departures:
            copy.wait()

    return pl.pallas_call(
        body,
        out_shape=jax.ShapeDtypeStruct((rows * total, columns), pieces[0].dtype),
        grid_spec=pltpu.PrefetchScalarGridSpec(
            num_scalar_prefetch=1,
            grid=(),
            in_specs=[pl.BlockSpec(memory_space=pl.ANY)] * len(pieces),
            out_specs=pl.BlockSpec(memory_space=pl.ANY),
            scratch_shapes=[
                pltpu.VMEM((total, rows, columns), pieces[0].dtype),
                pltpu.SemaphoreType.DMA((total,)),
                pltpu.SemaphoreType.DMA((total,)),
            ],
        ),
        cost_estimate=pl.CostEstimate(
            flops=0, transcendentals=0, bytes_accessed=4 * rows * total * columns
        ),
        name="place_blocks",
    )(targets.astype(jnp.int32), *pieces)


def after(value, *others):
    return lax.optimization_barrier((value, others))[0]


def take_units(matrices, peer, seqs, runs, unit_block):
    if unit_block % 128:
        return [
            lax.dynamic_index_in_dim(
                m.reshape(m.shape[0], runs, seqs, unit_block), peer, 2, keepdims=False
            ).reshape(m.shape[0], runs * unit_block)
            for m in matrices
        ]

    def body(peer_ref, *refs):
        for source, target in zip(refs[: len(matrices)], refs[len(matrices) :]):
            target[...] = source[...]

    return pl.pallas_call(
        body,
        grid_spec=pltpu.PrefetchScalarGridSpec(
            num_scalar_prefetch=1,
            grid=(runs,),
            in_specs=[
                pl.BlockSpec((m.shape[0], unit_block), lambda f, at: (0, f * seqs + at[0]))
                for m in matrices
            ],
            out_specs=[
                pl.BlockSpec((m.shape[0], unit_block), lambda f, at: (0, f)) for m in matrices
            ],
        ),
        out_shape=[
            jax.ShapeDtypeStruct((m.shape[0], runs * unit_block), m.dtype) for m in matrices
        ],
        name="take_units",
    )(peer.astype(jnp.int32)[None], *matrices)


def finish_units(whole, first, parts, runs, unit_block, factor):
    seqs, _, columns = whole.shape
    feed_units = seqs * runs * unit_block
    per = runs // parts

    def body(down_ref, gate_ref, up_ref, a_ref, b_ref):
        for s in range(seqs):
            here = slice(s * unit_block, (s + 1) * unit_block)
            a_ref[here, :] = down_ref[s].astype(F32).T * factor
            b_ref[0, :, here] = gate_ref[s].astype(F32) * factor
            b_ref[1, :, here] = up_ref[s].astype(F32) * factor

    def part(which):
        base = first // SPAN + which * parts
        return pl.BlockSpec((seqs, SPAN, unit_block), lambda k, g: (0, base + k, g))

    return pl.pallas_call(
        body,
        grid=(parts, per),
        in_specs=[part(0), part(1), part(2)],
        out_specs=[
            pl.BlockSpec((seqs * unit_block, SPAN), lambda k, g: (k * per + g, 0)),
            pl.BlockSpec((2, SPAN, seqs * unit_block), lambda k, g: (0, 0, k * per + g)),
        ],
        out_shape=[
            jax.ShapeDtypeStruct((feed_units, SPAN), F32),
            jax.ShapeDtypeStruct((2, SPAN, feed_units), F32),
        ],
        name="finish_units",
    )(whole, whole, whole)


def finish_model(whole, factor):
    seqs, _, columns = whole.shape

    def body(shared_ref, heads_ref, a_ref, b_ref):
        def rows(k):
            return shared_ref[0, k * SPAN : (k + 1) * SPAN].astype(F32) * factor

        a_ref[0] = rows(3).T
        a_ref[1] = rows(0).T
        a_ref[2] = rows(1).T
        b_ref[0] = heads_ref[0].astype(F32) * factor
        b_ref[1] = rows(4)
        b_ref[2] = rows(2)

    return pl.pallas_call(
        body,
        grid=(seqs,),
        in_specs=[
            pl.BlockSpec((1, 5 * SPAN, columns), lambda s: (s, 0, 0)),
            pl.BlockSpec((1, SPAN, columns), lambda s: (s, 5, 0)),
        ],
        out_specs=[
            pl.BlockSpec((3, columns, SPAN), lambda s: (1, s, 0)),
            pl.BlockSpec((3, SPAN, columns), lambda s: (0, 0, s)),
        ],
        out_shape=[
            jax.ShapeDtypeStruct((6, MODEL_WIDTH, SPAN), F32),
            jax.ShapeDtypeStruct((3, SPAN, MODEL_WIDTH), F32),
        ],
        name="finish_model",
    )(whole, whole)


def finish_late(late, a_all, factor):
    seqs, _, columns = late.shape

    def body(late_ref, held_ref, a_ref):
        for j in range(3):
            a_ref[j] = late_ref[0, j * SPAN : (j + 1) * SPAN].astype(F32).T * factor

    return pl.pallas_call(
        body,
        grid=(seqs,),
        in_specs=[
            pl.BlockSpec((1, 3 * SPAN, columns), lambda s: (s, 0, 0)),
            pl.BlockSpec(memory_space=pl.ANY),
        ],
        out_specs=pl.BlockSpec((3, columns, SPAN), lambda s: (0, s, 0)),
        out_shape=jax.ShapeDtypeStruct(a_all.shape, F32),
        input_output_aliases={1: 0},
        name="finish_late",
    )(late, a_all)


def half_lanes(shape):
    lane = lax.broadcasted_iota(jnp.int32, shape, 1)
    return lane % HEAD_DIM < HEAD_DIM // 2


def turn_tile(x, cosine, sine):
    quarter = HEAD_DIM // 2
    ahead = pltpu.roll(x, 2 * HEAD_DIM - quarter, 1)
    behind = pltpu.roll(x, quarter, 1)
    return x * cosine + jnp.where(half_lanes(x.shape), -ahead, behind) * sine


def dot_tn(left, right):
    return lax.dot_general(left, right, (((0,), (0,)), ((), ())), preferred_element_type=F32)


def dot_nt(left, right):
    return lax.dot_general(left, right, (((1,), (1,)), ((), ())), preferred_element_type=F32)


def allowed_pairs(seg_col, seg_row, block):
    keys = (block + 1) * QBLOCK
    shape = (keys, QBLOCK)
    key_at = lax.broadcasted_iota(jnp.int32, shape, 0)
    query_at = lax.broadcasted_iota(jnp.int32, shape, 1) + block * QBLOCK
    same = seg_col[:keys, :] == seg_row[:, block * QBLOCK : keys]
    return same & (key_at <= query_at)


def forward_body(
    blocks, slot_ref, q_ref, k_ref, v_ref, cos_ref, sin_ref, col_ref, row_ref,
    qn_ref, kn_ref, vn_ref, out_ref, lse_ref,
):
    for j in range(blocks):
        here = slice(j * QBLOCK, (j + 1) * QBLOCK)
        there = pl.ds(pl.multiple_of(slot_ref[j] * QBLOCK, QBLOCK), QBLOCK)
        cosine, sine = cos_ref[here, :], sin_ref[here, :]
        qn_ref[here, :] = turn_tile(q_ref[there, :], cosine, sine).astype(BF16)
        kn_ref[here, :] = turn_tile(k_ref[there, :], cosine, sine).astype(BF16)
        vn_ref[here, :] = v_ref[there, :].astype(BF16)
    lane = lax.broadcasted_iota(jnp.int32, (QBLOCK, 2 * HEAD_DIM), 1)
    row = lax.broadcasted_iota(jnp.int32, (2 * HEAD_DIM, QBLOCK), 0)
    for i in range(blocks):
        here = slice(i * QBLOCK, (i + 1) * QBLOCK)
        keys = (i + 1) * QBLOCK
        allowed = allowed_pairs(col_ref[...], row_ref[...], i)
        query = (qn_ref[here, :].astype(F32) * SCORE_SCALE).astype(BF16)
        outs = []
        for e in range(2):
            mine = jnp.where(lane // HEAD_DIM == e, query, jnp.zeros_like(query))
            scores = jnp.where(allowed, dot_nt(kn_ref[:keys, :], mine), -MASK_FILL)
            most = jnp.max(scores, axis=0, keepdims=True)
            exponent = jnp.exp(scores - most)
            total = jnp.sum(exponent, axis=0, keepdims=True)
            probs = (exponent * (1.0 / total)).astype(BF16)
            lse_ref[0, e : e + 1, here] = most + jnp.log(total)
            outs.append(dot_tn(vn_ref[:keys, :], probs))
        out = jnp.where(row < HEAD_DIM, outs[0], outs[1]).T
        there = pl.ds(pl.multiple_of(slot_ref[i] * QBLOCK, QBLOCK), QBLOCK)
        out_ref[there, :] = out.astype(BF16)


def backward_body(
    blocks, groups, slot_ref, qn_ref, kn_ref, vn_ref, do_ref, lse_ref, cos_ref, sin_ref, col_ref,
    row_ref, out_ref, dk_sum, dv_sum,
):
    pairs_per_group = GROUP // 2
    pair = pl.program_id(0)
    step = lax.rem(pair, pairs_per_group)
    two = 2 * HEAD_DIM

    @pl.when(step == 0)
    def _():
        dk_sum[...] = jnp.zeros_like(dk_sum)
        dv_sum[...] = jnp.zeros_like(dv_sum)

    lane = lax.broadcasted_iota(jnp.int32, (QBLOCK, two), 1)
    row = lax.broadcasted_iota(jnp.int32, (two, QBLOCK), 0)

    def place(j):
        return pl.ds(pl.multiple_of(slot_ref[j] * QBLOCK, QBLOCK), QBLOCK)

    for i in range(blocks):
        here = slice(i * QBLOCK, (i + 1) * QBLOCK)
        keys = (i + 1) * QBLOCK
        allowed = allowed_pairs(col_ref[...], row_ref[...], i)
        query = (qn_ref[here, :].astype(F32) * SCORE_SCALE).astype(BF16)
        grad = do_ref[place(i), :]
        outs = []
        for e in range(2):
            mine = jnp.where(lane // HEAD_DIM == e, query, jnp.zeros_like(query))
            grad_mine = jnp.where(lane // HEAD_DIM == e, grad, jnp.zeros_like(grad))
            scores = jnp.where(allowed, dot_nt(kn_ref[:keys, :], mine), -MASK_FILL)
            probs = jnp.exp(scores - lse_ref[0, e : e + 1, here])
            grad_probs = dot_nt(vn_ref[:keys, :], grad_mine)
            delta = jnp.sum(probs * grad_probs, axis=0, keepdims=True)
            grad_scores = (probs * (grad_probs - delta)).astype(BF16)
            dv_sum[:keys, :] += jnp.dot(probs.astype(BF16), grad_mine, preferred_element_type=F32)
            dk_sum[:keys, :] += jnp.dot(grad_scores, mine, preferred_element_type=F32)
            outs.append(dot_tn(kn_ref[:keys, :], grad_scores))
        out = jnp.where(row < HEAD_DIM, outs[0], outs[1]).T * SCORE_SCALE
        out = out.astype(BF16).astype(F32)
        out_ref[place(i), pl.ds(pl.multiple_of(pair * two, two), two)] = turn_tile(
            out, cos_ref[here, :], -sin_ref[here, :]
        ).astype(BF16)

    width = groups * GROUP * HEAD_DIM
    for g in range(groups):

        @pl.when(pair == (g + 1) * pairs_per_group - 1)
        def _(g=g):
            for j in range(blocks):
                here = slice(j * QBLOCK, (j + 1) * QBLOCK)
                dk = dk_sum[here, :]
                dk = (dk + pltpu.roll(dk, HEAD_DIM, 1)).astype(BF16).astype(F32)
                dk = turn_tile(dk, cos_ref[here, :], -sin_ref[here, :]).astype(BF16)
                dv = dv_sum[here, :]
                dv = (dv + pltpu.roll(dv, HEAD_DIM, 1)).astype(BF16)
                for base, values in ((width, dk), (width + groups * HEAD_DIM, dv)):
                    first = base + g * HEAD_DIM
                    tile = slice(first // two * two, first // two * two + two)
                    half = first // HEAD_DIM % 2
                    old = out_ref[place(j), tile]
                    out_ref[place(j), tile] = jnp.where(lane // HEAD_DIM == half, values, old)


def attention_specs():
    tile = pl.BlockSpec((PACK, 2 * HEAD_DIM), lambda p, slot: (0, p))
    group = pl.BlockSpec((PACK, 2 * HEAD_DIM), lambda p, slot: (0, p // (GROUP // 2)))
    lse = pl.BlockSpec((1, 2, PACK), lambda p, slot: (p, 0, 0))
    table = pl.BlockSpec((PACK, 2 * HEAD_DIM), lambda p, slot: (0, 0))
    col = pl.BlockSpec((PACK, 1), lambda p, slot: (0, 0))
    row = pl.BlockSpec((1, PACK), lambda p, slot: (0, 0))
    return tile, group, lse, [table, table, col, row]


def attend_forward(slots, query, key, value, tables):
    pairs = query.shape[1] // (2 * HEAD_DIM)
    groups = key.shape[1] // (2 * HEAD_DIM)
    tile, group, lse, rest = attention_specs()
    blocks = PACK // QBLOCK
    return pl.pallas_call(
        lambda *refs: forward_body(blocks, *refs),
        grid_spec=pltpu.PrefetchScalarGridSpec(
            num_scalar_prefetch=1,
            grid=(pairs,),
            in_specs=[tile, group, group] + rest,
            out_specs=[tile, group, group, tile, lse],
        ),
        out_shape=[
            jax.ShapeDtypeStruct((PACK, pairs * 2 * HEAD_DIM), BF16),
            jax.ShapeDtypeStruct((PACK, groups * 2 * HEAD_DIM), BF16),
            jax.ShapeDtypeStruct((PACK, groups * 2 * HEAD_DIM), BF16),
            jax.ShapeDtypeStruct((PACK, pairs * 2 * HEAD_DIM), BF16),
            jax.ShapeDtypeStruct((pairs, 2, PACK), F32),
        ],
        cost_estimate=pl.CostEstimate(
            flops=4 * pairs * 2 * PACK * PACK * HEAD_DIM,
            transcendentals=pairs * PACK * PACK,
            bytes_accessed=8 * PACK * MODEL_WIDTH,
        ),
        name="attend_forward",
    )(slots, query, key, value, *tables)


def attend_backward(slots, saved, grad, log_totals, tables):
    query, key, value = saved
    pairs = query.shape[1] // (2 * HEAD_DIM)
    groups = key.shape[1] // (2 * HEAD_DIM)
    tile, group, lse, rest = attention_specs()
    blocks = PACK // QBLOCK
    columns = pairs * 2 * HEAD_DIM + groups * 2 * HEAD_DIM
    return pl.pallas_call(
        lambda *refs: backward_body(blocks, groups, *refs),
        grid_spec=pltpu.PrefetchScalarGridSpec(
            num_scalar_prefetch=1,
            grid=(pairs,),
            in_specs=[tile, group, group, tile, lse] + rest,
            out_specs=pl.BlockSpec((PACK, columns), lambda p, slot: (0, 0)),
            scratch_shapes=[pltpu.VMEM((PACK, 2 * HEAD_DIM), F32)] * 2,
        ),
        out_shape=jax.ShapeDtypeStruct((PACK, columns), BF16),
        cost_estimate=pl.CostEstimate(flops=0, transcendentals=0, bytes_accessed=0),
        name="attend_backward",
    )(slots, query, key, value, grad, log_totals, *tables)


def tile_of(count):
    return 256 if count % 256 == 0 else 128


def gate_grads(grad_down, down, grad_low, first_down, gate, up):
    tokens, units = gate.shape
    tile = tile_of(units)

    def body(gd_ref, down_ref, gl_ref, fd_ref, gate_ref, up_ref, gg_ref, gu_ref):
        grad_act = dot_nt(gd_ref[...], down_ref[...]) + dot_nt(gl_ref[...], fd_ref[...])
        gate_here = gate_ref[...]
        share = jax.nn.sigmoid(gate_here)
        gu_ref[...] = (grad_act * share * gate_here).astype(BF16)
        gg_ref[...] = (
            grad_act * up_ref[...] * share * (1.0 + gate_here * (1.0 - share))
        ).astype(BF16)

    def whole(array):
        return pl.BlockSpec(array.shape, lambda t: (0, 0))

    def rows(array):
        return pl.BlockSpec((tile, array.shape[1]), lambda t: (t, 0))

    cols = pl.BlockSpec((tokens, tile), lambda t: (0, t))
    return pl.pallas_call(
        body,
        grid=(units // tile,),
        in_specs=[whole(grad_down), rows(down), whole(grad_low), rows(first_down), cols, cols],
        out_specs=[cols, cols],
        out_shape=[jax.ShapeDtypeStruct((tokens, units), BF16)] * 2,
        cost_estimate=pl.CostEstimate(
            flops=2 * tokens * units * MODEL_WIDTH,
            transcendentals=tokens * units,
            bytes_accessed=12 * tokens * units + 2 * units * MODEL_WIDTH,
        ),
        name="gate_grads",
    )(grad_down, down, grad_low, first_down, gate, up)


def sum_products(lefts, rights):
    tokens, outs = lefts[0].shape[0], rights[0].shape[0]
    tile = tile_of(outs)
    count = len(lefts)

    def body(*refs):
        total = dot_nt(refs[0][...], refs[count][...])
        for k in range(1, count):
            total = total + dot_nt(refs[k][...], refs[count + k][...])
        refs[-2][...] = total[: tokens // 2].astype(BF16)
        refs[-1][...] = total[tokens // 2 :].astype(BF16)

    half = pl.BlockSpec((tokens // 2, tile), lambda t: (0, t))
    return pl.pallas_call(
        body,
        grid=(outs // tile,),
        in_specs=[pl.BlockSpec(a.shape, lambda t: (0, 0)) for a in lefts]
        + [pl.BlockSpec((tile, b.shape[1]), lambda t: (t, 0)) for b in rights],
        out_specs=[half, half],
        out_shape=[jax.ShapeDtypeStruct((tokens // 2, outs), BF16)] * 2,
        cost_estimate=pl.CostEstimate(
            flops=sum(2 * tokens * outs * a.shape[1] for a in lefts),
            transcendentals=0,
            bytes_accessed=2 * sum(a.size for a in [*lefts, *rights]) + 2 * tokens * outs,
        ),
        name="sum_products",
    )(*lefts, *rights)


def reverse_bits(value, count):
    out, bit, other = 0, 1, count >> 1
    while other:
        out = out + jnp.where((value & bit) != 0, other, 0)
        bit, other = bit << 1, other >> 1
    return out


def scatter_step(total, bit):
    half = total.shape[0] // 2
    high = ((lax.axis_index("fsdp") & bit) != 0).astype(jnp.int32)
    keep = lax.dynamic_slice_in_dim(total, high * half, half, 0)
    give = lax.dynamic_slice_in_dim(total, (1 - high) * half, half, 0)
    got = swap(give, "fsdp", bit)
    return (keep.astype(F32) + got.astype(F32)).astype(BF16)


def reduce_scatter_rows(total):
    for bit in reversed(bits_down(lax.axis_size("fsdp"))):
        total = scatter_step(total, bit)
    return total


def widen(piece, bit):
    return jnp.concatenate([piece, swap(piece, "fsdp", bit)], axis=0)


def share_out(piece):
    for bit in bits_down(lax.axis_size("fsdp")):
        piece = widen(piece, bit)
    return piece


def settle(pieces):
    count, seqs = lax.axis_size("fsdp"), lax.axis_size("seq")
    me, me_seq = lax.axis_index("fsdp"), lax.axis_index("seq")
    rows, columns = pieces[0].shape
    targets = jnp.stack(
        [
            (me_seq ^ s) * count + reverse_bits(me ^ o, count)
            for s in relative_order(seqs)
            for o in relative_order(count)
        ]
    )
    return place_blocks(pieces, count, targets).reshape(seqs, rows, columns)


def shards(
    tokens,
    cotangent,
    lengths,
    sequence_adapter,
    attention_norm_gain,
    feedfwd_norm_gain,
    query_matrix,
    key_matrix,
    value_matrix,
    output_matrix,
    gate_matrix,
    up_matrix,
    down_matrix,
    adapter_first_factors,
    adapter_first_down,
    adapter_second_model,
    adapter_second_keyvalue,
    adapter_second_feedfwd,
):
    seqs, fsdps = lax.axis_size("seq"), lax.axis_size("fsdp")
    me = lax.axis_index("seq")
    order = relative_order(seqs)
    peers = [me ^ o for o in order]
    resid_in = tokens[0]
    row_count = resid_in.shape[0]
    width = MODEL_WIDTH // seqs
    kv_width = KV_HEADS * HEAD_DIM // seqs
    my_groups = KV_HEADS // seqs
    feed_units = gate_matrix.shape[1]
    unit_block = feed_units // (seqs * fsdps)
    units = feed_units // seqs
    parts = units // width

    def columns_of(array, peer, count):
        return lax.dynamic_slice_in_dim(array, peer * count, count, array.ndim - 1)

    def rows_of(array, peer):
        return lax.dynamic_slice_in_dim(array, peer * row_count, row_count, 0)

    def relative_rows(array):
        return jnp.concatenate([rows_of(array, peer) for peer in peers], axis=0)

    def blocks_of(array):
        return [array[k * row_count : (k + 1) * row_count] for k in range(seqs)]

    def exchange(pieces):
        return [p if o == 0 else swap(p, "seq", o) for o, p in zip(order, pieces)]

    def place_columns(pieces):
        rows, count = pieces[0].shape
        whole = jnp.zeros((rows, count * seqs), pieces[0].dtype)
        for peer, piece in zip(peers, pieces):
            whole = lax.dynamic_update_slice(whole, piece, (0, peer * count))
        return whole

    rings = Rings()
    qkv_share = jnp.concatenate(
        [
            columns_of(query_matrix, me, width),
            columns_of(key_matrix, me, kv_width),
            columns_of(value_matrix, me, kv_width),
        ],
        axis=1,
    )
    gate_share, up_share = take_units([gate_matrix, up_matrix], me, seqs, fsdps, unit_block)
    out_share = columns_of(output_matrix, me, width)
    down_share = lax.dynamic_slice_in_dim(down_matrix, me * unit_block, unit_block, 0)
    half_block = unit_block // 2
    lists = rings.gather(
        [
            qkv_share,
            out_share,
            gate_share,
            up_share,
            down_share[:half_block],
            down_share[half_block:],
        ],
        [0, 0, 2, 3, 5, 6],
    )
    qkv_mine, out_mine, gate_full, up_full = (
        place_blocks(blocks, 1, rings.owner) for blocks in lists[:4]
    )

    segment, position, valid_row, onehot = pack_tables(
        lengths[0], sequence_adapter[0], PACK, ADAPTER_TOTAL
    )
    valid_all = jnp.where(valid_row, 1.0, 0.0).astype(F32)[:, None]
    mask_all = jnp.repeat(onehot, ADAPTER_RANK, axis=1).astype(BF16)
    valid_rel = relative_rows(valid_all)
    mask_rel = relative_rows(mask_all)
    valid_col, mask_own = valid_rel[:row_count], mask_rel[:row_count]
    mask_own_three = jnp.tile(mask_own, (1, 3))
    mask_rel_two = jnp.tile(mask_rel, (1, 2))
    mask_rel_three = jnp.tile(mask_rel, (1, 3))
    cosine, sine = rope_tables(position, HEAD_DIM, 2)
    tables = (cosine, sine, segment[:, None], segment[None, :])
    slot_of = [0] * seqs
    for k, o in enumerate(order):
        slot_of[o] = k
    slot_table = jnp.array(slot_of, jnp.int32)
    sub = row_count // QBLOCK if row_count >= QBLOCK else 1
    if row_count >= QBLOCK:
        slots = jnp.stack(
            [
                slot_table[me ^ (j // sub)] * sub + j % sub
                for j in range(PACK // QBLOCK)
            ]
        )
    else:
        slots = jnp.arange(PACK // QBLOCK, dtype=jnp.int32)

    def to_kernel(array):
        if row_count >= QBLOCK:
            return array
        whole = jnp.zeros_like(array)
        for peer, piece in zip(peers, blocks_of(array)):
            whole = lax.dynamic_update_slice(whole, piece, (peer * row_count, 0))
        return whole

    def from_kernel(array):
        return array if row_count >= QBLOCK else relative_rows(array)

    hidden_in = resid_in.astype(F32)
    normed_own = rms_norm(hidden_in, attention_norm_gain).astype(BF16)
    normed_one = jnp.concatenate(gather_relative(normed_own, "seq"), axis=0)
    first_qkv = jnp.concatenate([adapter_first_factors[k] for k in range(3)], axis=1)
    low_qkv = (mm(normed_one, first_qkv) * mask_rel_three).astype(BF16)
    low_q, low_k, low_v = (low_qkv[:, k * SPAN : (k + 1) * SPAN] for k in range(3))
    second_q = [columns_of(adapter_second_model[0], me, width)]
    second_k = [columns_of(adapter_second_keyvalue[0], me, kv_width)]
    second_v = [columns_of(adapter_second_keyvalue[1], me, kv_width)]

    def twice(rows):
        heads = [rows[:, g * HEAD_DIM : (g + 1) * HEAD_DIM] for g in range(my_groups)]
        return jnp.concatenate([h for h in heads for _ in (0, 1)], axis=1)

    projected = mm(normed_one, qkv_mine)
    query = projected[:, :width] + mm(low_q, second_q[0])
    key = projected[:, width : width + kv_width] + mm(low_k, second_k[0])
    value = projected[:, width + kv_width :] + mm(low_v, second_v[0])
    *saved, attn_heads, log_totals = attend_forward(
        slots, to_kernel(query), to_kernel(twice(key)), to_kernel(twice(value)), tables
    )
    attn_heads = from_kernel(attn_heads)
    attn_own = place_columns(exchange(blocks_of(attn_heads)))
    out_weights = gather_relative(out_mine, "seq")
    low_o = (mm(attn_own, adapter_first_factors[3]) * mask_own).astype(BF16)
    branch = place_columns([mm(attn_own, piece) for piece in out_weights]) + mm(
        low_o, adapter_second_model[1]
    )
    hidden_mid = hidden_in + RESIDUAL_FACTOR * branch
    normed_two_own = rms_norm(hidden_mid, feedfwd_norm_gain).astype(BF16)

    normed_two = jnp.concatenate(gather_relative(normed_two_own, "seq"), axis=0)
    cot_all = jnp.concatenate(gather_relative(cotangent[0], "seq"), axis=0)
    first_ffn = jnp.concatenate([adapter_first_factors[4], adapter_first_factors[5]], axis=1)
    low_ffn = (mm(normed_two, first_ffn) * mask_rel_two).astype(BF16)
    low_g, low_u = low_ffn[:, :SPAN], low_ffn[:, SPAN:]
    (second_ffn,) = take_units(
        [adapter_second_feedfwd.reshape(2 * SPAN, feed_units)], me, seqs, fsdps, unit_block
    )
    second_gate, second_up = second_ffn[:SPAN], second_ffn[SPAN:]
    gate = mm(normed_two, gate_full) + mm(low_g, second_gate)
    up = mm(normed_two, up_full) + mm(low_u, second_up)

    def swiglu(gate_arg, up_arg):
        return jax.nn.sigmoid(gate_arg) * gate_arg * up_arg

    act = swiglu(gate, up).astype(BF16)
    down_full = place_blocks(
        lists[4] + lists[5], 1, jnp.concatenate([rings.owner * 2, rings.owner * 2 + 1])
    )
    first_down = lax.dynamic_index_in_dim(
        adapter_first_down.reshape(fsdps, seqs, unit_block, SPAN), me, 1, keepdims=False
    ).reshape(units, SPAN)
    grad_out = cotangent[0].astype(F32) * valid_col
    grad_down = (RESIDUAL_FACTOR * (cot_all.astype(F32) * valid_rel)).astype(BF16)
    grad_low_d = mm_nt(grad_down, adapter_second_model[2]).astype(BF16) * mask_rel
    grad_gate, grad_up = gate_grads(grad_down, down_full, grad_low_d, first_down, gate, up)
    grad_low_ffn = (
        jnp.concatenate([mm_nt(grad_gate, second_gate), mm_nt(grad_up, second_up)], axis=1).astype(
            BF16
        )
        * mask_rel_two
    )
    keep, give = sum_products(
        [grad_gate, grad_up, grad_low_ffn], [gate_full, up_full, first_ffn]
    )
    act, late_gate, late_up = after((act, grad_gate, grad_up), give)
    grad_normed_two = reduce_halves(keep, give, "seq")
    grad_a_down = mm_tn(grad_low_d, act)
    grad_b_gate = mm_tn(low_g, late_gate)
    grad_b_up = mm_tn(low_u, late_up)

    def split_units(rows):
        return [rows[:, k * width : (k + 1) * width].astype(BF16) for k in range(parts)]

    unit_grads = jnp.concatenate(
        split_units(grad_a_down) + split_units(grad_b_gate) + split_units(grad_b_up), axis=0
    )
    act = after(act, unit_grads)
    unit_bits = list(reversed(bits_down(fsdps)))
    unit_sums = scatter_step(unit_grads, unit_bits[0])
    grad_normed_two, unit_sums = after((grad_normed_two, unit_sums))
    unit_sums = scatter_step(unit_sums, unit_bits[1])
    low_d = (mm(act, first_down) * mask_rel).astype(BF16)
    down_part = mm(act, down_full) + mm(low_d, adapter_second_model[2])
    grad_b_down = mm_tn(low_d, grad_down)
    grad_a_ffn = mm_tn(grad_low_ffn, normed_two)
    _, norm_two_back = jax.vjp(lambda hidden: rms_norm(hidden, feedfwd_norm_gain), hidden_mid)
    grad_mid = grad_out + norm_two_back(grad_normed_two)[0]

    grad_branch = (RESIDUAL_FACTOR * grad_mid).astype(BF16)
    grad_low_o = mm_nt(grad_branch, adapter_second_model[1]).astype(BF16) * mask_own
    grad_b_out = mm_tn(low_o, grad_branch)
    grad_a_out = mm_tn(grad_low_o, attn_own)
    grad_attn = mm_nt(grad_low_o, adapter_first_factors[3]) + mm_nt(
        jnp.concatenate([columns_of(grad_branch, peer, width) for peer in peers], axis=1),
        jnp.concatenate(out_weights, axis=1),
    )
    grad_attn = grad_attn.astype(BF16)
    grad_heads = jnp.concatenate(
        exchange([columns_of(grad_attn, peer, width) for peer in peers]), axis=0
    )
    grad_heads, unit_sums = after((grad_heads, unit_sums))
    for bit in unit_bits[2:]:
        unit_sums = scatter_step(unit_sums, bit)
    down_sum = reduce_relative(blocks_of(down_part), "seq", [grad_heads])
    shared_terms = jnp.concatenate([grad_a_ffn, grad_b_down, grad_a_out, grad_b_out], axis=0)
    shared_sum = reduce_relative(
        [columns_of(shared_terms, peer, width) for peer in peers], "seq", [grad_heads]
    ).astype(BF16)
    grad_qkv = from_kernel(
        attend_backward(slots, saved, to_kernel(grad_heads), log_totals, tables)
    )
    grad_qkv, unit_sums = after((grad_qkv, unit_sums), shared_sum, down_sum)
    grad_query = grad_qkv[:, :width]
    grad_key = grad_qkv[:, width : width + kv_width]
    grad_value = grad_qkv[:, width + kv_width :]
    low_part = jnp.concatenate(
        [
            mm_nt(grad_query, second_q[0]),
            mm_nt(grad_key, second_k[0]),
            mm_nt(grad_value, second_v[0]),
        ],
        axis=1,
    ).astype(BF16)
    grad_low_qkv = reduce_halves(low_part[: PACK // 2], low_part[PACK // 2 :], "seq")
    grad_low_qkv = grad_low_qkv.astype(BF16) * mask_own_three
    wide_bits = bits_down(fsdps)
    unit_sums = widen(unit_sums, wide_bits[0])
    grad_low_qkv, unit_sums = after((grad_low_qkv, unit_sums))
    grad_low_all = jnp.concatenate(gather_relative(grad_low_qkv, "seq"), axis=0)
    for bit in wide_bits[1:-1]:
        unit_sums = widen(unit_sums, bit)
    grad_low_all, unit_sums = after((grad_low_all, unit_sums))
    grad_a_qkv = mm_tn(grad_low_all, columns_of(normed_one, me, width))
    grad_b_q = mm_tn(low_q, grad_query)
    grad_b_kv = [mm_tn(low_k, grad_key), mm_tn(low_v, grad_value)]
    keep_one, give_one = sum_products([grad_qkv], [qkv_mine])
    grad_normed_one = reduce_halves(keep_one, after(give_one, grad_low_all), "seq")
    grad_normed_one = grad_normed_one + mm_nt(grad_low_qkv, first_qkv)
    layer_out = (valid_col * (hidden_mid + RESIDUAL_FACTOR * down_sum)).astype(BF16)
    _, norm_one_back = jax.vjp(lambda hidden: rms_norm(hidden, attention_norm_gain), hidden_in)
    grad_input = (grad_mid + norm_one_back(grad_normed_one)[0]).astype(BF16)

    factor = ADAPTER_TOTAL / math.sqrt(PACK * fsdps)

    def units_out(whole, first):
        part = whole[:, first : first + parts * SPAN]
        part = part.reshape(seqs, parts, SPAN, fsdps // parts, unit_block)
        return part.transpose(2, 1, 3, 0, 4).reshape(SPAN, feed_units)

    late_sums = scatter_step(grad_a_qkv.astype(BF16), unit_bits[0])
    unit_sums = widen(unit_sums, wide_bits[-1])
    late_sums, unit_sums = after((late_sums, unit_sums), grad_normed_one)
    for bit in unit_bits[1:]:
        late_sums = scatter_step(late_sums, bit)
    unit_pieces = gather_relative(unit_sums, "seq")
    early = settle(unit_pieces)
    blank = jnp.zeros((SPAN, width - 2 * kv_width), BF16)
    middle_sums = share_out(
        reduce_scatter_rows(
            jnp.concatenate(
                [
                    shared_sum,
                    grad_b_q.astype(BF16),
                    jnp.concatenate([g.astype(BF16) for g in grad_b_kv] + [blank], axis=1),
                ],
                axis=0,
            )
        )
    )
    def scaled(array):
        return array.astype(F32) * factor

    if unit_block % 128 == 0:
        a_down, b_ffn = finish_units(early, 0, parts, fsdps, unit_block, factor)
    else:
        a_down = scaled(units_out(early, 0).T)
        b_ffn = scaled(
            jnp.stack(
                [units_out(early, parts * SPAN), units_out(early, 2 * parts * SPAN)]
            )
        )
    middle_pieces = gather_relative(middle_sums, "seq", [a_down])
    middle = settle(middle_pieces)
    b_kv = middle[:, 6 * SPAN :, : 2 * kv_width].reshape(seqs, SPAN, 2, kv_width)
    a_all, b_model = finish_model(middle, factor)
    late_sums = share_out(late_sums)
    late = settle(gather_relative(late_sums, "seq", [b_model]))
    return (
        layer_out[None],
        grad_input[None],
        finish_late(late, a_all, factor),
        a_down,
        b_model,
        scaled(b_kv.transpose(2, 1, 0, 3).reshape(2, SPAN, KV_HEADS * HEAD_DIM)),
        b_ffn,
    )


def solution(mesh):
    rows = P("fsdp", None)
    placed = (
        (P("fsdp", "seq", None),) * 2 + (rows,) * 2 + (P(),) * 2 + (rows,) * 7 + (P(),) * 5
    )
    return jax.shard_map(
        shards,
        mesh=mesh,
        in_specs=placed,
        out_specs=(P("fsdp", "seq", None), P("fsdp", "seq", None), P(), P(), P(), P(), P()),
        check_vma=False,
    )
```

```python
import math

import jax
import jax.numpy as jnp
from jax import lax
from jax.experimental import pallas as pl
from jax.experimental.pallas import tpu as pltpu
from jax.sharding import PartitionSpec as P

MODEL_WIDTH = 2048
HEADS = 32
KV_HEADS = 8
HEAD_DIM = 64
ADAPTER_RANK = 16
ADAPTER_TOTAL = 8
PACK = 1024
QBLOCK = 256
SPAN = ADAPTER_TOTAL * ADAPTER_RANK
GROUP = HEADS // KV_HEADS

SCORE_SCALE = 0.015625
RESIDUAL_FACTOR = 0.22
NORM_EPSILON = 1e-05
ROPE_BASE = 10000000.0
MASK_FILL = 1e30

BF16 = jnp.bfloat16
F32 = jnp.float32


def mm(left, right):
    return jnp.dot(left, right, preferred_element_type=F32)


def mm_nt(left, right):
    return lax.dot_general(left, right, (((1,), (1,)), ((), ())), preferred_element_type=F32)


def mm_tn(left, right):
    return lax.dot_general(left, right, (((0,), (0,)), ((), ())), preferred_element_type=F32)


def rms_norm(hidden, gain_vec):
    mean_square = jnp.mean(hidden * hidden, axis=-1, keepdims=True)
    return hidden * lax.rsqrt(mean_square + NORM_EPSILON) * gain_vec


def pack_tables(seq_lengths, adapter_id, token_count, adapter_count):
    slots = seq_lengths.shape[0]
    places = jnp.arange(token_count, dtype=jnp.int32)
    seq_ends = jnp.cumsum(seq_lengths)
    seq_starts = seq_ends - seq_lengths
    used_len = seq_ends[slots - 1]
    segment = jnp.sum((places[:, None] >= seq_ends[None, :]).astype(jnp.int32), axis=1)
    member = segment[:, None] == jnp.arange(slots, dtype=jnp.int32)[None, :]
    start_tok = jnp.sum(jnp.where(member, seq_starts[None, :], 0), axis=1) + jnp.where(
        segment == slots, used_len, 0
    )
    position = places - start_tok
    valid_row = segment < slots
    chosen = adapter_id[:, None] == jnp.arange(adapter_count, dtype=jnp.int32)[None, :]
    onehot = jnp.sum(jnp.where(member[:, :, None] & chosen[None, :, :], 1.0, 0.0), axis=1).astype(F32)
    return (segment, position, valid_row, onehot)


def rope_tables(position, head_size, copies):
    frequency = ROPE_BASE ** (-(jnp.arange(head_size // 2, dtype=F32) * 2.0) / head_size)
    angles = position.astype(F32)[:, None] * frequency[None, :]
    cosine, sine = jnp.cos(angles), jnp.sin(angles)
    return (jnp.tile(cosine, (1, 2 * copies)), jnp.tile(sine, (1, 2 * copies)))


def bits_down(count):
    bits, bit = [], count >> 1
    while bit:
        bits.append(bit)
        bit >>= 1
    return bits


def relative_order(count):
    order = [0]
    for bit in bits_down(count):
        order = order + [o ^ bit for o in order]
    return order


def swap(block, axis, offset):
    count = lax.axis_size(axis)
    return lax.ppermute(block, axis, [(i, i ^ offset) for i in range(count)])


def gather_relative(block, axis, last=()):
    pieces = [block]
    for bit in bits_down(lax.axis_size(axis)):
        if bit == 1:
            pieces[-1] = after(pieces[-1], *last)
        pieces = pieces + [swap(piece, axis, bit) for piece in pieces]
    return pieces


def reduce_relative(pieces, axis, last=()):
    for bit in reversed(bits_down(lax.axis_size(axis))):
        half = len(pieces) // 2
        given = [piece.astype(BF16) for piece in pieces[half:]]
        if half == 1:
            given = [after(given[0], *last)]
        got = [swap(piece, axis, bit) for piece in given]
        pieces = [mine.astype(F32) + other.astype(F32) for mine, other in zip(pieces[:half], got)]
    return pieces[0]


def reduce_halves(keep, give, axis):
    bits = list(reversed(bits_down(lax.axis_size(axis))))
    for bit in bits:
        got = swap(give, axis, bit)
        total = keep.astype(F32) + got.astype(F32)
        half = total.shape[0] // 2
        keep, give = total[:half], total[half:].astype(BF16)
    return total


def cycle_of(count):
    return list(range(0, count, 2)) + list(range(count - 1, 0, -2))


class Rings:
    WINDOW = 3

    def __init__(self):
        self.count = lax.axis_size("fsdp")
        cycle = cycle_of(self.count)
        place = {device: k for k, device in enumerate(cycle)}
        table = [
            [cycle[(place[device] - k) % self.count] for k in range(self.count)]
            for device in range(self.count)
        ]
        self.owner = lax.dynamic_index_in_dim(
            jnp.array(table, jnp.int32), lax.axis_index("fsdp"), 0, keepdims=False
        )
        ahead = [(cycle[k], cycle[(k + 1) % self.count]) for k in range(self.count)]
        self.perms = (ahead, [(b, a) for a, b in ahead])
        self.sent = ([], [])

    def send(self, way, block):
        sent = self.sent[way]
        if len(sent) >= self.WINDOW:
            block, _ = lax.optimization_barrier((block, sent[-self.WINDOW]))
        got = lax.ppermute(block, "fsdp", self.perms[way])
        sent.append(got)
        return got

    def gather(self, blocks, starts):
        half = self.count // 2
        found = [{0: block} for block in blocks]
        latest = [[block, block] for block in blocks]
        for time in range(1, half + max(starts) + 1):
            for which in range(len(blocks)):
                step = time - starts[which]
                if not 1 <= step <= half:
                    continue
                for way in (0, 1):
                    if step == half and way != which % 2:
                        continue
                    got = self.send(way, latest[which][way])
                    latest[which][way] = got
                    found[which][step if way == 0 else self.count - step] = got
        return [[f[k] for k in range(self.count)] for f in found]


def place_blocks(pieces, counts, targets):
    rows = pieces[0].shape[0] // counts
    columns = pieces[0].shape[1]
    total = len(pieces) * counts

    def body(target_ref, *refs):
        out_ref, held, came, left = refs[-4:]
        arrivals, departures = [], []
        for i in range(len(pieces)):
            for j in range(counts):
                k = i * counts + j
                first = pl.multiple_of(target_ref[k] * rows, rows)
                arrivals.append(
                    pltpu.make_async_copy(
                        refs[i].at[pl.ds(j * rows, rows), :], held.at[k], came.at[k]
                    )
                )
                departures.append(
                    pltpu.make_async_copy(
                        held.at[k], out_ref.at[pl.ds(first, rows), :], left.at[k]
                    )
                )
        for copy in arrivals:
            copy.start()
        for arrival, departure in zip(arrivals, departures):
            arrival.wait()
            departure.start()
        for copy in departures:
            copy.wait()

    return pl.pallas_call(
        body,
        out_shape=jax.ShapeDtypeStruct((rows * total, columns), pieces[0].dtype),
        grid_spec=pltpu.PrefetchScalarGridSpec(
            num_scalar_prefetch=1,
            grid=(),
            in_specs=[pl.BlockSpec(memory_space=pl.ANY)] * len(pieces),
            out_specs=pl.BlockSpec(memory_space=pl.ANY),
            scratch_shapes=[
                pltpu.VMEM((total, rows, columns), pieces[0].dtype),
                pltpu.SemaphoreType.DMA((total,)),
                pltpu.SemaphoreType.DMA((total,)),
            ],
        ),
        cost_estimate=pl.CostEstimate(
            flops=0, transcendentals=0, bytes_accessed=4 * rows * total * columns
        ),
        name="place_blocks",
    )(targets.astype(jnp.int32), *pieces)


def after(value, *others):
    return lax.optimization_barrier((value, others))[0]


def take_units(matrices, peer, seqs, runs, unit_block):
    if unit_block % 128:
        return [
            lax.dynamic_index_in_dim(
                m.reshape(m.shape[0], runs, seqs, unit_block), peer, 2, keepdims=False
            ).reshape(m.shape[0], runs * unit_block)
            for m in matrices
        ]

    def body(peer_ref, *refs):
        for source, target in zip(refs[: len(matrices)], refs[len(matrices) :]):
            target[...] = source[...]

    return pl.pallas_call(
        body,
        grid_spec=pltpu.PrefetchScalarGridSpec(
            num_scalar_prefetch=1,
            grid=(runs,),
            in_specs=[
                pl.BlockSpec((m.shape[0], unit_block), lambda f, at: (0, f * seqs + at[0]))
                for m in matrices
            ],
            out_specs=[
                pl.BlockSpec((m.shape[0], unit_block), lambda f, at: (0, f)) for m in matrices
            ],
        ),
        out_shape=[
            jax.ShapeDtypeStruct((m.shape[0], runs * unit_block), m.dtype) for m in matrices
        ],
        name="take_units",
    )(peer.astype(jnp.int32)[None], *matrices)


def finish_units(whole, first, parts, runs, unit_block, factor):
    seqs, _, columns = whole.shape
    feed_units = seqs * runs * unit_block
    per = runs // parts

    def body(down_ref, gate_ref, up_ref, a_ref, b_ref):
        for s in range(seqs):
            here = slice(s * unit_block, (s + 1) * unit_block)
            a_ref[here, :] = down_ref[s].astype(F32).T * factor
            b_ref[0, :, here] = gate_ref[s].astype(F32) * factor
            b_ref[1, :, here] = up_ref[s].astype(F32) * factor

    def part(which):
        base = first // SPAN + which * parts
        return pl.BlockSpec((seqs, SPAN, unit_block), lambda k, g: (0, base + k, g))

    return pl.pallas_call(
        body,
        grid=(parts, per),
        in_specs=[part(0), part(1), part(2)],
        out_specs=[
            pl.BlockSpec((seqs * unit_block, SPAN), lambda k, g: (k * per + g, 0)),
            pl.BlockSpec((2, SPAN, seqs * unit_block), lambda k, g: (0, 0, k * per + g)),
        ],
        out_shape=[
            jax.ShapeDtypeStruct((feed_units, SPAN), F32),
            jax.ShapeDtypeStruct((2, SPAN, feed_units), F32),
        ],
        name="finish_units",
    )(whole, whole, whole)


def finish_model(whole, factor):
    seqs, _, columns = whole.shape

    def body(shared_ref, heads_ref, a_ref, b_ref):
        def rows(k):
            return shared_ref[0, k * SPAN : (k + 1) * SPAN].astype(F32) * factor

        a_ref[0] = rows(3).T
        a_ref[1] = rows(0).T
        a_ref[2] = rows(1).T
        b_ref[0] = heads_ref[0].astype(F32) * factor
        b_ref[1] = rows(4)
        b_ref[2] = rows(2)

    return pl.pallas_call(
        body,
        grid=(seqs,),
        in_specs=[
            pl.BlockSpec((1, 5 * SPAN, columns), lambda s: (s, 0, 0)),
            pl.BlockSpec((1, SPAN, columns), lambda s: (s, 5, 0)),
        ],
        out_specs=[
            pl.BlockSpec((3, columns, SPAN), lambda s: (1, s, 0)),
            pl.BlockSpec((3, SPAN, columns), lambda s: (0, 0, s)),
        ],
        out_shape=[
            jax.ShapeDtypeStruct((6, MODEL_WIDTH, SPAN), F32),
            jax.ShapeDtypeStruct((3, SPAN, MODEL_WIDTH), F32),
        ],
        name="finish_model",
    )(whole, whole)


def finish_late(late, a_all, factor):
    seqs, _, columns = late.shape

    def body(late_ref, held_ref, a_ref):
        for j in range(3):
            a_ref[j] = late_ref[0, j * SPAN : (j + 1) * SPAN].astype(F32).T * factor

    return pl.pallas_call(
        body,
        grid=(seqs,),
        in_specs=[
            pl.BlockSpec((1, 3 * SPAN, columns), lambda s: (s, 0, 0)),
            pl.BlockSpec(memory_space=pl.ANY),
        ],
        out_specs=pl.BlockSpec((3, columns, SPAN), lambda s: (0, s, 0)),
        out_shape=jax.ShapeDtypeStruct(a_all.shape, F32),
        input_output_aliases={1: 0},
        name="finish_late",
    )(late, a_all)


def half_lanes(shape):
    lane = lax.broadcasted_iota(jnp.int32, shape, 1)
    return lane % HEAD_DIM < HEAD_DIM // 2


def turn_tile(x, cosine, sine):
    quarter = HEAD_DIM // 2
    ahead = pltpu.roll(x, 2 * HEAD_DIM - quarter, 1)
    behind = pltpu.roll(x, quarter, 1)
    return x * cosine + jnp.where(half_lanes(x.shape), -ahead, behind) * sine


def dot_tn(left, right):
    return lax.dot_general(left, right, (((0,), (0,)), ((), ())), preferred_element_type=F32)


def dot_nt(left, right):
    return lax.dot_general(left, right, (((1,), (1,)), ((), ())), preferred_element_type=F32)


def allowed_pairs(seg_col, seg_row, block):
    keys = (block + 1) * QBLOCK
    shape = (keys, QBLOCK)
    key_at = lax.broadcasted_iota(jnp.int32, shape, 0)
    query_at = lax.broadcasted_iota(jnp.int32, shape, 1) + block * QBLOCK
    same = seg_col[:keys, :] == seg_row[:, block * QBLOCK : keys]
    return same & (key_at <= query_at)


def forward_body(
    blocks, slot_ref, q_ref, k_ref, v_ref, cos_ref, sin_ref, col_ref, row_ref,
    qn_ref, kn_ref, vn_ref, out_ref, lse_ref,
):
    for j in range(blocks):
        here = slice(j * QBLOCK, (j + 1) * QBLOCK)
        there = pl.ds(pl.multiple_of(slot_ref[j] * QBLOCK, QBLOCK), QBLOCK)
        cosine, sine = cos_ref[here, :], sin_ref[here, :]
        qn_ref[here, :] = turn_tile(q_ref[there, :], cosine, sine).astype(BF16)
        kn_ref[here, :] = turn_tile(k_ref[there, :], cosine, sine).astype(BF16)
        vn_ref[here, :] = v_ref[there, :].astype(BF16)
    lane = lax.broadcasted_iota(jnp.int32, (QBLOCK, 2 * HEAD_DIM), 1)
    row = lax.broadcasted_iota(jnp.int32, (2 * HEAD_DIM, QBLOCK), 0)
    for i in range(blocks):
        here = slice(i * QBLOCK, (i + 1) * QBLOCK)
        keys = (i + 1) * QBLOCK
        allowed = allowed_pairs(col_ref[...], row_ref[...], i)
        query = (qn_ref[here, :].astype(F32) * SCORE_SCALE).astype(BF16)
        outs = []
        for e in range(2):
            mine = jnp.where(lane // HEAD_DIM == e, query, jnp.zeros_like(query))
            scores = jnp.where(allowed, dot_nt(kn_ref[:keys, :], mine), -MASK_FILL)
            most = jnp.max(scores, axis=0, keepdims=True)
            exponent = jnp.exp(scores - most)
            total = jnp.sum(exponent, axis=0, keepdims=True)
            probs = (exponent * (1.0 / total)).astype(BF16)
            lse_ref[0, e : e + 1, here] = most + jnp.log(total)
            outs.append(dot_tn(vn_ref[:keys, :], probs))
        out = jnp.where(row < HEAD_DIM, outs[0], outs[1]).T
        there = pl.ds(pl.multiple_of(slot_ref[i] * QBLOCK, QBLOCK), QBLOCK)
        out_ref[there, :] = out.astype(BF16)


def backward_body(
    blocks, groups, slot_ref, qn_ref, kn_ref, vn_ref, do_ref, lse_ref, cos_ref, sin_ref, col_ref,
    row_ref, out_ref, dk_sum, dv_sum,
):
    pairs_per_group = GROUP // 2
    pair = pl.program_id(0)
    step = lax.rem(pair, pairs_per_group)
    two = 2 * HEAD_DIM

    @pl.when(step == 0)
    def _():
        dk_sum[...] = jnp.zeros_like(dk_sum)
        dv_sum[...] = jnp.zeros_like(dv_sum)

    lane = lax.broadcasted_iota(jnp.int32, (QBLOCK, two), 1)
    row = lax.broadcasted_iota(jnp.int32, (two, QBLOCK), 0)

    def place(j):
        return pl.ds(pl.multiple_of(slot_ref[j] * QBLOCK, QBLOCK), QBLOCK)

    for i in range(blocks):
        here = slice(i * QBLOCK, (i + 1) * QBLOCK)
        keys = (i + 1) * QBLOCK
        allowed = allowed_pairs(col_ref[...], row_ref[...], i)
        query = (qn_ref[here, :].astype(F32) * SCORE_SCALE).astype(BF16)
        grad = do_ref[place(i), :]
        outs = []
        for e in range(2):
            mine = jnp.where(lane // HEAD_DIM == e, query, jnp.zeros_like(query))
            grad_mine = jnp.where(lane // HEAD_DIM == e, grad, jnp.zeros_like(grad))
            scores = jnp.where(allowed, dot_nt(kn_ref[:keys, :], mine), -MASK_FILL)
            probs = jnp.exp(scores - lse_ref[0, e : e + 1, here])
            grad_probs = dot_nt(vn_ref[:keys, :], grad_mine)
            delta = jnp.sum(probs * grad_probs, axis=0, keepdims=True)
            grad_scores = (probs * (grad_probs - delta)).astype(BF16)
            dv_sum[:keys, :] += jnp.dot(probs.astype(BF16), grad_mine, preferred_element_type=F32)
            dk_sum[:keys, :] += jnp.dot(grad_scores, mine, preferred_element_type=F32)
            outs.append(dot_tn(kn_ref[:keys, :], grad_scores))
        out = jnp.where(row < HEAD_DIM, outs[0], outs[1]).T * SCORE_SCALE
        out = out.astype(BF16).astype(F32)
        out_ref[place(i), pl.ds(pl.multiple_of(pair * two, two), two)] = turn_tile(
            out, cos_ref[here, :], -sin_ref[here, :]
        ).astype(BF16)

    width = groups * GROUP * HEAD_DIM
    for g in range(groups):

        @pl.when(pair == (g + 1) * pairs_per_group - 1)
        def _(g=g):
            for j in range(blocks):
                here = slice(j * QBLOCK, (j + 1) * QBLOCK)
                dk = dk_sum[here, :]
                dk = (dk + pltpu.roll(dk, HEAD_DIM, 1)).astype(BF16).astype(F32)
                dk = turn_tile(dk, cos_ref[here, :], -sin_ref[here, :]).astype(BF16)
                dv = dv_sum[here, :]
                dv = (dv + pltpu.roll(dv, HEAD_DIM, 1)).astype(BF16)
                for base, values in ((width, dk), (width + groups * HEAD_DIM, dv)):
                    first = base + g * HEAD_DIM
                    tile = slice(first // two * two, first // two * two + two)
                    half = first // HEAD_DIM % 2
                    old = out_ref[place(j), tile]
                    out_ref[place(j), tile] = jnp.where(lane // HEAD_DIM == half, values, old)


def attention_specs():
    tile = pl.BlockSpec((PACK, 2 * HEAD_DIM), lambda p, slot: (0, p))
    group = pl.BlockSpec((PACK, 2 * HEAD_DIM), lambda p, slot: (0, p // (GROUP // 2)))
    lse = pl.BlockSpec((1, 2, PACK), lambda p, slot: (p, 0, 0))
    table = pl.BlockSpec((PACK, 2 * HEAD_DIM), lambda p, slot: (0, 0))
    col = pl.BlockSpec((PACK, 1), lambda p, slot: (0, 0))
    row = pl.BlockSpec((1, PACK), lambda p, slot: (0, 0))
    return tile, group, lse, [table, table, col, row]


def attend_forward(slots, query, key, value, tables):
    pairs = query.shape[1] // (2 * HEAD_DIM)
    groups = key.shape[1] // (2 * HEAD_DIM)
    tile, group, lse, rest = attention_specs()
    blocks = PACK // QBLOCK
    return pl.pallas_call(
        lambda *refs: forward_body(blocks, *refs),
        grid_spec=pltpu.PrefetchScalarGridSpec(
            num_scalar_prefetch=1,
            grid=(pairs,),
            in_specs=[tile, group, group] + rest,
            out_specs=[tile, group, group, tile, lse],
        ),
        out_shape=[
            jax.ShapeDtypeStruct((PACK, pairs * 2 * HEAD_DIM), BF16),
            jax.ShapeDtypeStruct((PACK, groups * 2 * HEAD_DIM), BF16),
            jax.ShapeDtypeStruct((PACK, groups * 2 * HEAD_DIM), BF16),
            jax.ShapeDtypeStruct((PACK, pairs * 2 * HEAD_DIM), BF16),
            jax.ShapeDtypeStruct((pairs, 2, PACK), F32),
        ],
        cost_estimate=pl.CostEstimate(
            flops=4 * pairs * 2 * PACK * PACK * HEAD_DIM,
            transcendentals=pairs * PACK * PACK,
            bytes_accessed=8 * PACK * MODEL_WIDTH,
        ),
        name="attend_forward",
    )(slots, query, key, value, *tables)


def attend_backward(slots, saved, grad, log_totals, tables):
    query, key, value = saved
    pairs = query.shape[1] // (2 * HEAD_DIM)
    groups = key.shape[1] // (2 * HEAD_DIM)
    tile, group, lse, rest = attention_specs()
    blocks = PACK // QBLOCK
    columns = pairs * 2 * HEAD_DIM + groups * 2 * HEAD_DIM
    return pl.pallas_call(
        lambda *refs: backward_body(blocks, groups, *refs),
        grid_spec=pltpu.PrefetchScalarGridSpec(
            num_scalar_prefetch=1,
            grid=(pairs,),
            in_specs=[tile, group, group, tile, lse] + rest,
            out_specs=pl.BlockSpec((PACK, columns), lambda p, slot: (0, 0)),
            scratch_shapes=[pltpu.VMEM((PACK, 2 * HEAD_DIM), F32)] * 2,
        ),
        out_shape=jax.ShapeDtypeStruct((PACK, columns), BF16),
        cost_estimate=pl.CostEstimate(flops=0, transcendentals=0, bytes_accessed=0),
        name="attend_backward",
    )(slots, query, key, value, grad, log_totals, *tables)


def tile_of(count):
    return 256 if count % 256 == 0 else 128


def gate_grads(grad_down, down, grad_low, first_down, gate, up):
    tokens, units = gate.shape
    tile = tile_of(units)

    def body(gd_ref, down_ref, gl_ref, fd_ref, gate_ref, up_ref, gg_ref, gu_ref):
        grad_act = dot_nt(gd_ref[...], down_ref[...]) + dot_nt(gl_ref[...], fd_ref[...])
        gate_here = gate_ref[...]
        share = jax.nn.sigmoid(gate_here)
        gu_ref[...] = (grad_act * share * gate_here).astype(BF16)
        gg_ref[...] = (
            grad_act * up_ref[...] * share * (1.0 + gate_here * (1.0 - share))
        ).astype(BF16)

    def whole(array):
        return pl.BlockSpec(array.shape, lambda t: (0, 0))

    def rows(array):
        return pl.BlockSpec((tile, array.shape[1]), lambda t: (t, 0))

    cols = pl.BlockSpec((tokens, tile), lambda t: (0, t))
    return pl.pallas_call(
        body,
        grid=(units // tile,),
        in_specs=[whole(grad_down), rows(down), whole(grad_low), rows(first_down), cols, cols],
        out_specs=[cols, cols],
        out_shape=[jax.ShapeDtypeStruct((tokens, units), BF16)] * 2,
        cost_estimate=pl.CostEstimate(
            flops=2 * tokens * units * MODEL_WIDTH,
            transcendentals=tokens * units,
            bytes_accessed=12 * tokens * units + 2 * units * MODEL_WIDTH,
        ),
        name="gate_grads",
    )(grad_down, down, grad_low, first_down, gate, up)


def sum_products(lefts, rights):
    tokens, outs = lefts[0].shape[0], rights[0].shape[0]
    tile = tile_of(outs)
    count = len(lefts)

    def body(*refs):
        total = dot_nt(refs[0][...], refs[count][...])
        for k in range(1, count):
            total = total + dot_nt(refs[k][...], refs[count + k][...])
        refs[-2][...] = total[: tokens // 2].astype(BF16)
        refs[-1][...] = total[tokens // 2 :].astype(BF16)

    half = pl.BlockSpec((tokens // 2, tile), lambda t: (0, t))
    return pl.pallas_call(
        body,
        grid=(outs // tile,),
        in_specs=[pl.BlockSpec(a.shape, lambda t: (0, 0)) for a in lefts]
        + [pl.BlockSpec((tile, b.shape[1]), lambda t: (t, 0)) for b in rights],
        out_specs=[half, half],
        out_shape=[jax.ShapeDtypeStruct((tokens // 2, outs), BF16)] * 2,
        cost_estimate=pl.CostEstimate(
            flops=sum(2 * tokens * outs * a.shape[1] for a in lefts),
            transcendentals=0,
            bytes_accessed=2 * sum(a.size for a in [*lefts, *rights]) + 2 * tokens * outs,
        ),
        name="sum_products",
    )(*lefts, *rights)


def reverse_bits(value, count):
    out, bit, other = 0, 1, count >> 1
    while other:
        out = out + jnp.where((value & bit) != 0, other, 0)
        bit, other = bit << 1, other >> 1
    return out


def pairs_of(bits):
    return [bits[k : k + 2] for k in range(0, len(bits), 2)]


def scatter_step(total, *bits):
    me = lax.axis_index("fsdp")
    rows = total.shape[0] >> len(bits)
    offsets = [0]
    for bit in bits:
        offsets = offsets + [o ^ bit for o in offsets]

    def run_of(device):
        number = 0
        for bit in bits:
            number = 2 * number + ((device & bit) != 0).astype(jnp.int32)
        return lax.dynamic_slice_in_dim(total, number * rows, rows, 0)

    kept = run_of(me).astype(F32)
    for got in [swap(run_of(me ^ o), "fsdp", o) for o in offsets[1:]]:
        kept = kept + got.astype(F32)
    return kept.astype(BF16)


def reduce_scatter_rows(total):
    first, *rest = reversed(bits_down(lax.axis_size("fsdp")))
    total = scatter_step(total, first)
    for bits in pairs_of(rest):
        total = scatter_step(total, *bits)
    return total


def widen(piece, *bits):
    pieces, sent = [piece], [0]
    for bit in bits:
        sent = sent + [o ^ bit for o in sent]
    return jnp.concatenate(pieces + [swap(piece, "fsdp", o) for o in sent[1:]], axis=0)


def share_out(piece):
    for bits in pairs_of(bits_down(lax.axis_size("fsdp"))):
        piece = widen(piece, *bits)
    return piece


def settle(pieces):
    count, seqs = lax.axis_size("fsdp"), lax.axis_size("seq")
    me, me_seq = lax.axis_index("fsdp"), lax.axis_index("seq")
    rows, columns = pieces[0].shape
    targets = jnp.stack(
        [
            (me_seq ^ s) * count + reverse_bits(me ^ o, count)
            for s in relative_order(seqs)
            for o in relative_order(count)
        ]
    )
    return place_blocks(pieces, count, targets).reshape(seqs, rows, columns)


def shards(
    tokens,
    cotangent,
    lengths,
    sequence_adapter,
    attention_norm_gain,
    feedfwd_norm_gain,
    query_matrix,
    key_matrix,
    value_matrix,
    output_matrix,
    gate_matrix,
    up_matrix,
    down_matrix,
    adapter_first_factors,
    adapter_first_down,
    adapter_second_model,
    adapter_second_keyvalue,
    adapter_second_feedfwd,
):
    seqs, fsdps = lax.axis_size("seq"), lax.axis_size("fsdp")
    me = lax.axis_index("seq")
    order = relative_order(seqs)
    peers = [me ^ o for o in order]
    resid_in = tokens[0]
    row_count = resid_in.shape[0]
    width = MODEL_WIDTH // seqs
    kv_width = KV_HEADS * HEAD_DIM // seqs
    my_groups = KV_HEADS // seqs
    feed_units = gate_matrix.shape[1]
    unit_block = feed_units // (seqs * fsdps)
    units = feed_units // seqs
    parts = units // width

    def columns_of(array, peer, count):
        return lax.dynamic_slice_in_dim(array, peer * count, count, array.ndim - 1)

    def rows_of(array, peer):
        return lax.dynamic_slice_in_dim(array, peer * row_count, row_count, 0)

    def relative_rows(array):
        return jnp.concatenate([rows_of(array, peer) for peer in peers], axis=0)

    def blocks_of(array):
        return [array[k * row_count : (k + 1) * row_count] for k in range(seqs)]

    def exchange(pieces):
        return [p if o == 0 else swap(p, "seq", o) for o, p in zip(order, pieces)]

    def place_columns(pieces):
        rows, count = pieces[0].shape
        whole = jnp.zeros((rows, count * seqs), pieces[0].dtype)
        for peer, piece in zip(peers, pieces):
            whole = lax.dynamic_update_slice(whole, piece, (0, peer * count))
        return whole

    rings = Rings()
    qkv_share = jnp.concatenate(
        [
            columns_of(query_matrix, me, width),
            columns_of(key_matrix, me, kv_width),
            columns_of(value_matrix, me, kv_width),
        ],
        axis=1,
    )
    gate_share, up_share = take_units([gate_matrix, up_matrix], me, seqs, fsdps, unit_block)
    out_share = columns_of(output_matrix, me, width)
    down_share = lax.dynamic_slice_in_dim(down_matrix, me * unit_block, unit_block, 0)
    half_block = unit_block // 2
    lists = rings.gather(
        [
            qkv_share,
            out_share,
            gate_share,
            up_share,
            down_share[:half_block],
            down_share[half_block:],
        ],
        [0, 0, 2, 3, 5, 6],
    )
    qkv_mine, out_mine, gate_full, up_full = (
        place_blocks(blocks, 1, rings.owner) for blocks in lists[:4]
    )

    segment, position, valid_row, onehot = pack_tables(
        lengths[0], sequence_adapter[0], PACK, ADAPTER_TOTAL
    )
    valid_all = jnp.where(valid_row, 1.0, 0.0).astype(F32)[:, None]
    mask_all = jnp.repeat(onehot, ADAPTER_RANK, axis=1).astype(BF16)
    valid_rel = relative_rows(valid_all)
    mask_rel = relative_rows(mask_all)
    valid_col, mask_own = valid_rel[:row_count], mask_rel[:row_count]
    mask_own_three = jnp.tile(mask_own, (1, 3))
    mask_rel_two = jnp.tile(mask_rel, (1, 2))
    mask_rel_three = jnp.tile(mask_rel, (1, 3))
    cosine, sine = rope_tables(position, HEAD_DIM, 2)
    tables = (cosine, sine, segment[:, None], segment[None, :])
    slot_of = [0] * seqs
    for k, o in enumerate(order):
        slot_of[o] = k
    slot_table = jnp.array(slot_of, jnp.int32)
    sub = row_count // QBLOCK if row_count >= QBLOCK else 1
    if row_count >= QBLOCK:
        slots = jnp.stack(
            [
                slot_table[me ^ (j // sub)] * sub + j % sub
                for j in range(PACK // QBLOCK)
            ]
        )
    else:
        slots = jnp.arange(PACK // QBLOCK, dtype=jnp.int32)

    def to_kernel(array):
        if row_count >= QBLOCK:
            return array
        whole = jnp.zeros_like(array)
        for peer, piece in zip(peers, blocks_of(array)):
            whole = lax.dynamic_update_slice(whole, piece, (peer * row_count, 0))
        return whole

    def from_kernel(array):
        return array if row_count >= QBLOCK else relative_rows(array)

    hidden_in = resid_in.astype(F32)
    normed_own = rms_norm(hidden_in, attention_norm_gain).astype(BF16)
    normed_one = jnp.concatenate(gather_relative(normed_own, "seq"), axis=0)
    first_qkv = jnp.concatenate([adapter_first_factors[k] for k in range(3)], axis=1)
    low_qkv = (mm(normed_one, first_qkv) * mask_rel_three).astype(BF16)
    low_q, low_k, low_v = (low_qkv[:, k * SPAN : (k + 1) * SPAN] for k in range(3))
    second_q = [columns_of(adapter_second_model[0], me, width)]
    second_k = [columns_of(adapter_second_keyvalue[0], me, kv_width)]
    second_v = [columns_of(adapter_second_keyvalue[1], me, kv_width)]

    def twice(rows):
        heads = [rows[:, g * HEAD_DIM : (g + 1) * HEAD_DIM] for g in range(my_groups)]
        return jnp.concatenate([h for h in heads for _ in (0, 1)], axis=1)

    projected = mm(normed_one, qkv_mine)
    query = projected[:, :width] + mm(low_q, second_q[0])
    key = projected[:, width : width + kv_width] + mm(low_k, second_k[0])
    value = projected[:, width + kv_width :] + mm(low_v, second_v[0])
    *saved, attn_heads, log_totals = attend_forward(
        slots, to_kernel(query), to_kernel(twice(key)), to_kernel(twice(value)), tables
    )
    attn_heads = from_kernel(attn_heads)
    attn_own = place_columns(exchange(blocks_of(attn_heads)))
    out_weights = gather_relative(out_mine, "seq")
    low_o = (mm(attn_own, adapter_first_factors[3]) * mask_own).astype(BF16)
    branch = place_columns([mm(attn_own, piece) for piece in out_weights]) + mm(
        low_o, adapter_second_model[1]
    )
    hidden_mid = hidden_in + RESIDUAL_FACTOR * branch
    normed_two_own = rms_norm(hidden_mid, feedfwd_norm_gain).astype(BF16)

    normed_two = jnp.concatenate(gather_relative(normed_two_own, "seq"), axis=0)
    cot_all = jnp.concatenate(gather_relative(cotangent[0], "seq"), axis=0)
    first_ffn = jnp.concatenate([adapter_first_factors[4], adapter_first_factors[5]], axis=1)
    low_ffn = (mm(normed_two, first_ffn) * mask_rel_two).astype(BF16)
    low_g, low_u = low_ffn[:, :SPAN], low_ffn[:, SPAN:]
    (second_ffn,) = take_units(
        [adapter_second_feedfwd.reshape(2 * SPAN, feed_units)], me, seqs, fsdps, unit_block
    )
    second_gate, second_up = second_ffn[:SPAN], second_ffn[SPAN:]
    gate = mm(normed_two, gate_full) + mm(low_g, second_gate)
    up = mm(normed_two, up_full) + mm(low_u, second_up)

    def swiglu(gate_arg, up_arg):
        return jax.nn.sigmoid(gate_arg) * gate_arg * up_arg

    act = swiglu(gate, up).astype(BF16)
    down_full = place_blocks(
        lists[4] + lists[5], 1, jnp.concatenate([rings.owner * 2, rings.owner * 2 + 1])
    )
    first_down = lax.dynamic_index_in_dim(
        adapter_first_down.reshape(fsdps, seqs, unit_block, SPAN), me, 1, keepdims=False
    ).reshape(units, SPAN)
    grad_out = cotangent[0].astype(F32) * valid_col
    grad_down = (RESIDUAL_FACTOR * (cot_all.astype(F32) * valid_rel)).astype(BF16)
    grad_low_d = mm_nt(grad_down, adapter_second_model[2]).astype(BF16) * mask_rel
    grad_gate, grad_up = gate_grads(grad_down, down_full, grad_low_d, first_down, gate, up)
    grad_low_ffn = (
        jnp.concatenate([mm_nt(grad_gate, second_gate), mm_nt(grad_up, second_up)], axis=1).astype(
            BF16
        )
        * mask_rel_two
    )
    keep, give = sum_products(
        [grad_gate, grad_up, grad_low_ffn], [gate_full, up_full, first_ffn]
    )
    act, late_gate, late_up = after((act, grad_gate, grad_up), give)
    grad_normed_two = reduce_halves(keep, give, "seq")
    grad_a_down = mm_tn(grad_low_d, act)
    grad_b_gate = mm_tn(low_g, late_gate)
    grad_b_up = mm_tn(low_u, late_up)

    def split_units(rows):
        return [rows[:, k * width : (k + 1) * width].astype(BF16) for k in range(parts)]

    unit_grads = jnp.concatenate(
        split_units(grad_a_down) + split_units(grad_b_gate) + split_units(grad_b_up), axis=0
    )
    act = after(act, unit_grads)
    unit_bits = list(reversed(bits_down(fsdps)))
    unit_sums = scatter_step(unit_grads, unit_bits[0])
    grad_normed_two, unit_sums = after((grad_normed_two, unit_sums))
    unit_sums = scatter_step(unit_sums, unit_bits[1])
    low_d = (mm(act, first_down) * mask_rel).astype(BF16)
    down_part = mm(act, down_full) + mm(low_d, adapter_second_model[2])
    grad_b_down = mm_tn(low_d, grad_down)
    grad_a_ffn = mm_tn(grad_low_ffn, normed_two)
    _, norm_two_back = jax.vjp(lambda hidden: rms_norm(hidden, feedfwd_norm_gain), hidden_mid)
    grad_mid = grad_out + norm_two_back(grad_normed_two)[0]

    grad_branch = (RESIDUAL_FACTOR * grad_mid).astype(BF16)
    grad_low_o = mm_nt(grad_branch, adapter_second_model[1]).astype(BF16) * mask_own
    grad_b_out = mm_tn(low_o, grad_branch)
    grad_a_out = mm_tn(grad_low_o, attn_own)
    grad_attn = mm_nt(grad_low_o, adapter_first_factors[3]) + mm_nt(
        jnp.concatenate([columns_of(grad_branch, peer, width) for peer in peers], axis=1),
        jnp.concatenate(out_weights, axis=1),
    )
    grad_attn = grad_attn.astype(BF16)
    grad_heads = jnp.concatenate(
        exchange([columns_of(grad_attn, peer, width) for peer in peers]), axis=0
    )
    grad_heads, unit_sums = after((grad_heads, unit_sums))
    for bit in unit_bits[2:]:
        unit_sums = scatter_step(unit_sums, bit)
    down_sum = reduce_relative(blocks_of(down_part), "seq", [grad_heads])
    shared_terms = jnp.concatenate([grad_a_ffn, grad_b_down, grad_a_out, grad_b_out], axis=0)
    shared_sum = reduce_relative(
        [columns_of(shared_terms, peer, width) for peer in peers], "seq", [grad_heads]
    ).astype(BF16)
    grad_qkv = from_kernel(
        attend_backward(slots, saved, to_kernel(grad_heads), log_totals, tables)
    )
    grad_qkv, unit_sums = after((grad_qkv, unit_sums), shared_sum, down_sum)
    grad_query = grad_qkv[:, :width]
    grad_key = grad_qkv[:, width : width + kv_width]
    grad_value = grad_qkv[:, width + kv_width :]
    low_part = jnp.concatenate(
        [
            mm_nt(grad_query, second_q[0]),
            mm_nt(grad_key, second_k[0]),
            mm_nt(grad_value, second_v[0]),
        ],
        axis=1,
    ).astype(BF16)
    grad_low_qkv = reduce_halves(low_part[: PACK // 2], low_part[PACK // 2 :], "seq")
    grad_low_qkv = grad_low_qkv.astype(BF16) * mask_own_three
    wide_bits = bits_down(fsdps)
    unit_sums = widen(unit_sums, wide_bits[0])
    grad_low_qkv, unit_sums = after((grad_low_qkv, unit_sums))
    grad_low_all = jnp.concatenate(gather_relative(grad_low_qkv, "seq"), axis=0)
    for bit in wide_bits[1:-1]:
        unit_sums = widen(unit_sums, bit)
    grad_low_all, unit_sums = after((grad_low_all, unit_sums))
    grad_a_qkv = mm_tn(grad_low_all, columns_of(normed_one, me, width))
    grad_b_q = mm_tn(low_q, grad_query)
    grad_b_kv = [mm_tn(low_k, grad_key), mm_tn(low_v, grad_value)]
    keep_one, give_one = sum_products([grad_qkv], [qkv_mine])
    grad_normed_one = reduce_halves(keep_one, after(give_one, grad_low_all), "seq")
    grad_normed_one = grad_normed_one + mm_nt(grad_low_qkv, first_qkv)
    layer_out = (valid_col * (hidden_mid + RESIDUAL_FACTOR * down_sum)).astype(BF16)
    _, norm_one_back = jax.vjp(lambda hidden: rms_norm(hidden, attention_norm_gain), hidden_in)
    grad_input = (grad_mid + norm_one_back(grad_normed_one)[0]).astype(BF16)

    factor = ADAPTER_TOTAL / math.sqrt(PACK * fsdps)

    def units_out(whole, first):
        part = whole[:, first : first + parts * SPAN]
        part = part.reshape(seqs, parts, SPAN, fsdps // parts, unit_block)
        return part.transpose(2, 1, 3, 0, 4).reshape(SPAN, feed_units)

    late_sums = scatter_step(grad_a_qkv.astype(BF16), unit_bits[0])
    unit_sums = widen(after(unit_sums, late_sums), wide_bits[-1])
    for bits in pairs_of(unit_bits[1:]):
        late_sums = scatter_step(late_sums, *bits)
    late_sums = after(late_sums, grad_normed_one)
    first_bits, *rest_bits = pairs_of(wide_bits)
    late_sums = widen(late_sums, *first_bits)
    late_sums, unit_sums = after((late_sums, unit_sums))
    for bits in rest_bits:
        late_sums = widen(late_sums, *bits)
    unit_pieces = gather_relative(unit_sums, "seq")
    early = settle(unit_pieces)
    blank = jnp.zeros((SPAN, width - 2 * kv_width), BF16)
    middle_sums = share_out(
        reduce_scatter_rows(
            jnp.concatenate(
                [
                    shared_sum,
                    grad_b_q.astype(BF16),
                    jnp.concatenate([g.astype(BF16) for g in grad_b_kv] + [blank], axis=1),
                ],
                axis=0,
            )
        )
    )
    def scaled(array):
        return array.astype(F32) * factor

    if unit_block % 128 == 0:
        a_down, b_ffn = finish_units(early, 0, parts, fsdps, unit_block, factor)
    else:
        a_down = scaled(units_out(early, 0).T)
        b_ffn = scaled(
            jnp.stack(
                [units_out(early, parts * SPAN), units_out(early, 2 * parts * SPAN)]
            )
        )
    middle_pieces = gather_relative(middle_sums, "seq", [a_down])
    middle = settle(middle_pieces)
    b_kv = middle[:, 6 * SPAN :, : 2 * kv_width].reshape(seqs, SPAN, 2, kv_width)
    a_all, b_model = finish_model(middle, factor)
    late = settle(gather_relative(late_sums, "seq", [b_model]))
    return (
        layer_out[None],
        grad_input[None],
        finish_late(late, a_all, factor),
        a_down,
        b_model,
        scaled(b_kv.transpose(2, 1, 0, 3).reshape(2, SPAN, KV_HEADS * HEAD_DIM)),
        b_ffn,
    )


def solution(mesh):
    rows = P("fsdp", None)
    placed = (
        (P("fsdp", "seq", None),) * 2 + (rows,) * 2 + (P(),) * 2 + (rows,) * 7 + (P(),) * 5
    )
    return jax.shard_map(
        shards,
        mesh=mesh,
        in_specs=placed,
        out_specs=(P("fsdp", "seq", None), P("fsdp", "seq", None), P(), P(), P(), P(), P()),
        check_vma=False,
    )
```

```python
import math

import jax
import jax.numpy as jnp
from jax import lax
from jax.experimental import pallas as pl
from jax.experimental.pallas import tpu as pltpu
from jax.sharding import PartitionSpec as P

MODEL_WIDTH = 2048
HEADS = 32
KV_HEADS = 8
HEAD_DIM = 64
ADAPTER_RANK = 16
ADAPTER_TOTAL = 8
PACK = 1024
QBLOCK = 256
SPAN = ADAPTER_TOTAL * ADAPTER_RANK
GROUP = HEADS // KV_HEADS

SCORE_SCALE = 0.015625
RESIDUAL_FACTOR = 0.22
NORM_EPSILON = 1e-05
ROPE_BASE = 10000000.0
MASK_FILL = 1e30

BF16 = jnp.bfloat16
F32 = jnp.float32


def mm(left, right):
    return jnp.dot(left, right, preferred_element_type=F32)


def mm_nt(left, right):
    return lax.dot_general(left, right, (((1,), (1,)), ((), ())), preferred_element_type=F32)


def mm_tn(left, right):
    return lax.dot_general(left, right, (((0,), (0,)), ((), ())), preferred_element_type=F32)


def rms_norm(hidden, gain_vec):
    mean_square = jnp.mean(hidden * hidden, axis=-1, keepdims=True)
    return hidden * lax.rsqrt(mean_square + NORM_EPSILON) * gain_vec


def pack_tables(seq_lengths, adapter_id, token_count, adapter_count):
    slots = seq_lengths.shape[0]
    places = jnp.arange(token_count, dtype=jnp.int32)
    seq_ends = jnp.cumsum(seq_lengths)
    seq_starts = seq_ends - seq_lengths
    used_len = seq_ends[slots - 1]
    segment = jnp.sum((places[:, None] >= seq_ends[None, :]).astype(jnp.int32), axis=1)
    member = segment[:, None] == jnp.arange(slots, dtype=jnp.int32)[None, :]
    start_tok = jnp.sum(jnp.where(member, seq_starts[None, :], 0), axis=1) + jnp.where(
        segment == slots, used_len, 0
    )
    position = places - start_tok
    valid_row = segment < slots
    chosen = adapter_id[:, None] == jnp.arange(adapter_count, dtype=jnp.int32)[None, :]
    onehot = jnp.sum(jnp.where(member[:, :, None] & chosen[None, :, :], 1.0, 0.0), axis=1).astype(F32)
    return (segment, position, valid_row, onehot)


def rope_tables(position, head_size, copies):
    frequency = ROPE_BASE ** (-(jnp.arange(head_size // 2, dtype=F32) * 2.0) / head_size)
    angles = position.astype(F32)[:, None] * frequency[None, :]
    cosine, sine = jnp.cos(angles), jnp.sin(angles)
    return (jnp.tile(cosine, (1, 2 * copies)), jnp.tile(sine, (1, 2 * copies)))


def bits_down(count):
    bits, bit = [], count >> 1
    while bit:
        bits.append(bit)
        bit >>= 1
    return bits


def relative_order(count):
    order = [0]
    for bit in bits_down(count):
        order = order + [o ^ bit for o in order]
    return order


def swap(block, axis, offset):
    count = lax.axis_size(axis)
    return lax.ppermute(block, axis, [(i, i ^ offset) for i in range(count)])


def gather_relative(block, axis, last=()):
    pieces = [block]
    for bit in bits_down(lax.axis_size(axis)):
        if bit == 1:
            pieces[-1] = after(pieces[-1], *last)
        pieces = pieces + [swap(piece, axis, bit) for piece in pieces]
    return pieces


def reduce_relative(pieces, axis, last=()):
    for bit in reversed(bits_down(lax.axis_size(axis))):
        half = len(pieces) // 2
        given = [piece.astype(BF16) for piece in pieces[half:]]
        if half == 1:
            given = [after(given[0], *last)]
        got = [swap(piece, axis, bit) for piece in given]
        pieces = [mine.astype(F32) + other.astype(F32) for mine, other in zip(pieces[:half], got)]
    return pieces[0]


def reduce_halves(keep, give, axis):
    bits = list(reversed(bits_down(lax.axis_size(axis))))
    for bit in bits:
        got = swap(give, axis, bit)
        total = keep.astype(F32) + got.astype(F32)
        half = total.shape[0] // 2
        keep, give = total[:half], total[half:].astype(BF16)
    return total


def cycle_of(count):
    return list(range(0, count, 2)) + list(range(count - 1, 0, -2))


class Rings:
    WINDOW = 4

    def __init__(self):
        self.count = lax.axis_size("fsdp")
        cycle = cycle_of(self.count)
        place = {device: k for k, device in enumerate(cycle)}
        table = [
            [cycle[(place[device] - k) % self.count] for k in range(self.count)]
            for device in range(self.count)
        ]
        self.owner = lax.dynamic_index_in_dim(
            jnp.array(table, jnp.int32), lax.axis_index("fsdp"), 0, keepdims=False
        )
        ahead = [(cycle[k], cycle[(k + 1) % self.count]) for k in range(self.count)]
        self.perms = (ahead, [(b, a) for a, b in ahead])
        self.sent = ([], [])

    def send(self, way, block):
        sent = self.sent[way]
        if len(sent) >= self.WINDOW:
            block, _ = lax.optimization_barrier((block, sent[-self.WINDOW]))
        got = lax.ppermute(block, "fsdp", self.perms[way])
        sent.append(got)
        return got

    def gather(self, blocks, starts):
        half = self.count // 2
        found = [{0: block} for block in blocks]
        latest = [[block, block] for block in blocks]
        for time in range(1, half + max(starts) + 1):
            for which in range(len(blocks)):
                step = time - starts[which]
                if not 1 <= step <= half:
                    continue
                for way in (0, 1):
                    if step == half and way != which % 2:
                        continue
                    got = self.send(way, latest[which][way])
                    latest[which][way] = got
                    found[which][step if way == 0 else self.count - step] = got
        return [[f[k] for k in range(self.count)] for f in found]


def place_blocks(pieces, counts, targets):
    rows = pieces[0].shape[0] // counts
    columns = pieces[0].shape[1]
    total = len(pieces) * counts

    def body(target_ref, *refs):
        out_ref, held, came, left = refs[-4:]
        arrivals, departures = [], []
        for i in range(len(pieces)):
            for j in range(counts):
                k = i * counts + j
                first = pl.multiple_of(target_ref[k] * rows, rows)
                arrivals.append(
                    pltpu.make_async_copy(
                        refs[i].at[pl.ds(j * rows, rows), :], held.at[k], came.at[k]
                    )
                )
                departures.append(
                    pltpu.make_async_copy(
                        held.at[k], out_ref.at[pl.ds(first, rows), :], left.at[k]
                    )
                )
        for copy in arrivals:
            copy.start()
        for arrival, departure in zip(arrivals, departures):
            arrival.wait()
            departure.start()
        for copy in departures:
            copy.wait()

    return pl.pallas_call(
        body,
        out_shape=jax.ShapeDtypeStruct((rows * total, columns), pieces[0].dtype),
        grid_spec=pltpu.PrefetchScalarGridSpec(
            num_scalar_prefetch=1,
            grid=(),
            in_specs=[pl.BlockSpec(memory_space=pl.ANY)] * len(pieces),
            out_specs=pl.BlockSpec(memory_space=pl.ANY),
            scratch_shapes=[
                pltpu.VMEM((total, rows, columns), pieces[0].dtype),
                pltpu.SemaphoreType.DMA((total,)),
                pltpu.SemaphoreType.DMA((total,)),
            ],
        ),
        cost_estimate=pl.CostEstimate(
            flops=0, transcendentals=0, bytes_accessed=4 * rows * total * columns
        ),
        name="place_blocks",
    )(targets.astype(jnp.int32), *pieces)


def after(value, *others):
    return lax.optimization_barrier((value, others))[0]


def take_units(matrices, peer, seqs, runs, unit_block):
    if unit_block % 128:
        return [
            lax.dynamic_index_in_dim(
                m.reshape(m.shape[0], runs, seqs, unit_block), peer, 2, keepdims=False
            ).reshape(m.shape[0], runs * unit_block)
            for m in matrices
        ]

    def body(peer_ref, *refs):
        for source, target in zip(refs[: len(matrices)], refs[len(matrices) :]):
            target[...] = source[...]

    return pl.pallas_call(
        body,
        grid_spec=pltpu.PrefetchScalarGridSpec(
            num_scalar_prefetch=1,
            grid=(runs,),
            in_specs=[
                pl.BlockSpec((m.shape[0], unit_block), lambda f, at: (0, f * seqs + at[0]))
                for m in matrices
            ],
            out_specs=[
                pl.BlockSpec((m.shape[0], unit_block), lambda f, at: (0, f)) for m in matrices
            ],
        ),
        out_shape=[
            jax.ShapeDtypeStruct((m.shape[0], runs * unit_block), m.dtype) for m in matrices
        ],
        name="take_units",
    )(peer.astype(jnp.int32)[None], *matrices)


def finish_units(whole, first, parts, runs, unit_block, factor):
    seqs, _, columns = whole.shape
    feed_units = seqs * runs * unit_block
    per = runs // parts

    def body(down_ref, gate_ref, up_ref, a_ref, b_ref):
        for s in range(seqs):
            here = slice(s * unit_block, (s + 1) * unit_block)
            a_ref[here, :] = down_ref[s].astype(F32).T * factor
            b_ref[0, :, here] = gate_ref[s].astype(F32) * factor
            b_ref[1, :, here] = up_ref[s].astype(F32) * factor

    def part(which):
        base = first // SPAN + which * parts
        return pl.BlockSpec((seqs, SPAN, unit_block), lambda k, g: (0, base + k, g))

    return pl.pallas_call(
        body,
        grid=(parts, per),
        in_specs=[part(0), part(1), part(2)],
        out_specs=[
            pl.BlockSpec((seqs * unit_block, SPAN), lambda k, g: (k * per + g, 0)),
            pl.BlockSpec((2, SPAN, seqs * unit_block), lambda k, g: (0, 0, k * per + g)),
        ],
        out_shape=[
            jax.ShapeDtypeStruct((feed_units, SPAN), F32),
            jax.ShapeDtypeStruct((2, SPAN, feed_units), F32),
        ],
        name="finish_units",
    )(whole, whole, whole)


def finish_model(whole, factor):
    seqs, _, columns = whole.shape

    def body(shared_ref, heads_ref, a_ref, b_ref):
        def rows(k):
            return shared_ref[0, k * SPAN : (k + 1) * SPAN].astype(F32) * factor

        a_ref[0] = rows(3).T
        a_ref[1] = rows(0).T
        a_ref[2] = rows(1).T
        b_ref[0] = heads_ref[0].astype(F32) * factor
        b_ref[1] = rows(4)
        b_ref[2] = rows(2)

    return pl.pallas_call(
        body,
        grid=(seqs,),
        in_specs=[
            pl.BlockSpec((1, 5 * SPAN, columns), lambda s: (s, 0, 0)),
            pl.BlockSpec((1, SPAN, columns), lambda s: (s, 5, 0)),
        ],
        out_specs=[
            pl.BlockSpec((3, columns, SPAN), lambda s: (1, s, 0)),
            pl.BlockSpec((3, SPAN, columns), lambda s: (0, 0, s)),
        ],
        out_shape=[
            jax.ShapeDtypeStruct((6, MODEL_WIDTH, SPAN), F32),
            jax.ShapeDtypeStruct((3, SPAN, MODEL_WIDTH), F32),
        ],
        name="finish_model",
    )(whole, whole)


def finish_late(late, a_all, factor):
    seqs, _, columns = late.shape

    def body(late_ref, held_ref, a_ref):
        for j in range(3):
            a_ref[j] = late_ref[0, j * SPAN : (j + 1) * SPAN].astype(F32).T * factor

    return pl.pallas_call(
        body,
        grid=(seqs,),
        in_specs=[
            pl.BlockSpec((1, 3 * SPAN, columns), lambda s: (s, 0, 0)),
            pl.BlockSpec(memory_space=pl.ANY),
        ],
        out_specs=pl.BlockSpec((3, columns, SPAN), lambda s: (0, s, 0)),
        out_shape=jax.ShapeDtypeStruct(a_all.shape, F32),
        input_output_aliases={1: 0},
        name="finish_late",
    )(late, a_all)


def half_lanes(shape):
    lane = lax.broadcasted_iota(jnp.int32, shape, 1)
    return lane % HEAD_DIM < HEAD_DIM // 2


def turn_tile(x, cosine, sine):
    quarter = HEAD_DIM // 2
    ahead = pltpu.roll(x, 2 * HEAD_DIM - quarter, 1)
    behind = pltpu.roll(x, quarter, 1)
    return x * cosine + jnp.where(half_lanes(x.shape), -ahead, behind) * sine


def dot_tn(left, right):
    return lax.dot_general(left, right, (((0,), (0,)), ((), ())), preferred_element_type=F32)


def dot_nt(left, right):
    return lax.dot_general(left, right, (((1,), (1,)), ((), ())), preferred_element_type=F32)


def allowed_pairs(seg_col, seg_row, block):
    keys = (block + 1) * QBLOCK
    shape = (keys, QBLOCK)
    key_at = lax.broadcasted_iota(jnp.int32, shape, 0)
    query_at = lax.broadcasted_iota(jnp.int32, shape, 1) + block * QBLOCK
    same = seg_col[:keys, :] == seg_row[:, block * QBLOCK : keys]
    return same & (key_at <= query_at)


def forward_body(
    blocks, slot_ref, q_ref, k_ref, v_ref, cos_ref, sin_ref, col_ref, row_ref,
    qn_ref, kn_ref, vn_ref, out_ref, lse_ref,
):
    for j in range(blocks):
        here = slice(j * QBLOCK, (j + 1) * QBLOCK)
        there = pl.ds(pl.multiple_of(slot_ref[j] * QBLOCK, QBLOCK), QBLOCK)
        cosine, sine = cos_ref[here, :], sin_ref[here, :]
        qn_ref[here, :] = turn_tile(q_ref[there, :], cosine, sine).astype(BF16)
        kn_ref[here, :] = turn_tile(k_ref[there, :], cosine, sine).astype(BF16)
        vn_ref[here, :] = v_ref[there, :].astype(BF16)
    lane = lax.broadcasted_iota(jnp.int32, (QBLOCK, 2 * HEAD_DIM), 1)
    row = lax.broadcasted_iota(jnp.int32, (2 * HEAD_DIM, QBLOCK), 0)
    for i in range(blocks):
        here = slice(i * QBLOCK, (i + 1) * QBLOCK)
        keys = (i + 1) * QBLOCK
        allowed = allowed_pairs(col_ref[...], row_ref[...], i)
        query = (qn_ref[here, :].astype(F32) * SCORE_SCALE).astype(BF16)
        outs = []
        for e in range(2):
            mine = jnp.where(lane // HEAD_DIM == e, query, jnp.zeros_like(query))
            scores = jnp.where(allowed, dot_nt(kn_ref[:keys, :], mine), -MASK_FILL)
            most = jnp.max(scores, axis=0, keepdims=True)
            exponent = jnp.exp(scores - most)
            total = jnp.sum(exponent, axis=0, keepdims=True)
            probs = (exponent * (1.0 / total)).astype(BF16)
            lse_ref[0, e : e + 1, here] = most + jnp.log(total)
            outs.append(dot_tn(vn_ref[:keys, :], probs))
        out = jnp.where(row < HEAD_DIM, outs[0], outs[1]).T
        there = pl.ds(pl.multiple_of(slot_ref[i] * QBLOCK, QBLOCK), QBLOCK)
        out_ref[there, :] = out.astype(BF16)


def backward_body(
    blocks, groups, slot_ref, qn_ref, kn_ref, vn_ref, do_ref, lse_ref, cos_ref, sin_ref, col_ref,
    row_ref, out_ref, dk_sum, dv_sum,
):
    pairs_per_group = GROUP // 2
    pair = pl.program_id(0)
    step = lax.rem(pair, pairs_per_group)
    two = 2 * HEAD_DIM

    @pl.when(step == 0)
    def _():
        dk_sum[...] = jnp.zeros_like(dk_sum)
        dv_sum[...] = jnp.zeros_like(dv_sum)

    lane = lax.broadcasted_iota(jnp.int32, (QBLOCK, two), 1)
    row = lax.broadcasted_iota(jnp.int32, (two, QBLOCK), 0)

    def place(j):
        return pl.ds(pl.multiple_of(slot_ref[j] * QBLOCK, QBLOCK), QBLOCK)

    for i in range(blocks):
        here = slice(i * QBLOCK, (i + 1) * QBLOCK)
        keys = (i + 1) * QBLOCK
        allowed = allowed_pairs(col_ref[...], row_ref[...], i)
        query = (qn_ref[here, :].astype(F32) * SCORE_SCALE).astype(BF16)
        grad = do_ref[place(i), :]
        outs = []
        for e in range(2):
            mine = jnp.where(lane // HEAD_DIM == e, query, jnp.zeros_like(query))
            grad_mine = jnp.where(lane // HEAD_DIM == e, grad, jnp.zeros_like(grad))
            scores = jnp.where(allowed, dot_nt(kn_ref[:keys, :], mine), -MASK_FILL)
            probs = jnp.exp(scores - lse_ref[0, e : e + 1, here])
            grad_probs = dot_nt(vn_ref[:keys, :], grad_mine)
            delta = jnp.sum(probs * grad_probs, axis=0, keepdims=True)
            grad_scores = (probs * (grad_probs - delta)).astype(BF16)
            dv_sum[:keys, :] += jnp.dot(probs.astype(BF16), grad_mine, preferred_element_type=F32)
            dk_sum[:keys, :] += jnp.dot(grad_scores, mine, preferred_element_type=F32)
            outs.append(dot_tn(kn_ref[:keys, :], grad_scores))
        out = jnp.where(row < HEAD_DIM, outs[0], outs[1]).T * SCORE_SCALE
        out = out.astype(BF16).astype(F32)
        out_ref[place(i), pl.ds(pl.multiple_of(pair * two, two), two)] = turn_tile(
            out, cos_ref[here, :], -sin_ref[here, :]
        ).astype(BF16)

    width = groups * GROUP * HEAD_DIM
    for g in range(groups):

        @pl.when(pair == (g + 1) * pairs_per_group - 1)
        def _(g=g):
            for j in range(blocks):
                here = slice(j * QBLOCK, (j + 1) * QBLOCK)
                dk = dk_sum[here, :]
                dk = (dk + pltpu.roll(dk, HEAD_DIM, 1)).astype(BF16).astype(F32)
                dk = turn_tile(dk, cos_ref[here, :], -sin_ref[here, :]).astype(BF16)
                dv = dv_sum[here, :]
                dv = (dv + pltpu.roll(dv, HEAD_DIM, 1)).astype(BF16)
                for base, values in ((width, dk), (width + groups * HEAD_DIM, dv)):
                    first = base + g * HEAD_DIM
                    tile = slice(first // two * two, first // two * two + two)
                    half = first // HEAD_DIM % 2
                    old = out_ref[place(j), tile]
                    out_ref[place(j), tile] = jnp.where(lane // HEAD_DIM == half, values, old)


def attention_specs():
    tile = pl.BlockSpec((PACK, 2 * HEAD_DIM), lambda p, slot: (0, p))
    group = pl.BlockSpec((PACK, 2 * HEAD_DIM), lambda p, slot: (0, p // (GROUP // 2)))
    lse = pl.BlockSpec((1, 2, PACK), lambda p, slot: (p, 0, 0))
    table = pl.BlockSpec((PACK, 2 * HEAD_DIM), lambda p, slot: (0, 0))
    col = pl.BlockSpec((PACK, 1), lambda p, slot: (0, 0))
    row = pl.BlockSpec((1, PACK), lambda p, slot: (0, 0))
    return tile, group, lse, [table, table, col, row]


def attend_forward(slots, query, key, value, tables):
    pairs = query.shape[1] // (2 * HEAD_DIM)
    groups = key.shape[1] // (2 * HEAD_DIM)
    tile, group, lse, rest = attention_specs()
    blocks = PACK // QBLOCK
    return pl.pallas_call(
        lambda *refs: forward_body(blocks, *refs),
        grid_spec=pltpu.PrefetchScalarGridSpec(
            num_scalar_prefetch=1,
            grid=(pairs,),
            in_specs=[tile, group, group] + rest,
            out_specs=[tile, group, group, tile, lse],
        ),
        out_shape=[
            jax.ShapeDtypeStruct((PACK, pairs * 2 * HEAD_DIM), BF16),
            jax.ShapeDtypeStruct((PACK, groups * 2 * HEAD_DIM), BF16),
            jax.ShapeDtypeStruct((PACK, groups * 2 * HEAD_DIM), BF16),
            jax.ShapeDtypeStruct((PACK, pairs * 2 * HEAD_DIM), BF16),
            jax.ShapeDtypeStruct((pairs, 2, PACK), F32),
        ],
        cost_estimate=pl.CostEstimate(
            flops=4 * pairs * 2 * PACK * PACK * HEAD_DIM,
            transcendentals=pairs * PACK * PACK,
            bytes_accessed=8 * PACK * MODEL_WIDTH,
        ),
        name="attend_forward",
    )(slots, query, key, value, *tables)


def attend_backward(slots, saved, grad, log_totals, tables):
    query, key, value = saved
    pairs = query.shape[1] // (2 * HEAD_DIM)
    groups = key.shape[1] // (2 * HEAD_DIM)
    tile, group, lse, rest = attention_specs()
    blocks = PACK // QBLOCK
    columns = pairs * 2 * HEAD_DIM + groups * 2 * HEAD_DIM
    return pl.pallas_call(
        lambda *refs: backward_body(blocks, groups, *refs),
        grid_spec=pltpu.PrefetchScalarGridSpec(
            num_scalar_prefetch=1,
            grid=(pairs,),
            in_specs=[tile, group, group, tile, lse] + rest,
            out_specs=pl.BlockSpec((PACK, columns), lambda p, slot: (0, 0)),
            scratch_shapes=[pltpu.VMEM((PACK, 2 * HEAD_DIM), F32)] * 2,
        ),
        out_shape=jax.ShapeDtypeStruct((PACK, columns), BF16),
        cost_estimate=pl.CostEstimate(flops=0, transcendentals=0, bytes_accessed=0),
        name="attend_backward",
    )(slots, query, key, value, grad, log_totals, *tables)


def tile_of(count):
    return 256 if count % 256 == 0 else 128


def gate_grads(grad_down, down, grad_low, first_down, gate, up):
    tokens, units = gate.shape
    tile = tile_of(units)

    def body(gd_ref, down_ref, gl_ref, fd_ref, gate_ref, up_ref, gg_ref, gu_ref):
        grad_act = dot_nt(gd_ref[...], down_ref[...]) + dot_nt(gl_ref[...], fd_ref[...])
        gate_here = gate_ref[...]
        share = jax.nn.sigmoid(gate_here)
        gu_ref[...] = (grad_act * share * gate_here).astype(BF16)
        gg_ref[...] = (
            grad_act * up_ref[...] * share * (1.0 + gate_here * (1.0 - share))
        ).astype(BF16)

    def whole(array):
        return pl.BlockSpec(array.shape, lambda t: (0, 0))

    def rows(array):
        return pl.BlockSpec((tile, array.shape[1]), lambda t: (t, 0))

    cols = pl.BlockSpec((tokens, tile), lambda t: (0, t))
    return pl.pallas_call(
        body,
        grid=(units // tile,),
        in_specs=[whole(grad_down), rows(down), whole(grad_low), rows(first_down), cols, cols],
        out_specs=[cols, cols],
        out_shape=[jax.ShapeDtypeStruct((tokens, units), BF16)] * 2,
        cost_estimate=pl.CostEstimate(
            flops=2 * tokens * units * MODEL_WIDTH,
            transcendentals=tokens * units,
            bytes_accessed=12 * tokens * units + 2 * units * MODEL_WIDTH,
        ),
        name="gate_grads",
    )(grad_down, down, grad_low, first_down, gate, up)


def sum_products(lefts, rights):
    tokens, outs = lefts[0].shape[0], rights[0].shape[0]
    tile = tile_of(outs)
    count = len(lefts)

    def body(*refs):
        total = dot_nt(refs[0][...], refs[count][...])
        for k in range(1, count):
            total = total + dot_nt(refs[k][...], refs[count + k][...])
        refs[-2][...] = total[: tokens // 2].astype(BF16)
        refs[-1][...] = total[tokens // 2 :].astype(BF16)

    half = pl.BlockSpec((tokens // 2, tile), lambda t: (0, t))
    return pl.pallas_call(
        body,
        grid=(outs // tile,),
        in_specs=[pl.BlockSpec(a.shape, lambda t: (0, 0)) for a in lefts]
        + [pl.BlockSpec((tile, b.shape[1]), lambda t: (t, 0)) for b in rights],
        out_specs=[half, half],
        out_shape=[jax.ShapeDtypeStruct((tokens // 2, outs), BF16)] * 2,
        cost_estimate=pl.CostEstimate(
            flops=sum(2 * tokens * outs * a.shape[1] for a in lefts),
            transcendentals=0,
            bytes_accessed=2 * sum(a.size for a in [*lefts, *rights]) + 2 * tokens * outs,
        ),
        name="sum_products",
    )(*lefts, *rights)


def reverse_bits(value, count):
    out, bit, other = 0, 1, count >> 1
    while other:
        out = out + jnp.where((value & bit) != 0, other, 0)
        bit, other = bit << 1, other >> 1
    return out


def pairs_of(bits):
    return [bits[k : k + 2] for k in range(0, len(bits), 2)]


def scatter_step(total, *bits):
    me = lax.axis_index("fsdp")
    rows = total.shape[0] >> len(bits)
    offsets = [0]
    for bit in bits:
        offsets = offsets + [o ^ bit for o in offsets]

    def run_of(device):
        number = 0
        for bit in bits:
            number = 2 * number + ((device & bit) != 0).astype(jnp.int32)
        return lax.dynamic_slice_in_dim(total, number * rows, rows, 0)

    kept = run_of(me).astype(F32)
    for got in [swap(run_of(me ^ o), "fsdp", o) for o in offsets[1:]]:
        kept = kept + got.astype(F32)
    return kept.astype(BF16)


def reduce_scatter_rows(total):
    first, *rest = reversed(bits_down(lax.axis_size("fsdp")))
    total = scatter_step(total, first)
    for bits in pairs_of(rest):
        total = scatter_step(total, *bits)
    return total


def widen(piece, *bits):
    pieces, sent = [piece], [0]
    for bit in bits:
        sent = sent + [o ^ bit for o in sent]
    return jnp.concatenate(pieces + [swap(piece, "fsdp", o) for o in sent[1:]], axis=0)


def share_out(piece):
    for bits in pairs_of(bits_down(lax.axis_size("fsdp"))):
        piece = widen(piece, *bits)
    return piece


def settle(pieces):
    count, seqs = lax.axis_size("fsdp"), lax.axis_size("seq")
    me, me_seq = lax.axis_index("fsdp"), lax.axis_index("seq")
    rows, columns = pieces[0].shape
    targets = jnp.stack(
        [
            (me_seq ^ s) * count + reverse_bits(me ^ o, count)
            for s in relative_order(seqs)
            for o in relative_order(count)
        ]
    )
    return place_blocks(pieces, count, targets).reshape(seqs, rows, columns)


def shards(
    tokens,
    cotangent,
    lengths,
    sequence_adapter,
    attention_norm_gain,
    feedfwd_norm_gain,
    query_matrix,
    key_matrix,
    value_matrix,
    output_matrix,
    gate_matrix,
    up_matrix,
    down_matrix,
    adapter_first_factors,
    adapter_first_down,
    adapter_second_model,
    adapter_second_keyvalue,
    adapter_second_feedfwd,
):
    seqs, fsdps = lax.axis_size("seq"), lax.axis_size("fsdp")
    me = lax.axis_index("seq")
    order = relative_order(seqs)
    peers = [me ^ o for o in order]
    resid_in = tokens[0]
    row_count = resid_in.shape[0]
    width = MODEL_WIDTH // seqs
    kv_width = KV_HEADS * HEAD_DIM // seqs
    my_groups = KV_HEADS // seqs
    feed_units = gate_matrix.shape[1]
    unit_block = feed_units // (seqs * fsdps)
    units = feed_units // seqs
    parts = units // width

    def columns_of(array, peer, count):
        return lax.dynamic_slice_in_dim(array, peer * count, count, array.ndim - 1)

    def rows_of(array, peer):
        return lax.dynamic_slice_in_dim(array, peer * row_count, row_count, 0)

    def relative_rows(array):
        return jnp.concatenate([rows_of(array, peer) for peer in peers], axis=0)

    def blocks_of(array):
        return [array[k * row_count : (k + 1) * row_count] for k in range(seqs)]

    def exchange(pieces):
        return [p if o == 0 else swap(p, "seq", o) for o, p in zip(order, pieces)]

    def place_columns(pieces):
        rows, count = pieces[0].shape
        whole = jnp.zeros((rows, count * seqs), pieces[0].dtype)
        for peer, piece in zip(peers, pieces):
            whole = lax.dynamic_update_slice(whole, piece, (0, peer * count))
        return whole

    rings = Rings()
    qkv_share = jnp.concatenate(
        [
            columns_of(query_matrix, me, width),
            columns_of(key_matrix, me, kv_width),
            columns_of(value_matrix, me, kv_width),
        ],
        axis=1,
    )
    gate_share, up_share = take_units([gate_matrix, up_matrix], me, seqs, fsdps, unit_block)
    out_share = columns_of(output_matrix, me, width)
    down_share = lax.dynamic_slice_in_dim(down_matrix, me * unit_block, unit_block, 0)
    half_block = unit_block // 2
    lists = rings.gather(
        [
            qkv_share,
            out_share,
            gate_share,
            up_share,
            down_share[:half_block],
            down_share[half_block:],
        ],
        [0, 0, 2, 3, 5, 6],
    )
    qkv_mine, out_mine, gate_full, up_full = (
        place_blocks(blocks, 1, rings.owner) for blocks in lists[:4]
    )

    segment, position, valid_row, onehot = pack_tables(
        lengths[0], sequence_adapter[0], PACK, ADAPTER_TOTAL
    )
    valid_all = jnp.where(valid_row, 1.0, 0.0).astype(F32)[:, None]
    mask_all = jnp.repeat(onehot, ADAPTER_RANK, axis=1).astype(BF16)
    valid_rel = relative_rows(valid_all)
    mask_rel = relative_rows(mask_all)
    valid_col, mask_own = valid_rel[:row_count], mask_rel[:row_count]
    mask_own_three = jnp.tile(mask_own, (1, 3))
    mask_rel_two = jnp.tile(mask_rel, (1, 2))
    mask_rel_three = jnp.tile(mask_rel, (1, 3))
    cosine, sine = rope_tables(position, HEAD_DIM, 2)
    tables = (cosine, sine, segment[:, None], segment[None, :])
    slot_of = [0] * seqs
    for k, o in enumerate(order):
        slot_of[o] = k
    slot_table = jnp.array(slot_of, jnp.int32)
    sub = row_count // QBLOCK if row_count >= QBLOCK else 1
    if row_count >= QBLOCK:
        slots = jnp.stack(
            [
                slot_table[me ^ (j // sub)] * sub + j % sub
                for j in range(PACK // QBLOCK)
            ]
        )
    else:
        slots = jnp.arange(PACK // QBLOCK, dtype=jnp.int32)

    def to_kernel(array):
        if row_count >= QBLOCK:
            return array
        whole = jnp.zeros_like(array)
        for peer, piece in zip(peers, blocks_of(array)):
            whole = lax.dynamic_update_slice(whole, piece, (peer * row_count, 0))
        return whole

    def from_kernel(array):
        return array if row_count >= QBLOCK else relative_rows(array)

    hidden_in = resid_in.astype(F32)
    normed_own = rms_norm(hidden_in, attention_norm_gain).astype(BF16)
    normed_one = jnp.concatenate(gather_relative(normed_own, "seq"), axis=0)
    first_qkv = jnp.concatenate([adapter_first_factors[k] for k in range(3)], axis=1)
    low_qkv = (mm(normed_one, first_qkv) * mask_rel_three).astype(BF16)
    low_q, low_k, low_v = (low_qkv[:, k * SPAN : (k + 1) * SPAN] for k in range(3))
    second_q = [columns_of(adapter_second_model[0], me, width)]
    second_k = [columns_of(adapter_second_keyvalue[0], me, kv_width)]
    second_v = [columns_of(adapter_second_keyvalue[1], me, kv_width)]

    def twice(rows):
        heads = [rows[:, g * HEAD_DIM : (g + 1) * HEAD_DIM] for g in range(my_groups)]
        return jnp.concatenate([h for h in heads for _ in (0, 1)], axis=1)

    projected = mm(normed_one, qkv_mine)
    query = projected[:, :width] + mm(low_q, second_q[0])
    key = projected[:, width : width + kv_width] + mm(low_k, second_k[0])
    value = projected[:, width + kv_width :] + mm(low_v, second_v[0])
    *saved, attn_heads, log_totals = attend_forward(
        slots, to_kernel(query), to_kernel(twice(key)), to_kernel(twice(value)), tables
    )
    attn_heads = from_kernel(attn_heads)
    attn_own = place_columns(exchange(blocks_of(attn_heads)))
    out_weights = gather_relative(out_mine, "seq")
    low_o = (mm(attn_own, adapter_first_factors[3]) * mask_own).astype(BF16)
    branch = place_columns([mm(attn_own, piece) for piece in out_weights]) + mm(
        low_o, adapter_second_model[1]
    )
    hidden_mid = hidden_in + RESIDUAL_FACTOR * branch
    normed_two_own = rms_norm(hidden_mid, feedfwd_norm_gain).astype(BF16)

    normed_two = jnp.concatenate(gather_relative(normed_two_own, "seq"), axis=0)
    cot_all = jnp.concatenate(gather_relative(cotangent[0], "seq"), axis=0)
    first_ffn = jnp.concatenate([adapter_first_factors[4], adapter_first_factors[5]], axis=1)
    low_ffn = (mm(normed_two, first_ffn) * mask_rel_two).astype(BF16)
    low_g, low_u = low_ffn[:, :SPAN], low_ffn[:, SPAN:]
    (second_ffn,) = take_units(
        [adapter_second_feedfwd.reshape(2 * SPAN, feed_units)], me, seqs, fsdps, unit_block
    )
    second_gate, second_up = second_ffn[:SPAN], second_ffn[SPAN:]
    gate = mm(normed_two, gate_full) + mm(low_g, second_gate)
    up = mm(normed_two, up_full) + mm(low_u, second_up)

    def swiglu(gate_arg, up_arg):
        return jax.nn.sigmoid(gate_arg) * gate_arg * up_arg

    act = swiglu(gate, up).astype(BF16)
    down_full = place_blocks(
        lists[4] + lists[5], 1, jnp.concatenate([rings.owner * 2, rings.owner * 2 + 1])
    )
    first_down = lax.dynamic_index_in_dim(
        adapter_first_down.reshape(fsdps, seqs, unit_block, SPAN), me, 1, keepdims=False
    ).reshape(units, SPAN)
    grad_out = cotangent[0].astype(F32) * valid_col
    grad_down = (RESIDUAL_FACTOR * (cot_all.astype(F32) * valid_rel)).astype(BF16)
    grad_low_d = mm_nt(grad_down, adapter_second_model[2]).astype(BF16) * mask_rel
    grad_gate, grad_up = gate_grads(grad_down, down_full, grad_low_d, first_down, gate, up)
    grad_low_ffn = (
        jnp.concatenate([mm_nt(grad_gate, second_gate), mm_nt(grad_up, second_up)], axis=1).astype(
            BF16
        )
        * mask_rel_two
    )
    keep, give = sum_products(
        [grad_gate, grad_up, grad_low_ffn], [gate_full, up_full, first_ffn]
    )
    act, late_gate, late_up = after((act, grad_gate, grad_up), give)
    grad_normed_two = reduce_halves(keep, give, "seq")
    grad_a_down = mm_tn(grad_low_d, act)
    grad_b_gate = mm_tn(low_g, late_gate)
    grad_b_up = mm_tn(low_u, late_up)

    def split_units(rows):
        return [rows[:, k * width : (k + 1) * width].astype(BF16) for k in range(parts)]

    unit_grads = jnp.concatenate(
        split_units(grad_a_down) + split_units(grad_b_gate) + split_units(grad_b_up), axis=0
    )
    act = after(act, unit_grads)
    unit_bits = list(reversed(bits_down(fsdps)))
    unit_sums = scatter_step(unit_grads, unit_bits[0])
    grad_normed_two, unit_sums = after((grad_normed_two, unit_sums))
    unit_sums = scatter_step(unit_sums, unit_bits[1])
    low_d = (mm(act, first_down) * mask_rel).astype(BF16)
    down_part = mm(act, down_full) + mm(low_d, adapter_second_model[2])
    grad_b_down = mm_tn(low_d, grad_down)
    grad_a_ffn = mm_tn(grad_low_ffn, normed_two)
    _, norm_two_back = jax.vjp(lambda hidden: rms_norm(hidden, feedfwd_norm_gain), hidden_mid)
    grad_mid = grad_out + norm_two_back(grad_normed_two)[0]

    grad_branch = (RESIDUAL_FACTOR * grad_mid).astype(BF16)
    grad_low_o = mm_nt(grad_branch, adapter_second_model[1]).astype(BF16) * mask_own
    grad_b_out = mm_tn(low_o, grad_branch)
    grad_a_out = mm_tn(grad_low_o, attn_own)
    grad_attn = mm_nt(grad_low_o, adapter_first_factors[3]) + mm_nt(
        jnp.concatenate([columns_of(grad_branch, peer, width) for peer in peers], axis=1),
        jnp.concatenate(out_weights, axis=1),
    )
    grad_attn = grad_attn.astype(BF16)
    grad_heads = jnp.concatenate(
        exchange([columns_of(grad_attn, peer, width) for peer in peers]), axis=0
    )
    grad_heads, unit_sums = after((grad_heads, unit_sums))
    for bit in unit_bits[2:]:
        unit_sums = scatter_step(unit_sums, bit)
    down_sum = reduce_relative(blocks_of(down_part), "seq", [grad_heads])
    shared_terms = jnp.concatenate([grad_a_ffn, grad_b_down, grad_a_out, grad_b_out], axis=0)
    shared_sum = reduce_relative(
        [columns_of(shared_terms, peer, width) for peer in peers], "seq", [grad_heads]
    ).astype(BF16)
    grad_qkv = from_kernel(
        attend_backward(slots, saved, to_kernel(grad_heads), log_totals, tables)
    )
    grad_qkv, unit_sums = after((grad_qkv, unit_sums), shared_sum, down_sum)
    grad_query = grad_qkv[:, :width]
    grad_key = grad_qkv[:, width : width + kv_width]
    grad_value = grad_qkv[:, width + kv_width :]
    low_part = jnp.concatenate(
        [
            mm_nt(grad_query, second_q[0]),
            mm_nt(grad_key, second_k[0]),
            mm_nt(grad_value, second_v[0]),
        ],
        axis=1,
    ).astype(BF16)
    grad_low_qkv = reduce_halves(low_part[: PACK // 2], low_part[PACK // 2 :], "seq")
    grad_low_qkv = grad_low_qkv.astype(BF16) * mask_own_three
    wide_bits = bits_down(fsdps)
    unit_sums = widen(unit_sums, wide_bits[0])
    grad_low_qkv, unit_sums = after((grad_low_qkv, unit_sums))
    grad_low_all = jnp.concatenate(gather_relative(grad_low_qkv, "seq"), axis=0)
    for bit in wide_bits[1:-1]:
        unit_sums = widen(unit_sums, bit)
    grad_low_all, unit_sums = after((grad_low_all, unit_sums))
    grad_a_qkv = mm_tn(grad_low_all, columns_of(normed_one, me, width))
    grad_b_q = mm_tn(low_q, grad_query)
    grad_b_kv = [mm_tn(low_k, grad_key), mm_tn(low_v, grad_value)]
    keep_one, give_one = sum_products([grad_qkv], [qkv_mine])
    grad_normed_one = reduce_halves(keep_one, after(give_one, grad_low_all), "seq")
    grad_normed_one = grad_normed_one + mm_nt(grad_low_qkv, first_qkv)
    layer_out = (valid_col * (hidden_mid + RESIDUAL_FACTOR * down_sum)).astype(BF16)
    _, norm_one_back = jax.vjp(lambda hidden: rms_norm(hidden, attention_norm_gain), hidden_in)
    grad_input = (grad_mid + norm_one_back(grad_normed_one)[0]).astype(BF16)

    factor = ADAPTER_TOTAL / math.sqrt(PACK * fsdps)

    def units_out(whole, first):
        part = whole[:, first : first + parts * SPAN]
        part = part.reshape(seqs, parts, SPAN, fsdps // parts, unit_block)
        return part.transpose(2, 1, 3, 0, 4).reshape(SPAN, feed_units)

    late_sums = scatter_step(grad_a_qkv.astype(BF16), unit_bits[0])
    unit_sums = widen(after(unit_sums, late_sums), wide_bits[-1])
    for bits in pairs_of(unit_bits[1:]):
        late_sums = scatter_step(late_sums, *bits)
    late_sums = after(late_sums, grad_normed_one)
    first_bits, *rest_bits = pairs_of(wide_bits)
    late_sums = widen(late_sums, *first_bits)
    late_sums, unit_sums = after((late_sums, unit_sums))
    for bits in rest_bits:
        late_sums = widen(late_sums, *bits)
    unit_pieces = gather_relative(unit_sums, "seq")
    early = settle(unit_pieces)
    blank = jnp.zeros((SPAN, width - 2 * kv_width), BF16)
    middle_sums = share_out(
        reduce_scatter_rows(
            jnp.concatenate(
                [
                    shared_sum,
                    grad_b_q.astype(BF16),
                    jnp.concatenate([g.astype(BF16) for g in grad_b_kv] + [blank], axis=1),
                ],
                axis=0,
            )
        )
    )
    def scaled(array):
        return array.astype(F32) * factor

    if unit_block % 128 == 0:
        a_down, b_ffn = finish_units(early, 0, parts, fsdps, unit_block, factor)
    else:
        a_down = scaled(units_out(early, 0).T)
        b_ffn = scaled(
            jnp.stack(
                [units_out(early, parts * SPAN), units_out(early, 2 * parts * SPAN)]
            )
        )
    middle_pieces = gather_relative(middle_sums, "seq", [a_down])
    middle = settle(middle_pieces)
    b_kv = middle[:, 6 * SPAN :, : 2 * kv_width].reshape(seqs, SPAN, 2, kv_width)
    a_all, b_model = finish_model(middle, factor)
    late = settle(gather_relative(late_sums, "seq", [b_model]))
    return (
        layer_out[None],
        grad_input[None],
        finish_late(late, a_all, factor),
        a_down,
        b_model,
        scaled(b_kv.transpose(2, 1, 0, 3).reshape(2, SPAN, KV_HEADS * HEAD_DIM)),
        b_ffn,
    )


def solution(mesh):
    rows = P("fsdp", None)
    placed = (
        (P("fsdp", "seq", None),) * 2 + (rows,) * 2 + (P(),) * 2 + (rows,) * 7 + (P(),) * 5
    )
    return jax.shard_map(
        shards,
        mesh=mesh,
        in_specs=placed,
        out_specs=(P("fsdp", "seq", None), P("fsdp", "seq", None), P(), P(), P(), P(), P()),
        check_vma=False,
    )
```
